512 devices in a mesh: space: 128 (over z, y, core), tm: 4 (over x).
Axes of the slice: x: 4, y: 4, z: 16, core: 2. Of those that a mesh axis runs over, the one named last changes fastest.
Arguments:
- snapshots: bfloat16 [262144, 2048], P('space', 'tm'), as said below
- sketch: bfloat16 [2048, 256], P('tm'), may hold values from -0.125 to 0.125
- rotation: float32 [256, 256], replicated, may hold values from -0.375 to 0.375
Outputs:
- basis: float32 [262144, 256], P(('space', 'tm'))
- triangle: float32 [256, 256], replicated
The draws below stay inside these ranges and needn't reach their ends.
Inputs may be any that keep to these rules, and one draw needn't show every extreme that they name: `snapshots`: the sketch has full column rank.
All inputs are finite; a program needn't handle non-finite values.
Results may differ from the reference program's by a relative error of at most 0.0003.
Values sent between devices are 32-bit elements; how exact they have to be, the bound alone decides.
A program may use at most 64 MiB of HBM per device.

```python
import math
import jax
import jax.numpy as jnp
from jax import lax

K = 256
NSNAP = 2048
NCELL = 262144


def draw_snapshots(key, part):
    keys = jax.random.split(key, 3)
    cells = jnp.arange(NCELL, dtype=jnp.float32)[:, None] / NCELL
    trend = 0.5 * jnp.exp(cells * math.log(3.0))
    rough = jnp.exp(jax.random.uniform(keys[1], (NCELL, 1), jnp.float32, math.log(0.5), math.log(2.0)))
    columns = jnp.exp(jax.random.uniform(keys[2], (1, NSNAP), jnp.float32, 0.0, math.log(10.0)))
    base = jax.random.normal(keys[0], (NCELL, NSNAP), jnp.float32)
    return (base * trend * rough * columns).astype(jnp.bfloat16)


def shard_levels(rng, dims, shards, low, top_value):
    gain = 1.0
    for position, blocks in shards:
        heights = jax.random.uniform(jax.random.fold_in(jax.random.fold_in(rng, 6), position), (blocks,), jnp.float32, low / len(shards), top_value / len(shards))
        gain = gain * jnp.repeat(jnp.exp(heights), dims[position] // blocks).reshape((-1,) + (1,) * (len(dims) - 1 - position))
    return gain


def normal_values(key, dims, width, most, cuts=(), kind=jnp.bfloat16):
    loudness = shard_levels(key, dims, cuts, -0.22, 0.18) if cuts else 1.0
    result = jax.random.normal(key, dims, jnp.float32) * width * loudness
    return jnp.minimum(jnp.maximum(result, -most), most).astype(kind)


def setup_inputs(seed: int = 0) -> dict:
    seeds = jax.random.split(jax.random.key(seed), 4)
    snapshots = draw_snapshots(jax.random.fold_in(seeds[3], 71), 0)
    sketch = normal_values(seeds[1], (NSNAP, K), NSNAP ** -0.5, 0.125, ((0, 4),))
    rotation = normal_values(seeds[2], (K, K), K ** -0.5, 0.375, (), jnp.float32)
    return {"snapshots": snapshots, "sketch": sketch, "rotation": rotation}


def reference(snapshots, sketch, rotation):
    sketched = jnp.dot(snapshots.astype(jnp.float32), sketch.astype(jnp.float32), preferred_element_type=jnp.float32)
    gram = lax.dot_general(sketched.astype(jnp.float32), sketched.astype(jnp.float32), (((0,), (0,)), ((), ())), precision=lax.Precision.HIGHEST, preferred_element_type=jnp.float32)
    lower = jnp.linalg.cholesky(gram)
    orthonormal = lax.linalg.triangular_solve(lower, sketched, left_side=False, lower=True, transpose_a=True)
    scale = jnp.sqrt(jnp.float32(NCELL))
    basis = scale * jnp.dot(orthonormal.astype(jnp.float32), rotation.astype(jnp.float32), precision=lax.Precision.HIGHEST, preferred_element_type=jnp.float32)
    triangle = lower.T / scale
    return (basis, triangle)
```

```python
import functools

import jax
import jax.numpy as jnp
from jax import lax
from jax.experimental import pallas as pl
from jax.experimental.pallas import tpu as pltpu
from jax.sharding import Mesh, PartitionSpec as P

MESH = pl.DeviceIdType.MESH
AXES = ("z", "y", "c", "x")
SPACE = ("z", "y", "c")
TILES = 64


def sum_kernel(sizes, a_ref, o_ref, zbuf, zsum, ybuf, ysum, xbuf, xsum, cbuf, full,
               zr, zs, yr, ys, xr, xs, cr, cs, ygr, ygs, zgr, zgs):
    nz, ny, nc, nx = sizes
    zi, yi, ci, xi = (lax.axis_index(a) for a in AXES)
    cz = TILES // nz
    cy = cz // ny

    def peers(n, me):
        return [lax.rem(me + d, n) for d in range(1, n)]

    barrier = pltpu.get_barrier_semaphore()
    count = 0
    for n, me, make in (
        (nz, zi, lambda j: (j, yi, ci, xi)),
        (ny, yi, lambda j: (zi, j, ci, xi)),
        (nc, ci, lambda j: (zi, yi, j, xi)),
        (nx, xi, lambda j: (zi, yi, ci, j)),
    ):
        for j in peers(n, me):
            pl.semaphore_signal(barrier, inc=1, device_id=make(j), device_id_type=MESH)
            count += 1
    pl.semaphore_wait(barrier, count)

    def exchange(n, me, make, src_of, dst_of, rsem, ssem):
        copies = []
        for j in peers(n, me):
            cp = pltpu.make_async_remote_copy(
                src_ref=src_of(j), dst_ref=dst_of(me), send_sem=ssem.at[j],
                recv_sem=rsem.at[me], device_id=make(j), device_id_type=MESH)
            cp.start()
            copies.append(cp)
        for j in peers(n, me):
            pltpu.make_async_remote_copy(
                src_ref=src_of(j), dst_ref=dst_of(j), send_sem=ssem.at[j],
                recv_sem=rsem.at[j], device_id=make(j), device_id_type=MESH).wait_recv()
        for cp in copies:
            cp.wait_send()

    def ordered_sum(buf, n):
        acc = buf[0]
        for j in range(1, n):
            acc = acc + buf[j]
        return acc

    zbuf[zi] = a_ref[pl.ds(zi * cz, cz)]
    exchange(nz, zi, lambda j: (j, yi, ci, xi),
             lambda j: a_ref.at[pl.ds(j * cz, cz)], lambda j: zbuf.at[j], zr, zs)
    zsum[...] = ordered_sum(zbuf, nz)

    ybuf[yi] = zsum[pl.ds(yi * cy, cy)]
    exchange(ny, yi, lambda j: (zi, j, ci, xi),
             lambda j: zsum.at[pl.ds(j * cy, cy)], lambda j: ybuf.at[j], yr, ys)
    ysum[...] = ordered_sum(ybuf, ny)

    xbuf[xi] = ysum[...]
    exchange(nx, xi, lambda j: (zi, yi, ci, j), lambda j: ysum, lambda j: xbuf.at[j], xr, xs)
    xsum[...] = ordered_sum(xbuf, nx)

    cbuf[ci] = xsum[...]
    exchange(nc, ci, lambda j: (zi, yi, j, xi), lambda j: xsum, lambda j: cbuf.at[j], cr, cs)
    own = zi * cz + yi * cy
    full[pl.ds(own, cy)] = ordered_sum(cbuf, nc)

    exchange(ny, yi, lambda j: (zi, j, ci, xi),
             lambda j: full.at[pl.ds(own, cy)],
             lambda j: full.at[pl.ds(zi * cz + j * cy, cy)], ygr, ygs)
    exchange(nz, zi, lambda j: (j, yi, ci, xi),
             lambda j: full.at[pl.ds(zi * cz, cz)],
             lambda j: full.at[pl.ds(j * cz, cz)], zgr, zgs)
    o_ref[...] = full[...]


def all_sum(gram, sizes):
    nz, ny, nc, nx = sizes
    cz = TILES // nz
    cy = cz // ny
    rows, cols = gram.shape
    tiles = gram.reshape(TILES, (rows * cols) // (TILES * 128), 128)
    t = tiles.shape[1:]
    dma = pltpu.SemaphoreType.DMA
    out = pl.pallas_call(
        functools.partial(sum_kernel, sizes),
        out_shape=jax.ShapeDtypeStruct(tiles.shape, jnp.float32),
        in_specs=[pl.BlockSpec(memory_space=pltpu.VMEM)],
        out_specs=pl.BlockSpec(memory_space=pltpu.VMEM),
        scratch_shapes=[
            pltpu.VMEM((nz, cz) + t, jnp.float32),
            pltpu.VMEM((cz,) + t, jnp.float32),
            pltpu.VMEM((ny, cy) + t, jnp.float32),
            pltpu.VMEM((cy,) + t, jnp.float32),
            pltpu.VMEM((nx, cy) + t, jnp.float32),
            pltpu.VMEM((cy,) + t, jnp.float32),
            pltpu.VMEM((nc, cy) + t, jnp.float32),
            pltpu.VMEM(tiles.shape, jnp.float32),
            dma((nz,)), dma((nz,)), dma((ny,)), dma((ny,)),
            dma((nx,)), dma((nx,)), dma((nc,)), dma((nc,)),
            dma((ny,)), dma((ny,)), dma((nz,)), dma((nz,)),
        ],
        compiler_params=pltpu.CompilerParams(collective_id=0, has_side_effects=True),
    )(tiles)
    return out.reshape(rows, cols)


def shards(sizes, snapshots, sketch, rotation):
    sketched = lax.psum_scatter(
        jnp.dot(snapshots, sketch, preferred_element_type=jnp.float32),
        "x",
        scatter_dimension=0,
        tiled=True,
    )
    gram = lax.dot_general(
        sketched,
        sketched,
        (((0,), (0,)), ((), ())),
        precision=lax.Precision.HIGHEST,
        preferred_element_type=jnp.float32,
    )
    gram = all_sum(gram, sizes)
    lower = jnp.linalg.cholesky(gram)
    orthonormal = lax.linalg.triangular_solve(
        lower, sketched, left_side=False, lower=True, transpose_a=True
    )
    cell_count = sketched.shape[0] * sizes[0] * sizes[1] * sizes[2] * sizes[3]
    scale = jnp.sqrt(jnp.float32(cell_count))
    basis = scale * jnp.dot(
        orthonormal, rotation, precision=lax.Precision.HIGHEST, preferred_element_type=jnp.float32
    )
    triangle = lower.T / scale
    return (basis, triangle)


def physical_mesh(mesh):
    space, tm = mesh.devices.shape
    nc = 2
    ny = 4 if space % 8 == 0 else 1
    nz = space // (ny * nc)
    devs = mesh.devices.reshape(nz, ny, nc, tm)
    return Mesh(devs, AXES), (nz, ny, nc, tm)


def solution(mesh):
    m4, sizes = physical_mesh(mesh)
    in_specs = (P(SPACE, "x"), P("x", None), P())
    out_specs = (P(AXES, None), P())
    return jax.shard_map(functools.partial(shards, sizes), mesh=m4, in_specs=in_specs,
                         out_specs=out_specs, check_vma=False)
```

```python
import functools

import jax
import jax.numpy as jnp
from jax import lax
from jax.experimental import pallas as pl
from jax.experimental.pallas import tpu as pltpu
from jax.sharding import Mesh, PartitionSpec as P

MESH = pl.DeviceIdType.MESH
AXES = ("z", "y", "c", "x")
SPACE = ("z", "y", "c")
TILES = 64


def sum_kernel(sizes, a_ref, o_ref, zbuf, zsum, ybuf, ysum, xbuf, xsum, cbuf, full,
               zr, zs, yr, ys, xr, xs, cr, cs, ygr, ygs, zgr, zgs):
    nz, ny, nc, nx = sizes
    zi, yi, ci, xi = (lax.axis_index(a) for a in AXES)
    cz = TILES // nz
    cy = cz // ny

    def peers(n, me):
        return [lax.rem(me + d, n) for d in range(1, n)]

    barrier = pltpu.get_barrier_semaphore()
    count = 0
    for n, me, make in (
        (nz, zi, lambda j: (j, yi, ci, xi)),
        (ny, yi, lambda j: (zi, j, ci, xi)),
        (nc, ci, lambda j: (zi, yi, j, xi)),
        (nx, xi, lambda j: (zi, yi, ci, j)),
    ):
        for j in peers(n, me):
            pl.semaphore_signal(barrier, inc=1, device_id=make(j), device_id_type=MESH)
            count += 1
    pl.semaphore_wait(barrier, count)

    def exchange(n, me, make, src_of, dst_of, rsem, ssem):
        copies = []
        for j in peers(n, me):
            cp = pltpu.make_async_remote_copy(
                src_ref=src_of(j), dst_ref=dst_of(me), send_sem=ssem.at[j],
                recv_sem=rsem.at[me], device_id=make(j), device_id_type=MESH)
            cp.start()
            copies.append(cp)
        for j in peers(n, me):
            pltpu.make_async_remote_copy(
                src_ref=src_of(j), dst_ref=dst_of(j), send_sem=ssem.at[j],
                recv_sem=rsem.at[j], device_id=make(j), device_id_type=MESH).wait_recv()
        for cp in copies:
            cp.wait_send()

    def ordered_sum(buf, n):
        acc = buf[0]
        for j in range(1, n):
            acc = acc + buf[j]
        return acc

    zbuf[zi] = a_ref[pl.ds(zi * cz, cz)]
    exchange(nz, zi, lambda j: (j, yi, ci, xi),
             lambda j: a_ref.at[pl.ds(j * cz, cz)], lambda j: zbuf.at[j], zr, zs)
    zsum[...] = ordered_sum(zbuf, nz)

    ybuf[yi] = zsum[pl.ds(yi * cy, cy)]
    exchange(ny, yi, lambda j: (zi, j, ci, xi),
             lambda j: zsum.at[pl.ds(j * cy, cy)], lambda j: ybuf.at[j], yr, ys)
    ysum[...] = ordered_sum(ybuf, ny)

    xbuf[xi] = ysum[...]
    exchange(nx, xi, lambda j: (zi, yi, ci, j), lambda j: ysum, lambda j: xbuf.at[j], xr, xs)
    xsum[...] = ordered_sum(xbuf, nx)

    cbuf[ci] = xsum[...]
    exchange(nc, ci, lambda j: (zi, yi, j, xi), lambda j: xsum, lambda j: cbuf.at[j], cr, cs)
    own = zi * cz + yi * cy
    full[pl.ds(own, cy)] = ordered_sum(cbuf, nc)

    exchange(ny, yi, lambda j: (zi, j, ci, xi),
             lambda j: full.at[pl.ds(own, cy)],
             lambda j: full.at[pl.ds(zi * cz + j * cy, cy)], ygr, ygs)
    exchange(nz, zi, lambda j: (j, yi, ci, xi),
             lambda j: full.at[pl.ds(zi * cz, cz)],
             lambda j: full.at[pl.ds(j * cz, cz)], zgr, zgs)
    o_ref[...] = full[...]


def all_sum(gram, sizes):
    nz, ny, nc, nx = sizes
    cz = TILES // nz
    cy = cz // ny
    rows, cols = gram.shape
    tiles = gram.reshape(TILES, (rows * cols) // (TILES * 128), 128)
    t = tiles.shape[1:]
    dma = pltpu.SemaphoreType.DMA
    out = pl.pallas_call(
        functools.partial(sum_kernel, sizes),
        out_shape=jax.ShapeDtypeStruct(tiles.shape, jnp.float32),
        in_specs=[pl.BlockSpec(memory_space=pltpu.VMEM)],
        out_specs=pl.BlockSpec(memory_space=pltpu.VMEM),
        scratch_shapes=[
            pltpu.VMEM((nz, cz) + t, jnp.float32),
            pltpu.VMEM((cz,) + t, jnp.float32),
            pltpu.VMEM((ny, cy) + t, jnp.float32),
            pltpu.VMEM((cy,) + t, jnp.float32),
            pltpu.VMEM((nx, cy) + t, jnp.float32),
            pltpu.VMEM((cy,) + t, jnp.float32),
            pltpu.VMEM((nc, cy) + t, jnp.float32),
            pltpu.VMEM(tiles.shape, jnp.float32),
            dma((nz,)), dma((nz,)), dma((ny,)), dma((ny,)),
            dma((nx,)), dma((nx,)), dma((nc,)), dma((nc,)),
            dma((ny,)), dma((ny,)), dma((nz,)), dma((nz,)),
        ],
        compiler_params=pltpu.CompilerParams(collective_id=0, has_side_effects=True),
    )(tiles)
    return out.reshape(rows, cols)


def scatter_kernel(nx, s_ref, k_ref, o_ref, part, rbuf, rs, ss):
    xi = lax.axis_index("x")
    rows = o_ref.shape[0]

    barrier = pltpu.get_barrier_semaphore()
    for d in range(1, nx):
        pl.semaphore_signal(barrier, inc=1, device_id={"x": lax.rem(xi + d, nx)},
                            device_id_type=MESH)
    pl.semaphore_wait(barrier, nx - 1)

    copies = []
    for d in range(1, nx):
        j = lax.rem(xi + d, nx)
        block = s_ref[pl.ds(pl.multiple_of(j * rows, rows), rows), :]
        part[j] = jnp.dot(block, k_ref[...], preferred_element_type=jnp.float32)
        cp = pltpu.make_async_remote_copy(
            src_ref=part.at[j], dst_ref=rbuf.at[xi], send_sem=ss.at[j],
            recv_sem=rs.at[xi], device_id={"x": j}, device_id_type=MESH)
        cp.start()
        copies.append(cp)
    block = s_ref[pl.ds(pl.multiple_of(xi * rows, rows), rows), :]
    rbuf[xi] = jnp.dot(block, k_ref[...], preferred_element_type=jnp.float32)
    for d in range(1, nx):
        j = lax.rem(xi + d, nx)
        pltpu.make_async_remote_copy(
            src_ref=part.at[j], dst_ref=rbuf.at[j], send_sem=ss.at[j],
            recv_sem=rs.at[j], device_id={"x": j}, device_id_type=MESH).wait_recv()
    acc = rbuf[0]
    for j in range(1, nx):
        acc = acc + rbuf[j]
    o_ref[...] = acc
    for cp in copies:
        cp.wait_send()


def sketch_scatter(snapshots, sketch, nx):
    cells = snapshots.shape[0]
    rows = cells // nx
    cols = sketch.shape[1]
    dma = pltpu.SemaphoreType.DMA
    return pl.pallas_call(
        functools.partial(scatter_kernel, nx),
        out_shape=jax.ShapeDtypeStruct((rows, cols), jnp.float32),
        in_specs=[pl.BlockSpec(memory_space=pltpu.VMEM)] * 2,
        out_specs=pl.BlockSpec(memory_space=pltpu.VMEM),
        scratch_shapes=[
            pltpu.VMEM((nx, rows, cols), jnp.float32),
            pltpu.VMEM((nx, rows, cols), jnp.float32),
            dma((nx,)), dma((nx,)),
        ],
        compiler_params=pltpu.CompilerParams(collective_id=1, has_side_effects=True,
                                             vmem_limit_bytes=48 * 1024 * 1024),
    )(snapshots, sketch)


def shards(sizes, snapshots, sketch, rotation):
    sketched = sketch_scatter(snapshots, sketch, sizes[3])
    gram = lax.dot_general(
        sketched,
        sketched,
        (((0,), (0,)), ((), ())),
        precision=lax.Precision.HIGHEST,
        preferred_element_type=jnp.float32,
    )
    gram = all_sum(gram, sizes)
    lower = jnp.linalg.cholesky(gram)
    orthonormal = lax.linalg.triangular_solve(
        lower, sketched, left_side=False, lower=True, transpose_a=True
    )
    cell_count = sketched.shape[0] * sizes[0] * sizes[1] * sizes[2] * sizes[3]
    scale = jnp.sqrt(jnp.float32(cell_count))
    basis = scale * jnp.dot(
        orthonormal, rotation, precision=lax.Precision.HIGHEST, preferred_element_type=jnp.float32
    )
    triangle = lower.T / scale
    return (basis, triangle)


def physical_mesh(mesh):
    space, tm = mesh.devices.shape
    nc = 2
    ny = 4 if space % 8 == 0 else 1
    nz = space // (ny * nc)
    devs = mesh.devices.reshape(nz, ny, nc, tm)
    return Mesh(devs, AXES), (nz, ny, nc, tm)


def solution(mesh):
    m4, sizes = physical_mesh(mesh)
    in_specs = (P(SPACE, "x"), P("x", None), P())
    out_specs = (P(AXES, None), P())
    return jax.shard_map(functools.partial(shards, sizes), mesh=m4, in_specs=in_specs,
                         out_specs=out_specs, check_vma=False)
```

```python
import functools

import jax
import jax.numpy as jnp
from jax import lax
from jax.experimental import pallas as pl
from jax.experimental.pallas import tpu as pltpu
from jax.sharding import Mesh, PartitionSpec as P

MESH = pl.DeviceIdType.MESH
AXES = ("z", "y", "c", "x")
SPACE = ("z", "y", "c")
TILES = 64


def sum_kernel(sizes, a_ref, o_ref, zbuf, zsum, ybuf, ysum, xbuf, xsum, cbuf, full,
               zr, zs, yr, ys, xr, xs, cr, cs, ygr, ygs, zgr, zgs):
    nz, ny, nc, nx = sizes
    zi, yi, ci, xi = (lax.axis_index(a) for a in AXES)
    cz = TILES // nz
    cy = cz // ny

    def peers(n, me):
        return [lax.rem(me + d, n) for d in range(1, n)]

    barrier = pltpu.get_barrier_semaphore()
    count = 0
    for n, me, make in (
        (nz, zi, lambda j: (j, yi, ci, xi)),
        (ny, yi, lambda j: (zi, j, ci, xi)),
        (nc, ci, lambda j: (zi, yi, j, xi)),
        (nx, xi, lambda j: (zi, yi, ci, j)),
    ):
        for j in peers(n, me):
            pl.semaphore_signal(barrier, inc=1, device_id=make(j), device_id_type=MESH)
            count += 1
    pl.semaphore_wait(barrier, count)

    def exchange(n, me, make, src_of, dst_of, rsem, ssem):
        copies = []
        for j in peers(n, me):
            cp = pltpu.make_async_remote_copy(
                src_ref=src_of(j), dst_ref=dst_of(me), send_sem=ssem.at[j],
                recv_sem=rsem.at[me], device_id=make(j), device_id_type=MESH)
            cp.start()
            copies.append(cp)
        for j in peers(n, me):
            pltpu.make_async_remote_copy(
                src_ref=src_of(j), dst_ref=dst_of(j), send_sem=ssem.at[j],
                recv_sem=rsem.at[j], device_id=make(j), device_id_type=MESH).wait_recv()
        for cp in copies:
            cp.wait_send()

    def ordered_sum(buf, n):
        acc = buf[0]
        for j in range(1, n):
            acc = acc + buf[j]
        return acc

    zbuf[zi] = a_ref[pl.ds(zi * cz, cz)]
    exchange(nz, zi, lambda j: (j, yi, ci, xi),
             lambda j: a_ref.at[pl.ds(j * cz, cz)], lambda j: zbuf.at[j], zr, zs)
    zsum[...] = ordered_sum(zbuf, nz)

    ybuf[yi] = zsum[pl.ds(yi * cy, cy)]
    exchange(ny, yi, lambda j: (zi, j, ci, xi),
             lambda j: zsum.at[pl.ds(j * cy, cy)], lambda j: ybuf.at[j], yr, ys)
    ysum[...] = ordered_sum(ybuf, ny)

    xbuf[xi] = ysum[...]
    exchange(nx, xi, lambda j: (zi, yi, ci, j), lambda j: ysum, lambda j: xbuf.at[j], xr, xs)
    xsum[...] = ordered_sum(xbuf, nx)

    cbuf[ci] = xsum[...]
    exchange(nc, ci, lambda j: (zi, yi, j, xi), lambda j: xsum, lambda j: cbuf.at[j], cr, cs)
    own = zi * cz + yi * cy
    full[pl.ds(own, cy)] = ordered_sum(cbuf, nc)

    exchange(ny, yi, lambda j: (zi, j, ci, xi),
             lambda j: full.at[pl.ds(own, cy)],
             lambda j: full.at[pl.ds(zi * cz + j * cy, cy)], ygr, ygs)
    exchange(nz, zi, lambda j: (j, yi, ci, xi),
             lambda j: full.at[pl.ds(zi * cz, cz)],
             lambda j: full.at[pl.ds(j * cz, cz)], zgr, zgs)
    o_ref[...] = full[...]


def all_sum(gram, sizes):
    nz, ny, nc, nx = sizes
    cz = TILES // nz
    cy = cz // ny
    rows, cols = gram.shape
    tiles = gram.reshape(TILES, (rows * cols) // (TILES * 128), 128)
    t = tiles.shape[1:]
    dma = pltpu.SemaphoreType.DMA
    out = pl.pallas_call(
        functools.partial(sum_kernel, sizes),
        out_shape=jax.ShapeDtypeStruct(tiles.shape, jnp.float32),
        in_specs=[pl.BlockSpec(memory_space=pltpu.VMEM)],
        out_specs=pl.BlockSpec(memory_space=pltpu.VMEM),
        scratch_shapes=[
            pltpu.VMEM((nz, cz) + t, jnp.float32),
            pltpu.VMEM((cz,) + t, jnp.float32),
            pltpu.VMEM((ny, cy) + t, jnp.float32),
            pltpu.VMEM((cy,) + t, jnp.float32),
            pltpu.VMEM((nx, cy) + t, jnp.float32),
            pltpu.VMEM((cy,) + t, jnp.float32),
            pltpu.VMEM((nc, cy) + t, jnp.float32),
            pltpu.VMEM(tiles.shape, jnp.float32),
            dma((nz,)), dma((nz,)), dma((ny,)), dma((ny,)),
            dma((nx,)), dma((nx,)), dma((nc,)), dma((nc,)),
            dma((ny,)), dma((ny,)), dma((nz,)), dma((nz,)),
        ],
        compiler_params=pltpu.CompilerParams(collective_id=0, has_side_effects=True),
    )(tiles)
    return out.reshape(rows, cols)


def scatter_kernel(nx, s_ref, k_ref, o_ref, part, rbuf, rs, ss):
    xi = lax.axis_index("x")
    rows = o_ref.shape[0]

    barrier = pltpu.get_barrier_semaphore()
    for d in range(1, nx):
        pl.semaphore_signal(barrier, inc=1, device_id={"x": lax.rem(xi + d, nx)},
                            device_id_type=MESH)
    pl.semaphore_wait(barrier, nx - 1)

    copies = []
    for d in range(1, nx):
        j = lax.rem(xi + d, nx)
        block = s_ref[pl.ds(pl.multiple_of(j * rows, rows), rows), :]
        part[j] = jnp.dot(block, k_ref[...], preferred_element_type=jnp.float32)
        cp = pltpu.make_async_remote_copy(
            src_ref=part.at[j], dst_ref=rbuf.at[xi], send_sem=ss.at[j],
            recv_sem=rs.at[xi], device_id={"x": j}, device_id_type=MESH)
        cp.start()
        copies.append(cp)
    block = s_ref[pl.ds(pl.multiple_of(xi * rows, rows), rows), :]
    rbuf[xi] = jnp.dot(block, k_ref[...], preferred_element_type=jnp.float32)
    for d in range(1, nx):
        j = lax.rem(xi + d, nx)
        pltpu.make_async_remote_copy(
            src_ref=part.at[j], dst_ref=rbuf.at[j], send_sem=ss.at[j],
            recv_sem=rs.at[j], device_id={"x": j}, device_id_type=MESH).wait_recv()
    acc = rbuf[0]
    for j in range(1, nx):
        acc = acc + rbuf[j]
    o_ref[...] = acc
    for cp in copies:
        cp.wait_send()


def sketch_scatter(snapshots, sketch, nx):
    cells = snapshots.shape[0]
    rows = cells // nx
    cols = sketch.shape[1]
    dma = pltpu.SemaphoreType.DMA
    return pl.pallas_call(
        functools.partial(scatter_kernel, nx),
        out_shape=jax.ShapeDtypeStruct((rows, cols), jnp.float32),
        in_specs=[pl.BlockSpec(memory_space=pltpu.VMEM)] * 2,
        out_specs=pl.BlockSpec(memory_space=pltpu.VMEM),
        scratch_shapes=[
            pltpu.VMEM((nx, rows, cols), jnp.float32),
            pltpu.VMEM((nx, rows, cols), jnp.float32),
            dma((nx,)), dma((nx,)),
        ],
        compiler_params=pltpu.CompilerParams(collective_id=1, has_side_effects=True,
                                             vmem_limit_bytes=48 * 1024 * 1024),
    )(snapshots, sketch)


def shards(sizes, snapshots, sketch, rotation):
    sketched = sketch_scatter(snapshots, sketch, sizes[3])
    gram = lax.dot_general(
        sketched,
        sketched,
        (((0,), (0,)), ((), ())),
        precision=lax.Precision.HIGHEST,
        preferred_element_type=jnp.float32,
    )
    gram = all_sum(gram, sizes)
    lower = jnp.linalg.cholesky(gram)
    rotated = lax.linalg.triangular_solve(
        lower, rotation, left_side=True, lower=True, transpose_a=True
    )
    cell_count = sketched.shape[0] * sizes[0] * sizes[1] * sizes[2] * sizes[3]
    scale = jnp.sqrt(jnp.float32(cell_count))
    basis = scale * jnp.dot(
        sketched, rotated, precision=lax.Precision.HIGHEST, preferred_element_type=jnp.float32
    )
    triangle = lower.T / scale
    return (basis, triangle)


def physical_mesh(mesh):
    space, tm = mesh.devices.shape
    nc = 2
    ny = 4 if space % 8 == 0 else 1
    nz = space // (ny * nc)
    devs = mesh.devices.reshape(nz, ny, nc, tm)
    return Mesh(devs, AXES), (nz, ny, nc, tm)


def solution(mesh):
    m4, sizes = physical_mesh(mesh)
    in_specs = (P(SPACE, "x"), P("x", None), P())
    out_specs = (P(AXES, None), P())
    return jax.shard_map(functools.partial(shards, sizes), mesh=m4, in_specs=in_specs,
                         out_specs=out_specs, check_vma=False)
```

```python
import functools

import jax
import jax.numpy as jnp
from jax import lax
from jax.experimental import pallas as pl
from jax.experimental.pallas import tpu as pltpu
from jax.sharding import Mesh, PartitionSpec as P

MESH = pl.DeviceIdType.MESH
AXES = ("z", "y", "c", "x")
SPACE = ("z", "y", "c")
TILES = 64


def sum_kernel(sizes, a_ref, o_ref, cbuf, csum, xbuf, xsum, ybuf, ysum, zbuf, full,
               cr, cs, xr, xs, yr, ys, zr, zs, ygr, ygs, xgr, xgs, cgr, cgs):
    nz, ny, nc, nx = sizes
    zi, yi, ci, xi = (lax.axis_index(a) for a in AXES)

    def peers(n, me):
        return [lax.rem(me + d, n) for d in range(1, n)]

    barrier = pltpu.get_barrier_semaphore()
    count = 0
    for n, me, make in (
        (nz, zi, lambda j: (j, yi, ci, xi)),
        (ny, yi, lambda j: (zi, j, ci, xi)),
        (nc, ci, lambda j: (zi, yi, j, xi)),
        (nx, xi, lambda j: (zi, yi, ci, j)),
    ):
        for j in peers(n, me):
            pl.semaphore_signal(barrier, inc=1, device_id=make(j), device_id_type=MESH)
            count += 1
    pl.semaphore_wait(barrier, count)

    def exchange(n, me, make, src_of, dst_of, rsem, ssem):
        copies = []
        for j in peers(n, me):
            cp = pltpu.make_async_remote_copy(
                src_ref=src_of(j), dst_ref=dst_of(me), send_sem=ssem.at[j],
                recv_sem=rsem.at[me], device_id=make(j), device_id_type=MESH)
            cp.start()
            copies.append(cp)
        for j in peers(n, me):
            pltpu.make_async_remote_copy(
                src_ref=src_of(j), dst_ref=dst_of(j), send_sem=ssem.at[j],
                recv_sem=rsem.at[j], device_id=make(j), device_id_type=MESH).wait_recv()
        for cp in copies:
            cp.wait_send()

    def ordered_sum(buf, n):
        acc = buf[0]
        for j in range(1, n):
            acc = acc + buf[j]
        return acc

    c1 = TILES // nc
    c2 = c1 // nx
    c3 = c2 // ny
    zdev = lambda j: (j, yi, ci, xi)
    ydev = lambda j: (zi, j, ci, xi)
    cdev = lambda j: (zi, yi, j, xi)
    xdev = lambda j: (zi, yi, ci, j)

    cbuf[ci] = a_ref[pl.ds(ci * c1, c1)]
    exchange(nc, ci, cdev, lambda j: a_ref.at[pl.ds(j * c1, c1)], lambda j: cbuf.at[j], cr, cs)
    csum[...] = ordered_sum(cbuf, nc)

    xbuf[xi] = csum[pl.ds(xi * c2, c2)]
    exchange(nx, xi, xdev, lambda j: csum.at[pl.ds(j * c2, c2)], lambda j: xbuf.at[j], xr, xs)
    xsum[...] = ordered_sum(xbuf, nx)

    ybuf[yi] = xsum[pl.ds(yi * c3, c3)]
    exchange(ny, yi, ydev, lambda j: xsum.at[pl.ds(j * c3, c3)], lambda j: ybuf.at[j], yr, ys)
    ysum[...] = ordered_sum(ybuf, ny)

    zbuf[zi] = ysum[...]
    exchange(nz, zi, zdev, lambda j: ysum, lambda j: zbuf.at[j], zr, zs)
    own = ci * c1 + xi * c2 + yi * c3
    full[pl.ds(own, c3)] = ordered_sum(zbuf, nz)

    exchange(ny, yi, ydev, lambda j: full.at[pl.ds(own, c3)],
             lambda j: full.at[pl.ds(ci * c1 + xi * c2 + j * c3, c3)], ygr, ygs)
    exchange(nx, xi, xdev, lambda j: full.at[pl.ds(ci * c1 + xi * c2, c2)],
             lambda j: full.at[pl.ds(ci * c1 + j * c2, c2)], xgr, xgs)
    exchange(nc, ci, cdev, lambda j: full.at[pl.ds(ci * c1, c1)],
             lambda j: full.at[pl.ds(j * c1, c1)], cgr, cgs)
    o_ref[...] = full[...]


def all_sum(gram, sizes):
    nz, ny, nc, nx = sizes
    c1 = TILES // nc
    c2 = c1 // nx
    c3 = c2 // ny
    rows, cols = gram.shape
    tiles = gram.reshape(TILES, (rows * cols) // (TILES * 128), 128)
    t = tiles.shape[1:]
    dma = pltpu.SemaphoreType.DMA
    out = pl.pallas_call(
        functools.partial(sum_kernel, sizes),
        out_shape=jax.ShapeDtypeStruct(tiles.shape, jnp.float32),
        in_specs=[pl.BlockSpec(memory_space=pltpu.VMEM)],
        out_specs=pl.BlockSpec(memory_space=pltpu.VMEM),
        scratch_shapes=[
            pltpu.VMEM((nc, c1) + t, jnp.float32),
            pltpu.VMEM((c1,) + t, jnp.float32),
            pltpu.VMEM((nx, c2) + t, jnp.float32),
            pltpu.VMEM((c2,) + t, jnp.float32),
            pltpu.VMEM((ny, c3) + t, jnp.float32),
            pltpu.VMEM((c3,) + t, jnp.float32),
            pltpu.VMEM((nz, c3) + t, jnp.float32),
            pltpu.VMEM(tiles.shape, jnp.float32),
            dma((nc,)), dma((nc,)), dma((nx,)), dma((nx,)),
            dma((ny,)), dma((ny,)), dma((nz,)), dma((nz,)),
            dma((ny,)), dma((ny,)), dma((nx,)), dma((nx,)),
            dma((nc,)), dma((nc,)),
        ],
        compiler_params=pltpu.CompilerParams(collective_id=0, has_side_effects=True),
    )(tiles)
    return out.reshape(rows, cols)


def scatter_kernel(nx, s_ref, k_ref, o_ref, part, rbuf, rs, ss):
    xi = lax.axis_index("x")
    rows = o_ref.shape[0]

    barrier = pltpu.get_barrier_semaphore()
    for d in range(1, nx):
        pl.semaphore_signal(barrier, inc=1, device_id={"x": lax.rem(xi + d, nx)},
                            device_id_type=MESH)
    pl.semaphore_wait(barrier, nx - 1)

    copies = []
    for d in range(1, nx):
        j = lax.rem(xi + d, nx)
        block = s_ref[pl.ds(pl.multiple_of(j * rows, rows), rows), :]
        part[j] = jnp.dot(block, k_ref[...], preferred_element_type=jnp.float32)
        cp = pltpu.make_async_remote_copy(
            src_ref=part.at[j], dst_ref=rbuf.at[xi], send_sem=ss.at[j],
            recv_sem=rs.at[xi], device_id={"x": j}, device_id_type=MESH)
        cp.start()
        copies.append(cp)
    block = s_ref[pl.ds(pl.multiple_of(xi * rows, rows), rows), :]
    rbuf[xi] = jnp.dot(block, k_ref[...], preferred_element_type=jnp.float32)
    for d in range(1, nx):
        j = lax.rem(xi + d, nx)
        pltpu.make_async_remote_copy(
            src_ref=part.at[j], dst_ref=rbuf.at[j], send_sem=ss.at[j],
            recv_sem=rs.at[j], device_id={"x": j}, device_id_type=MESH).wait_recv()
    acc = rbuf[0]
    for j in range(1, nx):
        acc = acc + rbuf[j]
    o_ref[...] = acc
    for cp in copies:
        cp.wait_send()


def sketch_scatter(snapshots, sketch, nx):
    cells = snapshots.shape[0]
    rows = cells // nx
    cols = sketch.shape[1]
    dma = pltpu.SemaphoreType.DMA
    return pl.pallas_call(
        functools.partial(scatter_kernel, nx),
        out_shape=jax.ShapeDtypeStruct((rows, cols), jnp.float32),
        in_specs=[pl.BlockSpec(memory_space=pltpu.VMEM)] * 2,
        out_specs=pl.BlockSpec(memory_space=pltpu.VMEM),
        scratch_shapes=[
            pltpu.VMEM((nx, rows, cols), jnp.float32),
            pltpu.VMEM((nx, rows, cols), jnp.float32),
            dma((nx,)), dma((nx,)),
        ],
        compiler_params=pltpu.CompilerParams(collective_id=1, has_side_effects=True,
                                             vmem_limit_bytes=48 * 1024 * 1024),
    )(snapshots, sketch)


def shards(sizes, snapshots, sketch, rotation):
    sketched = sketch_scatter(snapshots, sketch, sizes[3])
    gram = lax.dot_general(
        sketched,
        sketched,
        (((0,), (0,)), ((), ())),
        precision=lax.Precision.HIGHEST,
        preferred_element_type=jnp.float32,
    )
    gram = all_sum(gram, sizes)
    lower = jnp.linalg.cholesky(gram)
    rotated = lax.linalg.triangular_solve(
        lower, rotation, left_side=True, lower=True, transpose_a=True
    )
    cell_count = sketched.shape[0] * sizes[0] * sizes[1] * sizes[2] * sizes[3]
    scale = jnp.sqrt(jnp.float32(cell_count))
    basis = scale * jnp.dot(
        sketched, rotated, precision=lax.Precision.HIGHEST, preferred_element_type=jnp.float32
    )
    triangle = lower.T / scale
    return (basis, triangle)


def physical_mesh(mesh):
    space, tm = mesh.devices.shape
    nc = 2
    ny = 4 if space % 8 == 0 else 1
    nz = space // (ny * nc)
    devs = mesh.devices.reshape(nz, ny, nc, tm)
    return Mesh(devs, AXES), (nz, ny, nc, tm)


def solution(mesh):
    m4, sizes = physical_mesh(mesh)
    in_specs = (P(SPACE, "x"), P("x", None), P())
    out_specs = (P(AXES, None), P())
    return jax.shard_map(functools.partial(shards, sizes), mesh=m4, in_specs=in_specs,
                         out_specs=out_specs, check_vma=False)
```

```python
import functools

import jax
import jax.numpy as jnp
from jax import lax
from jax.experimental import pallas as pl
from jax.experimental.pallas import tpu as pltpu
from jax.sharding import Mesh, PartitionSpec as P

MESH = pl.DeviceIdType.MESH
AXES = ("z", "y", "c", "x")
SPACE = ("z", "y", "c")
TILES = 64


def sum_kernel(sizes, a_ref, o_ref, cbuf, csum, xbuf, xsum, ybuf, ysum, zbuf, full,
               cr, cs, xr, xs, yr, ys, zr, zs, ygr, ygs, xgr, xgs, cgr, cgs):
    nz, ny, nc, nx = sizes
    zi, yi, ci, xi = (lax.axis_index(a) for a in AXES)

    def peers(n, me):
        return [lax.rem(me + d, n) for d in range(1, n)]

    barrier = pltpu.get_barrier_semaphore()
    count = 0
    for n, me, make in (
        (nz, zi, lambda j: (j, yi, ci, xi)),
        (ny, yi, lambda j: (zi, j, ci, xi)),
        (nc, ci, lambda j: (zi, yi, j, xi)),
        (nx, xi, lambda j: (zi, yi, ci, j)),
    ):
        for j in peers(n, me):
            pl.semaphore_signal(barrier, inc=1, device_id=make(j), device_id_type=MESH)
            count += 1
    pl.semaphore_wait(barrier, count)

    def exchange(n, me, make, src_of, dst_of, rsem, ssem):
        copies = []
        for j in peers(n, me):
            cp = pltpu.make_async_remote_copy(
                src_ref=src_of(j), dst_ref=dst_of(me), send_sem=ssem.at[j],
                recv_sem=rsem.at[me], device_id=make(j), device_id_type=MESH)
            cp.start()
            copies.append(cp)
        for j in peers(n, me):
            pltpu.make_async_remote_copy(
                src_ref=src_of(j), dst_ref=dst_of(j), send_sem=ssem.at[j],
                recv_sem=rsem.at[j], device_id=make(j), device_id_type=MESH).wait_recv()
        for cp in copies:
            cp.wait_send()

    def ordered_sum(buf, n):
        acc = buf[0]
        for j in range(1, n):
            acc = acc + buf[j]
        return acc

    c1 = TILES // nc
    c2 = c1 // nx
    c3 = c2 // ny
    zdev = lambda j: (j, yi, ci, xi)
    ydev = lambda j: (zi, j, ci, xi)
    cdev = lambda j: (zi, yi, j, xi)
    xdev = lambda j: (zi, yi, ci, j)

    cbuf[ci] = a_ref[pl.ds(ci * c1, c1)]
    exchange(nc, ci, cdev, lambda j: a_ref.at[pl.ds(j * c1, c1)], lambda j: cbuf.at[j], cr, cs)
    csum[...] = ordered_sum(cbuf, nc)

    xbuf[xi] = csum[pl.ds(xi * c2, c2)]
    exchange(nx, xi, xdev, lambda j: csum.at[pl.ds(j * c2, c2)], lambda j: xbuf.at[j], xr, xs)
    xsum[...] = ordered_sum(xbuf, nx)

    ybuf[yi] = xsum[pl.ds(yi * c3, c3)]
    exchange(ny, yi, ydev, lambda j: xsum.at[pl.ds(j * c3, c3)], lambda j: ybuf.at[j], yr, ys)
    ysum[...] = ordered_sum(ybuf, ny)

    zbuf[zi] = ysum[...]
    exchange(nz, zi, zdev, lambda j: ysum, lambda j: zbuf.at[j], zr, zs)
    own = ci * c1 + xi * c2 + yi * c3
    full[pl.ds(own, c3)] = ordered_sum(zbuf, nz)

    exchange(ny, yi, ydev, lambda j: full.at[pl.ds(own, c3)],
             lambda j: full.at[pl.ds(ci * c1 + xi * c2 + j * c3, c3)], ygr, ygs)
    exchange(nx, xi, xdev, lambda j: full.at[pl.ds(ci * c1 + xi * c2, c2)],
             lambda j: full.at[pl.ds(ci * c1 + j * c2, c2)], xgr, xgs)
    exchange(nc, ci, cdev, lambda j: full.at[pl.ds(ci * c1, c1)],
             lambda j: full.at[pl.ds(j * c1, c1)], cgr, cgs)
    o_ref[...] = full[...]


def all_sum(gram, sizes):
    nz, ny, nc, nx = sizes
    c1 = TILES // nc
    c2 = c1 // nx
    c3 = c2 // ny
    rows, cols = gram.shape
    tiles = gram.reshape(TILES, (rows * cols) // (TILES * 128), 128)
    t = tiles.shape[1:]
    dma = pltpu.SemaphoreType.DMA
    out = pl.pallas_call(
        functools.partial(sum_kernel, sizes),
        out_shape=jax.ShapeDtypeStruct(tiles.shape, jnp.float32),
        in_specs=[pl.BlockSpec(memory_space=pltpu.VMEM)],
        out_specs=pl.BlockSpec(memory_space=pltpu.VMEM),
        scratch_shapes=[
            pltpu.VMEM((nc, c1) + t, jnp.float32),
            pltpu.VMEM((c1,) + t, jnp.float32),
            pltpu.VMEM((nx, c2) + t, jnp.float32),
            pltpu.VMEM((c2,) + t, jnp.float32),
            pltpu.VMEM((ny, c3) + t, jnp.float32),
            pltpu.VMEM((c3,) + t, jnp.float32),
            pltpu.VMEM((nz, c3) + t, jnp.float32),
            pltpu.VMEM(tiles.shape, jnp.float32),
            dma((nc,)), dma((nc,)), dma((nx,)), dma((nx,)),
            dma((ny,)), dma((ny,)), dma((nz,)), dma((nz,)),
            dma((ny,)), dma((ny,)), dma((nx,)), dma((nx,)),
            dma((nc,)), dma((nc,)),
        ],
        compiler_params=pltpu.CompilerParams(collective_id=0, has_side_effects=True),
    )(tiles)
    return out.reshape(rows, cols)


def scatter_kernel(nx, s_ref, k_ref, o_ref, part, rbuf, rs, ss):
    xi = lax.axis_index("x")
    rows = o_ref.shape[0]

    barrier = pltpu.get_barrier_semaphore()
    for d in range(1, nx):
        pl.semaphore_signal(barrier, inc=1, device_id={"x": lax.rem(xi + d, nx)},
                            device_id_type=MESH)
    pl.semaphore_wait(barrier, nx - 1)

    copies = []
    for d in range(1, nx):
        j = lax.rem(xi + d, nx)
        block = s_ref[pl.ds(pl.multiple_of(j * rows, rows), rows), :]
        part[j] = jnp.dot(block, k_ref[...], preferred_element_type=jnp.float32)
        cp = pltpu.make_async_remote_copy(
            src_ref=part.at[j], dst_ref=rbuf.at[xi], send_sem=ss.at[j],
            recv_sem=rs.at[xi], device_id={"x": j}, device_id_type=MESH)
        cp.start()
        copies.append(cp)
    block = s_ref[pl.ds(pl.multiple_of(xi * rows, rows), rows), :]
    rbuf[xi] = jnp.dot(block, k_ref[...], preferred_element_type=jnp.float32)
    for d in range(1, nx):
        j = lax.rem(xi + d, nx)
        pltpu.make_async_remote_copy(
            src_ref=part.at[j], dst_ref=rbuf.at[j], send_sem=ss.at[j],
            recv_sem=rs.at[j], device_id={"x": j}, device_id_type=MESH).wait_recv()
    acc = rbuf[0]
    for j in range(1, nx):
        acc = acc + rbuf[j]
    o_ref[...] = acc
    for cp in copies:
        cp.wait_send()


def sketch_scatter(snapshots, sketch, nx):
    cells = snapshots.shape[0]
    rows = cells // nx
    cols = sketch.shape[1]
    dma = pltpu.SemaphoreType.DMA
    return pl.pallas_call(
        functools.partial(scatter_kernel, nx),
        out_shape=jax.ShapeDtypeStruct((rows, cols), jnp.float32),
        in_specs=[pl.BlockSpec(memory_space=pltpu.VMEM)] * 2,
        out_specs=pl.BlockSpec(memory_space=pltpu.VMEM),
        scratch_shapes=[
            pltpu.VMEM((nx, rows, cols), jnp.float32),
            pltpu.VMEM((nx, rows, cols), jnp.float32),
            dma((nx,)), dma((nx,)),
        ],
        compiler_params=pltpu.CompilerParams(collective_id=1, has_side_effects=True,
                                             vmem_limit_bytes=48 * 1024 * 1024),
    )(snapshots, sketch)


def factor_kernel(b, g_ref, l_ref, w_ref):
    n = g_ref.shape[0]
    hi = lax.Precision.HIGHEST
    l_ref[...] = jnp.zeros_like(l_ref)
    w_ref[...] = jnp.zeros_like(w_ref)
    nt = (((1,), (1,)), ((), ()))
    rows = lax.broadcasted_iota(jnp.int32, (b, b), 0)
    cols = lax.broadcasted_iota(jnp.int32, (b, b), 1)

    def panel(p, carry):
        r0 = pl.multiple_of(p * b, b)
        arow = g_ref[pl.ds(r0, b), :]
        w = w_ref[...]
        x = lax.dot_general(arow, w, nt, precision=hi, preferred_element_type=jnp.float32)
        pick = (lax.broadcasted_iota(jnp.int32, (n, b), 0)
                == r0 + lax.broadcasted_iota(jnp.int32, (n, b), 1)).astype(jnp.float32)
        place = (lax.broadcasted_iota(jnp.int32, (b, n), 1)
                 == r0 + lax.broadcasted_iota(jnp.int32, (b, n), 0)).astype(jnp.float32)
        s = jnp.dot(arow, pick, precision=hi, preferred_element_type=jnp.float32)
        s = s - lax.dot_general(x, x, nt, precision=hi, preferred_element_type=jnp.float32)
        low = jnp.zeros((b, b), jnp.float32)
        inv = jnp.zeros((b, b), jnp.float32)
        rest = (rows == cols).astype(jnp.float32)
        for i in range(b):
            root = jnp.sqrt(s[i:i + 1, i:i + 1])
            col = jnp.where(rows[:, i:i + 1] >= i, s[:, i:i + 1] / root, 0.0)
            row = jnp.where(cols[i:i + 1, :] >= i, s[i:i + 1, :] / root, 0.0)
            s = s - col * row
            low = jnp.where(cols == i, col, low)
            irow = rest[i:i + 1, :] / col[i:i + 1, :]
            inv = jnp.where(rows == i, irow, inv)
            rest = rest - col * irow
        l_ref[pl.ds(r0, b), :] = x + jnp.dot(low, place, precision=hi,
                                             preferred_element_type=jnp.float32)
        y = jnp.dot(x, w, precision=hi, preferred_element_type=jnp.float32)
        w_ref[pl.ds(r0, b), :] = jnp.dot(inv, place - y, precision=hi,
                                         preferred_element_type=jnp.float32)
        return carry

    lax.fori_loop(0, n // b, panel, 0)


def factor(gram, b=32):
    n = gram.shape[0]
    return pl.pallas_call(
        functools.partial(factor_kernel, b),
        out_shape=(jax.ShapeDtypeStruct((n, n), jnp.float32),) * 2,
        in_specs=[pl.BlockSpec(memory_space=pltpu.VMEM)],
        out_specs=(pl.BlockSpec(memory_space=pltpu.VMEM),) * 2,
    )(gram)


def shards(sizes, snapshots, sketch, rotation):
    sketched = sketch_scatter(snapshots, sketch, sizes[3])
    gram = lax.dot_general(
        sketched,
        sketched,
        (((0,), (0,)), ((), ())),
        precision=lax.Precision.HIGHEST,
        preferred_element_type=jnp.float32,
    )
    gram = all_sum(gram, sizes)
    lower, inverse = factor(gram)
    rotated = lax.dot_general(
        inverse, rotation, (((0,), (0,)), ((), ())),
        precision=lax.Precision.HIGHEST, preferred_element_type=jnp.float32,
    )
    cell_count = sketched.shape[0] * sizes[0] * sizes[1] * sizes[2] * sizes[3]
    scale = jnp.sqrt(jnp.float32(cell_count))
    basis = scale * jnp.dot(
        sketched, rotated, precision=lax.Precision.HIGHEST, preferred_element_type=jnp.float32
    )
    triangle = lower.T / scale
    return (basis, triangle)


def physical_mesh(mesh):
    space, tm = mesh.devices.shape
    nc = 2
    ny = 4 if space % 8 == 0 else 1
    nz = space // (ny * nc)
    devs = mesh.devices.reshape(nz, ny, nc, tm)
    return Mesh(devs, AXES), (nz, ny, nc, tm)


def solution(mesh):
    m4, sizes = physical_mesh(mesh)
    in_specs = (P(SPACE, "x"), P("x", None), P())
    out_specs = (P(AXES, None), P())
    return jax.shard_map(functools.partial(shards, sizes), mesh=m4, in_specs=in_specs,
                         out_specs=out_specs, check_vma=False)
```

```python
import functools

import jax
import jax.numpy as jnp
from jax import lax
from jax.experimental import pallas as pl
from jax.experimental.pallas import tpu as pltpu
from jax.sharding import Mesh, PartitionSpec as P

MESH = pl.DeviceIdType.MESH
AXES = ("z", "y", "c", "x")
SPACE = ("z", "y", "c")


def sum_kernel(sizes, a_ref, o_ref, cbuf, csum, xbuf, xsum, ybuf, ysum, zbuf, full,
               cr, cs, xr, xs, yr, ys, zr, zs, ygr, ygs, xgr, xgs, cgr, cgs):
    nz, ny, nc, nx = sizes
    zi, yi, ci, xi = (lax.axis_index(a) for a in AXES)

    def peers(n, me):
        return [lax.rem(me + d, n) for d in range(1, n)]

    barrier = pltpu.get_barrier_semaphore()
    count = 0
    for n, me, make in (
        (nz, zi, lambda j: (j, yi, ci, xi)),
        (ny, yi, lambda j: (zi, j, ci, xi)),
        (nc, ci, lambda j: (zi, yi, j, xi)),
        (nx, xi, lambda j: (zi, yi, ci, j)),
    ):
        for j in peers(n, me):
            pl.semaphore_signal(barrier, inc=1, device_id=make(j), device_id_type=MESH)
            count += 1
    pl.semaphore_wait(barrier, count)

    def exchange(n, me, make, src_of, dst_of, rsem, ssem):
        copies = []
        for j in peers(n, me):
            cp = pltpu.make_async_remote_copy(
                src_ref=src_of(j), dst_ref=dst_of(me), send_sem=ssem.at[j],
                recv_sem=rsem.at[me], device_id=make(j), device_id_type=MESH)
            cp.start()
            copies.append(cp)
        for j in peers(n, me):
            pltpu.make_async_remote_copy(
                src_ref=src_of(j), dst_ref=dst_of(j), send_sem=ssem.at[j],
                recv_sem=rsem.at[j], device_id=make(j), device_id_type=MESH).wait_recv()
        for cp in copies:
            cp.wait_send()

    def ordered_sum(buf, n):
        acc = buf[0]
        for j in range(1, n):
            acc = acc + buf[j]
        return acc

    c1 = a_ref.shape[0] // nc
    c2 = c1 // nx
    c3 = c2 // ny
    zdev = lambda j: (j, yi, ci, xi)
    ydev = lambda j: (zi, j, ci, xi)
    cdev = lambda j: (zi, yi, j, xi)
    xdev = lambda j: (zi, yi, ci, j)

    cbuf[ci] = a_ref[pl.ds(ci * c1, c1)]
    exchange(nc, ci, cdev, lambda j: a_ref.at[pl.ds(j * c1, c1)], lambda j: cbuf.at[j], cr, cs)
    csum[...] = ordered_sum(cbuf, nc)

    xbuf[xi] = csum[pl.ds(xi * c2, c2)]
    exchange(nx, xi, xdev, lambda j: csum.at[pl.ds(j * c2, c2)], lambda j: xbuf.at[j], xr, xs)
    xsum[...] = ordered_sum(xbuf, nx)

    ybuf[yi] = xsum[pl.ds(yi * c3, c3)]
    exchange(ny, yi, ydev, lambda j: xsum.at[pl.ds(j * c3, c3)], lambda j: ybuf.at[j], yr, ys)
    ysum[...] = ordered_sum(ybuf, ny)

    zbuf[zi] = ysum[...]
    exchange(nz, zi, zdev, lambda j: ysum, lambda j: zbuf.at[j], zr, zs)
    own = ci * c1 + xi * c2 + yi * c3
    full[pl.ds(own, c3)] = ordered_sum(zbuf, nz)

    exchange(ny, yi, ydev, lambda j: full.at[pl.ds(own, c3)],
             lambda j: full.at[pl.ds(ci * c1 + xi * c2 + j * c3, c3)], ygr, ygs)
    exchange(nx, xi, xdev, lambda j: full.at[pl.ds(ci * c1 + xi * c2, c2)],
             lambda j: full.at[pl.ds(ci * c1 + j * c2, c2)], xgr, xgs)
    exchange(nc, ci, cdev, lambda j: full.at[pl.ds(ci * c1, c1)],
             lambda j: full.at[pl.ds(j * c1, c1)], cgr, cgs)
    o_ref[...] = full[...]


def all_sum(gram, sizes):
    nz, ny, nc, nx = sizes
    c1 = gram.shape[0] // nc
    c2 = c1 // nx
    c3 = c2 // ny
    t = gram.shape[1:]
    dma = pltpu.SemaphoreType.DMA
    return pl.pallas_call(
        functools.partial(sum_kernel, sizes),
        out_shape=jax.ShapeDtypeStruct(gram.shape, jnp.float32),
        in_specs=[pl.BlockSpec(memory_space=pltpu.VMEM)],
        out_specs=pl.BlockSpec(memory_space=pltpu.VMEM),
        scratch_shapes=[
            pltpu.VMEM((nc, c1) + t, jnp.float32),
            pltpu.VMEM((c1,) + t, jnp.float32),
            pltpu.VMEM((nx, c2) + t, jnp.float32),
            pltpu.VMEM((c2,) + t, jnp.float32),
            pltpu.VMEM((ny, c3) + t, jnp.float32),
            pltpu.VMEM((c3,) + t, jnp.float32),
            pltpu.VMEM((nz, c3) + t, jnp.float32),
            pltpu.VMEM(gram.shape, jnp.float32),
            dma((nc,)), dma((nc,)), dma((nx,)), dma((nx,)),
            dma((ny,)), dma((ny,)), dma((nz,)), dma((nz,)),
            dma((ny,)), dma((ny,)), dma((nx,)), dma((nx,)),
            dma((nc,)), dma((nc,)),
        ],
        compiler_params=pltpu.CompilerParams(collective_id=0, has_side_effects=True),
    )(gram)


def scatter_kernel(nx, s_ref, k_ref, o_ref, part, rbuf, rs, ss):
    xi = lax.axis_index("x")
    rows = o_ref.shape[0]

    barrier = pltpu.get_barrier_semaphore()
    for d in range(1, nx):
        pl.semaphore_signal(barrier, inc=1, device_id={"x": lax.rem(xi + d, nx)},
                            device_id_type=MESH)
    pl.semaphore_wait(barrier, nx - 1)

    copies = []
    for d in range(1, nx):
        j = lax.rem(xi + d, nx)
        block = s_ref[pl.ds(pl.multiple_of(j * rows, rows), rows), :]
        part[j] = jnp.dot(block, k_ref[...], preferred_element_type=jnp.float32)
        cp = pltpu.make_async_remote_copy(
            src_ref=part.at[j], dst_ref=rbuf.at[xi], send_sem=ss.at[j],
            recv_sem=rs.at[xi], device_id={"x": j}, device_id_type=MESH)
        cp.start()
        copies.append(cp)
    block = s_ref[pl.ds(pl.multiple_of(xi * rows, rows), rows), :]
    rbuf[xi] = jnp.dot(block, k_ref[...], preferred_element_type=jnp.float32)
    for d in range(1, nx):
        j = lax.rem(xi + d, nx)
        pltpu.make_async_remote_copy(
            src_ref=part.at[j], dst_ref=rbuf.at[j], send_sem=ss.at[j],
            recv_sem=rs.at[j], device_id={"x": j}, device_id_type=MESH).wait_recv()
    acc = rbuf[0]
    for j in range(1, nx):
        acc = acc + rbuf[j]
    o_ref[...] = acc
    for cp in copies:
        cp.wait_send()


def sketch_scatter(snapshots, sketch, nx):
    cells = snapshots.shape[0]
    rows = cells // nx
    cols = sketch.shape[1]
    dma = pltpu.SemaphoreType.DMA
    return pl.pallas_call(
        functools.partial(scatter_kernel, nx),
        out_shape=jax.ShapeDtypeStruct((rows, cols), jnp.float32),
        in_specs=[pl.BlockSpec(memory_space=pltpu.VMEM)] * 2,
        out_specs=pl.BlockSpec(memory_space=pltpu.VMEM),
        scratch_shapes=[
            pltpu.VMEM((nx, rows, cols), jnp.float32),
            pltpu.VMEM((nx, rows, cols), jnp.float32),
            dma((nx,)), dma((nx,)),
        ],
        compiler_params=pltpu.CompilerParams(collective_id=1, has_side_effects=True,
                                             vmem_limit_bytes=48 * 1024 * 1024),
    )(snapshots, sketch)


def factor_kernel(b, g_ref, l_ref, w_ref):
    n = g_ref.shape[0]
    hi = lax.Precision.HIGHEST
    l_ref[...] = jnp.zeros_like(l_ref)
    w_ref[...] = jnp.zeros_like(w_ref)
    nt = (((1,), (1,)), ((), ()))
    rows = lax.broadcasted_iota(jnp.int32, (b, b), 0)
    cols = lax.broadcasted_iota(jnp.int32, (b, b), 1)

    def panel(p, carry):
        r0 = pl.multiple_of(p * b, b)
        arow = g_ref[pl.ds(r0, b), :]
        w = w_ref[...]
        x = lax.dot_general(arow, w, nt, precision=hi, preferred_element_type=jnp.float32)
        pick = (lax.broadcasted_iota(jnp.int32, (n, b), 0)
                == r0 + lax.broadcasted_iota(jnp.int32, (n, b), 1)).astype(jnp.float32)
        place = (lax.broadcasted_iota(jnp.int32, (b, n), 1)
                 == r0 + lax.broadcasted_iota(jnp.int32, (b, n), 0)).astype(jnp.float32)
        s = jnp.dot(arow, pick, precision=hi, preferred_element_type=jnp.float32)
        s = s - lax.dot_general(x, x, nt, precision=hi, preferred_element_type=jnp.float32)
        low = jnp.zeros((b, b), jnp.float32)
        inv = jnp.zeros((b, b), jnp.float32)
        rest = (rows == cols).astype(jnp.float32)
        for i in range(b):
            root = jnp.sqrt(s[i:i + 1, i:i + 1])
            col = jnp.where(rows[:, i:i + 1] >= i, s[:, i:i + 1] / root, 0.0)
            row = jnp.where(cols[i:i + 1, :] >= i, s[i:i + 1, :] / root, 0.0)
            s = s - col * row
            low = jnp.where(cols == i, col, low)
            irow = rest[i:i + 1, :] / col[i:i + 1, :]
            inv = jnp.where(rows == i, irow, inv)
            rest = rest - col * irow
        l_ref[pl.ds(r0, b), :] = x + jnp.dot(low, place, precision=hi,
                                             preferred_element_type=jnp.float32)
        y = jnp.dot(x, w, precision=hi, preferred_element_type=jnp.float32)
        w_ref[pl.ds(r0, b), :] = jnp.dot(inv, place - y, precision=hi,
                                         preferred_element_type=jnp.float32)
        return carry

    lax.fori_loop(0, n // b, panel, 0)


def factor(gram, b=64):
    n = gram.shape[0]
    return pl.pallas_call(
        functools.partial(factor_kernel, b),
        out_shape=(jax.ShapeDtypeStruct((n, n), jnp.float32),) * 2,
        in_specs=[pl.BlockSpec(memory_space=pltpu.VMEM)],
        out_specs=(pl.BlockSpec(memory_space=pltpu.VMEM),) * 2,
    )(gram)


def shards(sizes, snapshots, sketch, rotation):
    sketched = sketch_scatter(snapshots, sketch, sizes[3])
    gram = lax.dot_general(
        sketched,
        sketched,
        (((0,), (0,)), ((), ())),
        precision=lax.Precision.HIGHEST,
        preferred_element_type=jnp.float32,
    )
    gram = all_sum(gram, sizes)
    lower, inverse = factor(gram)
    rotated = lax.dot_general(
        inverse, rotation, (((0,), (0,)), ((), ())),
        precision=lax.Precision.HIGHEST, preferred_element_type=jnp.float32,
    )
    cell_count = sketched.shape[0] * sizes[0] * sizes[1] * sizes[2] * sizes[3]
    scale = jnp.sqrt(jnp.float32(cell_count))
    basis = scale * jnp.dot(
        sketched, rotated, precision=lax.Precision.HIGHEST, preferred_element_type=jnp.float32
    )
    triangle = lower.T / scale
    return (basis, triangle)


def physical_mesh(mesh):
    space, tm = mesh.devices.shape
    nc = 2
    ny = 4 if space % 8 == 0 else 1
    nz = space // (ny * nc)
    devs = mesh.devices.reshape(nz, ny, nc, tm)
    return Mesh(devs, AXES), (nz, ny, nc, tm)


def solution(mesh):
    m4, sizes = physical_mesh(mesh)
    in_specs = (P(SPACE, "x"), P("x", None), P())
    out_specs = (P(AXES, None), P())
    return jax.shard_map(functools.partial(shards, sizes), mesh=m4, in_specs=in_specs,
                         out_specs=out_specs, check_vma=False)
```

```python
import functools

import jax
import jax.numpy as jnp
from jax import lax
from jax.experimental import pallas as pl
from jax.experimental.pallas import tpu as pltpu
from jax.sharding import Mesh, PartitionSpec as P

MESH = pl.DeviceIdType.MESH
AXES = ("z", "y", "c", "x")
SPACE = ("z", "y", "c")


def sum_kernel(sizes, a_ref, o_ref, cbuf, csum, xbuf, xsum, ybuf, ysum, zbuf, full,
               cr, cs, xr, xs, yr, ys, zr, zs, ygr, ygs, xgr, xgs, cgr, cgs):
    nz, ny, nc, nx = sizes
    zi, yi, ci, xi = (lax.axis_index(a) for a in AXES)

    def peers(n, me):
        return [lax.rem(me + d, n) for d in range(1, n)]

    barrier = pltpu.get_barrier_semaphore()
    count = 0
    for n, me, make in (
        (nz, zi, lambda j: (j, yi, ci, xi)),
        (ny, yi, lambda j: (zi, j, ci, xi)),
        (nc, ci, lambda j: (zi, yi, j, xi)),
        (nx, xi, lambda j: (zi, yi, ci, j)),
    ):
        for j in peers(n, me):
            pl.semaphore_signal(barrier, inc=1, device_id=make(j), device_id_type=MESH)
            count += 1
    pl.semaphore_wait(barrier, count)

    def exchange(n, me, make, src_of, dst_of, rsem, ssem):
        copies = []
        for j in peers(n, me):
            cp = pltpu.make_async_remote_copy(
                src_ref=src_of(j), dst_ref=dst_of(me), send_sem=ssem.at[j],
                recv_sem=rsem.at[me], device_id=make(j), device_id_type=MESH)
            cp.start()
            copies.append(cp)
        for j in peers(n, me):
            pltpu.make_async_remote_copy(
                src_ref=src_of(j), dst_ref=dst_of(j), send_sem=ssem.at[j],
                recv_sem=rsem.at[j], device_id=make(j), device_id_type=MESH).wait_recv()
        for cp in copies:
            cp.wait_send()

    def ordered_sum(buf, n):
        acc = buf[0]
        for j in range(1, n):
            acc = acc + buf[j]
        return acc

    c1 = a_ref.shape[0] // nc
    c2 = c1 // nx
    c3 = c2 // ny
    zdev = lambda j: (j, yi, ci, xi)
    ydev = lambda j: (zi, j, ci, xi)
    cdev = lambda j: (zi, yi, j, xi)
    xdev = lambda j: (zi, yi, ci, j)

    cbuf[ci] = a_ref[pl.ds(ci * c1, c1)]
    exchange(nc, ci, cdev, lambda j: a_ref.at[pl.ds(j * c1, c1)], lambda j: cbuf.at[j], cr, cs)
    csum[...] = ordered_sum(cbuf, nc)

    xbuf[xi] = csum[pl.ds(xi * c2, c2)]
    exchange(nx, xi, xdev, lambda j: csum.at[pl.ds(j * c2, c2)], lambda j: xbuf.at[j], xr, xs)
    xsum[...] = ordered_sum(xbuf, nx)

    ybuf[yi] = xsum[pl.ds(yi * c3, c3)]
    exchange(ny, yi, ydev, lambda j: xsum.at[pl.ds(j * c3, c3)], lambda j: ybuf.at[j], yr, ys)
    ysum[...] = ordered_sum(ybuf, ny)

    zbuf[zi] = ysum[...]
    exchange(nz, zi, zdev, lambda j: ysum, lambda j: zbuf.at[j], zr, zs)
    own = ci * c1 + xi * c2 + yi * c3
    full[pl.ds(own, c3)] = ordered_sum(zbuf, nz)

    exchange(ny, yi, ydev, lambda j: full.at[pl.ds(own, c3)],
             lambda j: full.at[pl.ds(ci * c1 + xi * c2 + j * c3, c3)], ygr, ygs)
    exchange(nx, xi, xdev, lambda j: full.at[pl.ds(ci * c1 + xi * c2, c2)],
             lambda j: full.at[pl.ds(ci * c1 + j * c2, c2)], xgr, xgs)
    exchange(nc, ci, cdev, lambda j: full.at[pl.ds(ci * c1, c1)],
             lambda j: full.at[pl.ds(j * c1, c1)], cgr, cgs)
    o_ref[...] = full[...]


def all_sum(gram, sizes):
    nz, ny, nc, nx = sizes
    c1 = gram.shape[0] // nc
    c2 = c1 // nx
    c3 = c2 // ny
    t = gram.shape[1:]
    dma = pltpu.SemaphoreType.DMA
    return pl.pallas_call(
        functools.partial(sum_kernel, sizes),
        out_shape=jax.ShapeDtypeStruct(gram.shape, jnp.float32),
        in_specs=[pl.BlockSpec(memory_space=pltpu.VMEM)],
        out_specs=pl.BlockSpec(memory_space=pltpu.VMEM),
        scratch_shapes=[
            pltpu.VMEM((nc, c1) + t, jnp.float32),
            pltpu.VMEM((c1,) + t, jnp.float32),
            pltpu.VMEM((nx, c2) + t, jnp.float32),
            pltpu.VMEM((c2,) + t, jnp.float32),
            pltpu.VMEM((ny, c3) + t, jnp.float32),
            pltpu.VMEM((c3,) + t, jnp.float32),
            pltpu.VMEM((nz, c3) + t, jnp.float32),
            pltpu.VMEM(gram.shape, jnp.float32),
            dma((nc,)), dma((nc,)), dma((nx,)), dma((nx,)),
            dma((ny,)), dma((ny,)), dma((nz,)), dma((nz,)),
            dma((ny,)), dma((ny,)), dma((nx,)), dma((nx,)),
            dma((nc,)), dma((nc,)),
        ],
        compiler_params=pltpu.CompilerParams(collective_id=0, has_side_effects=True),
    )(gram)


def scatter_kernel(nx, s_ref, k_ref, o_ref, part, rbuf, rs, ss):
    xi = lax.axis_index("x")
    rows = o_ref.shape[0]

    barrier = pltpu.get_barrier_semaphore()
    for d in range(1, nx):
        pl.semaphore_signal(barrier, inc=1, device_id={"x": lax.rem(xi + d, nx)},
                            device_id_type=MESH)
    pl.semaphore_wait(barrier, nx - 1)

    copies = []
    for d in range(1, nx):
        j = lax.rem(xi + d, nx)
        block = s_ref[pl.ds(pl.multiple_of(j * rows, rows), rows), :]
        part[j] = jnp.dot(block, k_ref[...], preferred_element_type=jnp.float32)
        cp = pltpu.make_async_remote_copy(
            src_ref=part.at[j], dst_ref=rbuf.at[xi], send_sem=ss.at[j],
            recv_sem=rs.at[xi], device_id={"x": j}, device_id_type=MESH)
        cp.start()
        copies.append(cp)
    block = s_ref[pl.ds(pl.multiple_of(xi * rows, rows), rows), :]
    rbuf[xi] = jnp.dot(block, k_ref[...], preferred_element_type=jnp.float32)
    for d in range(1, nx):
        j = lax.rem(xi + d, nx)
        pltpu.make_async_remote_copy(
            src_ref=part.at[j], dst_ref=rbuf.at[j], send_sem=ss.at[j],
            recv_sem=rs.at[j], device_id={"x": j}, device_id_type=MESH).wait_recv()
    acc = rbuf[0]
    for j in range(1, nx):
        acc = acc + rbuf[j]
    o_ref[...] = acc
    for cp in copies:
        cp.wait_send()


def sketch_scatter(snapshots, sketch, nx):
    cells = snapshots.shape[0]
    rows = cells // nx
    cols = sketch.shape[1]
    dma = pltpu.SemaphoreType.DMA
    return pl.pallas_call(
        functools.partial(scatter_kernel, nx),
        out_shape=jax.ShapeDtypeStruct((rows, cols), jnp.float32),
        in_specs=[pl.BlockSpec(memory_space=pltpu.VMEM)] * 2,
        out_specs=pl.BlockSpec(memory_space=pltpu.VMEM),
        scratch_shapes=[
            pltpu.VMEM((nx, rows, cols), jnp.float32),
            pltpu.VMEM((nx, rows, cols), jnp.float32),
            dma((nx,)), dma((nx,)),
        ],
        compiler_params=pltpu.CompilerParams(collective_id=1, has_side_effects=True,
                                             vmem_limit_bytes=48 * 1024 * 1024),
    )(snapshots, sketch)


def factor_kernel(b, g_ref, l_ref, w_ref):
    n = g_ref.shape[0]
    hi = lax.Precision.HIGHEST
    l_ref[...] = jnp.zeros_like(l_ref)
    w_ref[...] = jnp.zeros_like(w_ref)
    nt = (((1,), (1,)), ((), ()))
    rows = lax.broadcasted_iota(jnp.int32, (b, b), 0)
    cols = lax.broadcasted_iota(jnp.int32, (b, b), 1)

    def panel(p, carry):
        r0 = pl.multiple_of(p * b, b)
        arow = g_ref[pl.ds(r0, b), :]
        w = w_ref[...]
        x = lax.dot_general(arow, w, nt, precision=hi, preferred_element_type=jnp.float32)
        pick = (lax.broadcasted_iota(jnp.int32, (n, b), 0)
                == r0 + lax.broadcasted_iota(jnp.int32, (n, b), 1)).astype(jnp.float32)
        place = (lax.broadcasted_iota(jnp.int32, (b, n), 1)
                 == r0 + lax.broadcasted_iota(jnp.int32, (b, n), 0)).astype(jnp.float32)
        s = jnp.dot(arow, pick, precision=hi, preferred_element_type=jnp.float32)
        s = s - lax.dot_general(x, x, nt, precision=hi, preferred_element_type=jnp.float32)
        low = jnp.zeros((b, b), jnp.float32)
        inv = jnp.zeros((b, b), jnp.float32)
        rest = (rows == cols).astype(jnp.float32)
        for i in range(b):
            pivot = s[i:i + 1, i:i + 1]
            left = s[:, i:i + 1]
            s = s - left * (s[i:i + 1, :] * (1.0 / pivot))
            col = jnp.where(rows[:, i:i + 1] >= i, left / jnp.sqrt(pivot), 0.0)
            low = jnp.where(cols == i, col, low)
            irow = rest[i:i + 1, :] / col[i:i + 1, :]
            inv = jnp.where(rows == i, irow, inv)
            rest = rest - col * irow
        l_ref[pl.ds(r0, b), :] = x + jnp.dot(low, place, precision=hi,
                                             preferred_element_type=jnp.float32)
        y = jnp.dot(x, w, precision=hi, preferred_element_type=jnp.float32)
        w_ref[pl.ds(r0, b), :] = jnp.dot(inv, place - y, precision=hi,
                                         preferred_element_type=jnp.float32)
        return carry

    lax.fori_loop(0, n // b, panel, 0)


def factor(gram, b=128):
    n = gram.shape[0]
    return pl.pallas_call(
        functools.partial(factor_kernel, b),
        out_shape=(jax.ShapeDtypeStruct((n, n), jnp.float32),) * 2,
        in_specs=[pl.BlockSpec(memory_space=pltpu.VMEM)],
        out_specs=(pl.BlockSpec(memory_space=pltpu.VMEM),) * 2,
    )(gram)


def shards(sizes, snapshots, sketch, rotation):
    sketched = sketch_scatter(snapshots, sketch, sizes[3])
    gram = lax.dot_general(
        sketched,
        sketched,
        (((0,), (0,)), ((), ())),
        precision=lax.Precision.HIGHEST,
        preferred_element_type=jnp.float32,
    )
    gram = all_sum(gram, sizes)
    lower, inverse = factor(gram)
    rotated = lax.dot_general(
        inverse, rotation, (((0,), (0,)), ((), ())),
        precision=lax.Precision.HIGHEST, preferred_element_type=jnp.float32,
    )
    cell_count = sketched.shape[0] * sizes[0] * sizes[1] * sizes[2] * sizes[3]
    scale = jnp.sqrt(jnp.float32(cell_count))
    basis = scale * jnp.dot(
        sketched, rotated, precision=lax.Precision.HIGHEST, preferred_element_type=jnp.float32
    )
    triangle = lower.T / scale
    return (basis, triangle)


def physical_mesh(mesh):
    space, tm = mesh.devices.shape
    nc = 2
    ny = 4 if space % 8 == 0 else 1
    nz = space // (ny * nc)
    devs = mesh.devices.reshape(nz, ny, nc, tm)
    return Mesh(devs, AXES), (nz, ny, nc, tm)


def solution(mesh):
    m4, sizes = physical_mesh(mesh)
    in_specs = (P(SPACE, "x"), P("x", None), P())
    out_specs = (P(AXES, None), P())
    return jax.shard_map(functools.partial(shards, sizes), mesh=m4, in_specs=in_specs,
                         out_specs=out_specs, check_vma=False)
```

```python
import functools

import jax
import jax.numpy as jnp
from jax import lax
from jax.experimental import pallas as pl
from jax.experimental.pallas import tpu as pltpu
from jax.sharding import Mesh, PartitionSpec as P

MESH = pl.DeviceIdType.MESH
AXES = ("z", "y", "c", "x")
SPACE = ("z", "y", "c")


def sum_kernel(sizes, a_ref, o_ref, cbuf, csum, qbuf, qsum, zbuf, full,
               cr, cs, qr, qs, zr, zs, qgr, qgs, cgr, cgs):
    nz, ny, nc, nx = sizes
    nq = nx * ny
    zi, yi, ci, xi = (lax.axis_index(a) for a in AXES)
    qi = xi * ny + yi

    def peers(n, me):
        return [lax.rem(me + d, n) for d in range(1, n)]

    zdev = lambda j: (j, yi, ci, xi)
    cdev = lambda j: (zi, yi, j, xi)
    qdev = lambda q: (zi, lax.rem(q, ny), ci, q // ny)

    barrier = pltpu.get_barrier_semaphore()
    count = 0
    for n, me, make in ((nz, zi, zdev), (nq, qi, qdev), (nc, ci, cdev)):
        for j in peers(n, me):
            pl.semaphore_signal(barrier, inc=1, device_id=make(j), device_id_type=MESH)
            count += 1
    pl.semaphore_wait(barrier, count)

    def exchange(n, me, make, src_of, dst_of, rsem, ssem):
        copies = []
        for j in peers(n, me):
            cp = pltpu.make_async_remote_copy(
                src_ref=src_of(j), dst_ref=dst_of(me), send_sem=ssem.at[j],
                recv_sem=rsem.at[me], device_id=make(j), device_id_type=MESH)
            cp.start()
            copies.append(cp)
        for j in peers(n, me):
            pltpu.make_async_remote_copy(
                src_ref=src_of(j), dst_ref=dst_of(j), send_sem=ssem.at[j],
                recv_sem=rsem.at[j], device_id=make(j), device_id_type=MESH).wait_recv()
        for cp in copies:
            cp.wait_send()

    def ordered_sum(buf, n):
        acc = buf[0]
        for j in range(1, n):
            acc = acc + buf[j]
        return acc

    c1 = a_ref.shape[0] // nc
    c2 = c1 // nq

    cbuf[ci] = a_ref[pl.ds(ci * c1, c1)]
    exchange(nc, ci, cdev, lambda j: a_ref.at[pl.ds(j * c1, c1)], lambda j: cbuf.at[j], cr, cs)
    csum[...] = ordered_sum(cbuf, nc)

    qbuf[qi] = csum[pl.ds(qi * c2, c2)]
    exchange(nq, qi, qdev, lambda j: csum.at[pl.ds(j * c2, c2)], lambda j: qbuf.at[j], qr, qs)
    qsum[...] = ordered_sum(qbuf, nq)

    zbuf[zi] = qsum[...]
    exchange(nz, zi, zdev, lambda j: qsum, lambda j: zbuf.at[j], zr, zs)
    own = ci * c1 + qi * c2
    full[pl.ds(own, c2)] = ordered_sum(zbuf, nz)

    exchange(nq, qi, qdev, lambda j: full.at[pl.ds(own, c2)],
             lambda j: full.at[pl.ds(ci * c1 + j * c2, c2)], qgr, qgs)
    exchange(nc, ci, cdev, lambda j: full.at[pl.ds(ci * c1, c1)],
             lambda j: full.at[pl.ds(j * c1, c1)], cgr, cgs)
    o_ref[...] = full[...]


def all_sum(gram, sizes):
    nz, ny, nc, nx = sizes
    nq = nx * ny
    c1 = gram.shape[0] // nc
    c2 = c1 // nq
    t = gram.shape[1:]
    dma = pltpu.SemaphoreType.DMA
    return pl.pallas_call(
        functools.partial(sum_kernel, sizes),
        out_shape=jax.ShapeDtypeStruct(gram.shape, jnp.float32),
        in_specs=[pl.BlockSpec(memory_space=pltpu.VMEM)],
        out_specs=pl.BlockSpec(memory_space=pltpu.VMEM),
        scratch_shapes=[
            pltpu.VMEM((nc, c1) + t, jnp.float32),
            pltpu.VMEM((c1,) + t, jnp.float32),
            pltpu.VMEM((nq, c2) + t, jnp.float32),
            pltpu.VMEM((c2,) + t, jnp.float32),
            pltpu.VMEM((nz, c2) + t, jnp.float32),
            pltpu.VMEM(gram.shape, jnp.float32),
            dma((nc,)), dma((nc,)), dma((nq,)), dma((nq,)),
            dma((nz,)), dma((nz,)), dma((nq,)), dma((nq,)),
            dma((nc,)), dma((nc,)),
        ],
        compiler_params=pltpu.CompilerParams(collective_id=0, has_side_effects=True),
    )(gram)


def scatter_kernel(nx, s_ref, k_ref, o_ref, part, rbuf, rs, ss):
    xi = lax.axis_index("x")
    rows = o_ref.shape[0]

    barrier = pltpu.get_barrier_semaphore()
    for d in range(1, nx):
        pl.semaphore_signal(barrier, inc=1, device_id={"x": lax.rem(xi + d, nx)},
                            device_id_type=MESH)
    pl.semaphore_wait(barrier, nx - 1)

    copies = []
    for d in range(1, nx):
        j = lax.rem(xi + d, nx)
        block = s_ref[pl.ds(pl.multiple_of(j * rows, rows), rows), :]
        part[j] = jnp.dot(block, k_ref[...], preferred_element_type=jnp.float32)
        cp = pltpu.make_async_remote_copy(
            src_ref=part.at[j], dst_ref=rbuf.at[xi], send_sem=ss.at[j],
            recv_sem=rs.at[xi], device_id={"x": j}, device_id_type=MESH)
        cp.start()
        copies.append(cp)
    block = s_ref[pl.ds(pl.multiple_of(xi * rows, rows), rows), :]
    rbuf[xi] = jnp.dot(block, k_ref[...], preferred_element_type=jnp.float32)
    for d in range(1, nx):
        j = lax.rem(xi + d, nx)
        pltpu.make_async_remote_copy(
            src_ref=part.at[j], dst_ref=rbuf.at[j], send_sem=ss.at[j],
            recv_sem=rs.at[j], device_id={"x": j}, device_id_type=MESH).wait_recv()
    acc = rbuf[0]
    for j in range(1, nx):
        acc = acc + rbuf[j]
    o_ref[...] = acc
    for cp in copies:
        cp.wait_send()


def sketch_scatter(snapshots, sketch, nx):
    cells = snapshots.shape[0]
    rows = cells // nx
    cols = sketch.shape[1]
    dma = pltpu.SemaphoreType.DMA
    return pl.pallas_call(
        functools.partial(scatter_kernel, nx),
        out_shape=jax.ShapeDtypeStruct((rows, cols), jnp.float32),
        in_specs=[pl.BlockSpec(memory_space=pltpu.VMEM)] * 2,
        out_specs=pl.BlockSpec(memory_space=pltpu.VMEM),
        scratch_shapes=[
            pltpu.VMEM((nx, rows, cols), jnp.float32),
            pltpu.VMEM((nx, rows, cols), jnp.float32),
            dma((nx,)), dma((nx,)),
        ],
        compiler_params=pltpu.CompilerParams(collective_id=1, has_side_effects=True,
                                             vmem_limit_bytes=48 * 1024 * 1024),
    )(snapshots, sketch)


def factor_kernel(b, g_ref, l_ref, w_ref):
    n = g_ref.shape[0]
    hi = lax.Precision.HIGHEST
    l_ref[...] = jnp.zeros_like(l_ref)
    w_ref[...] = jnp.zeros_like(w_ref)
    nt = (((1,), (1,)), ((), ()))
    rows = lax.broadcasted_iota(jnp.int32, (b, b), 0)
    cols = lax.broadcasted_iota(jnp.int32, (b, b), 1)

    def panel(p, carry):
        r0 = pl.multiple_of(p * b, b)
        arow = g_ref[pl.ds(r0, b), :]
        w = w_ref[...]
        x = lax.dot_general(arow, w, nt, precision=hi, preferred_element_type=jnp.float32)
        pick = (lax.broadcasted_iota(jnp.int32, (n, b), 0)
                == r0 + lax.broadcasted_iota(jnp.int32, (n, b), 1)).astype(jnp.float32)
        place = (lax.broadcasted_iota(jnp.int32, (b, n), 1)
                 == r0 + lax.broadcasted_iota(jnp.int32, (b, n), 0)).astype(jnp.float32)
        s = jnp.dot(arow, pick, precision=hi, preferred_element_type=jnp.float32)
        s = s - lax.dot_general(x, x, nt, precision=hi, preferred_element_type=jnp.float32)
        low = jnp.zeros((b, b), jnp.float32)
        inv = jnp.zeros((b, b), jnp.float32)
        rest = (rows == cols).astype(jnp.float32)
        for i in range(b):
            pivot = s[i:i + 1, i:i + 1]
            left = s[:, i:i + 1]
            s = s - left * (s[i:i + 1, :] * (1.0 / pivot))
            col = jnp.where(rows[:, i:i + 1] >= i, left / jnp.sqrt(pivot), 0.0)
            low = jnp.where(cols == i, col, low)
            irow = rest[i:i + 1, :] / col[i:i + 1, :]
            inv = jnp.where(rows == i, irow, inv)
            rest = rest - col * irow
        l_ref[pl.ds(r0, b), :] = x + jnp.dot(low, place, precision=hi,
                                             preferred_element_type=jnp.float32)
        y = jnp.dot(x, w, precision=hi, preferred_element_type=jnp.float32)
        w_ref[pl.ds(r0, b), :] = jnp.dot(inv, place - y, precision=hi,
                                         preferred_element_type=jnp.float32)
        return carry

    lax.fori_loop(0, n // b, panel, 0)


def factor(gram, b=128):
    n = gram.shape[0]
    return pl.pallas_call(
        functools.partial(factor_kernel, b),
        out_shape=(jax.ShapeDtypeStruct((n, n), jnp.float32),) * 2,
        in_specs=[pl.BlockSpec(memory_space=pltpu.VMEM)],
        out_specs=(pl.BlockSpec(memory_space=pltpu.VMEM),) * 2,
    )(gram)


def shards(sizes, snapshots, sketch, rotation):
    sketched = sketch_scatter(snapshots, sketch, sizes[3])
    gram = lax.dot_general(
        sketched,
        sketched,
        (((0,), (0,)), ((), ())),
        precision=lax.Precision.HIGHEST,
        preferred_element_type=jnp.float32,
    )
    gram = all_sum(gram, sizes)
    lower, inverse = factor(gram)
    rotated = lax.dot_general(
        inverse, rotation, (((0,), (0,)), ((), ())),
        precision=lax.Precision.HIGHEST, preferred_element_type=jnp.float32,
    )
    cell_count = sketched.shape[0] * sizes[0] * sizes[1] * sizes[2] * sizes[3]
    scale = jnp.sqrt(jnp.float32(cell_count))
    basis = scale * jnp.dot(
        sketched, rotated, precision=lax.Precision.HIGHEST, preferred_element_type=jnp.float32
    )
    triangle = lower.T / scale
    return (basis, triangle)


def physical_mesh(mesh):
    space, tm = mesh.devices.shape
    nc = 2
    ny = 4 if space % 8 == 0 else 1
    nz = space // (ny * nc)
    devs = mesh.devices.reshape(nz, ny, nc, tm)
    return Mesh(devs, AXES), (nz, ny, nc, tm)


def solution(mesh):
    m4, sizes = physical_mesh(mesh)
    in_specs = (P(SPACE, "x"), P("x", None), P())
    out_specs = (P(AXES, None), P())
    return jax.shard_map(functools.partial(shards, sizes), mesh=m4, in_specs=in_specs,
                         out_specs=out_specs, check_vma=False)
```

```python
import functools

import jax
import jax.numpy as jnp
from jax import lax
from jax.experimental import pallas as pl
from jax.experimental.pallas import tpu as pltpu
from jax.sharding import Mesh, PartitionSpec as P

MESH = pl.DeviceIdType.MESH
AXES = ("z", "y", "c", "x")
SPACE = ("z", "y", "c")


def sum_kernel(sizes, a_ref, o_ref, qbuf, qsum, zbuf, full, qr, qs, zr, zs, qgr, qgs):
    nz, ny, nc, nx = sizes
    nq = nc * nx * ny
    zi, yi, ci, xi = (lax.axis_index(a) for a in AXES)
    qi = (ci * nx + xi) * ny + yi

    def peers(n, me):
        return [lax.rem(me + d, n) for d in range(1, n)]

    zdev = lambda j: (j, yi, ci, xi)
    qdev = lambda q: (zi, lax.rem(q, ny), q // (nx * ny), lax.rem(q // ny, nx))

    barrier = pltpu.get_barrier_semaphore()
    count = 0
    for n, me, make in ((nz, zi, zdev), (nq, qi, qdev)):
        for j in peers(n, me):
            pl.semaphore_signal(barrier, inc=1, device_id=make(j), device_id_type=MESH)
            count += 1
    pl.semaphore_wait(barrier, count)

    def exchange(n, me, make, src_of, dst_of, rsem, ssem):
        copies = []
        for j in peers(n, me):
            cp = pltpu.make_async_remote_copy(
                src_ref=src_of(j), dst_ref=dst_of(me), send_sem=ssem.at[j],
                recv_sem=rsem.at[me], device_id=make(j), device_id_type=MESH)
            cp.start()
            copies.append(cp)
        for j in peers(n, me):
            pltpu.make_async_remote_copy(
                src_ref=src_of(j), dst_ref=dst_of(j), send_sem=ssem.at[j],
                recv_sem=rsem.at[j], device_id=make(j), device_id_type=MESH).wait_recv()
        for cp in copies:
            cp.wait_send()

    def ordered_sum(buf, n):
        acc = buf[0]
        for j in range(1, n):
            acc = acc + buf[j]
        return acc

    c1 = a_ref.shape[0] // nq

    qbuf[qi] = a_ref[pl.ds(qi * c1, c1)]
    exchange(nq, qi, qdev, lambda j: a_ref.at[pl.ds(j * c1, c1)], lambda j: qbuf.at[j], qr, qs)
    qsum[...] = ordered_sum(qbuf, nq)

    zbuf[zi] = qsum[...]
    exchange(nz, zi, zdev, lambda j: qsum, lambda j: zbuf.at[j], zr, zs)
    own = qi * c1
    full[pl.ds(own, c1)] = ordered_sum(zbuf, nz)

    exchange(nq, qi, qdev, lambda j: full.at[pl.ds(own, c1)],
             lambda j: full.at[pl.ds(j * c1, c1)], qgr, qgs)
    o_ref[...] = full[...]


def all_sum(gram, sizes):
    nz, ny, nc, nx = sizes
    nq = nc * nx * ny
    c1 = gram.shape[0] // nq
    t = gram.shape[1:]
    dma = pltpu.SemaphoreType.DMA
    return pl.pallas_call(
        functools.partial(sum_kernel, sizes),
        out_shape=jax.ShapeDtypeStruct(gram.shape, jnp.float32),
        in_specs=[pl.BlockSpec(memory_space=pltpu.VMEM)],
        out_specs=pl.BlockSpec(memory_space=pltpu.VMEM),
        scratch_shapes=[
            pltpu.VMEM((nq, c1) + t, jnp.float32),
            pltpu.VMEM((c1,) + t, jnp.float32),
            pltpu.VMEM((nz, c1) + t, jnp.float32),
            pltpu.VMEM(gram.shape, jnp.float32),
            dma((nq,)), dma((nq,)), dma((nz,)), dma((nz,)), dma((nq,)), dma((nq,)),
        ],
        compiler_params=pltpu.CompilerParams(collective_id=0, has_side_effects=True),
    )(gram)


def scatter_kernel(nx, s_ref, k_ref, o_ref, part, rbuf, rs, ss):
    xi = lax.axis_index("x")
    rows = o_ref.shape[0]

    barrier = pltpu.get_barrier_semaphore()
    for d in range(1, nx):
        pl.semaphore_signal(barrier, inc=1, device_id={"x": lax.rem(xi + d, nx)},
                            device_id_type=MESH)
    pl.semaphore_wait(barrier, nx - 1)

    copies = []
    for d in range(1, nx):
        j = lax.rem(xi + d, nx)
        block = s_ref[pl.ds(pl.multiple_of(j * rows, rows), rows), :]
        part[j] = jnp.dot(block, k_ref[...], preferred_element_type=jnp.float32)
        cp = pltpu.make_async_remote_copy(
            src_ref=part.at[j], dst_ref=rbuf.at[xi], send_sem=ss.at[j],
            recv_sem=rs.at[xi], device_id={"x": j}, device_id_type=MESH)
        cp.start()
        copies.append(cp)
    block = s_ref[pl.ds(pl.multiple_of(xi * rows, rows), rows), :]
    rbuf[xi] = jnp.dot(block, k_ref[...], preferred_element_type=jnp.float32)
    for d in range(1, nx):
        j = lax.rem(xi + d, nx)
        pltpu.make_async_remote_copy(
            src_ref=part.at[j], dst_ref=rbuf.at[j], send_sem=ss.at[j],
            recv_sem=rs.at[j], device_id={"x": j}, device_id_type=MESH).wait_recv()
    acc = rbuf[0]
    for j in range(1, nx):
        acc = acc + rbuf[j]
    o_ref[...] = acc
    for cp in copies:
        cp.wait_send()


def sketch_scatter(snapshots, sketch, nx):
    cells = snapshots.shape[0]
    rows = cells // nx
    cols = sketch.shape[1]
    dma = pltpu.SemaphoreType.DMA
    return pl.pallas_call(
        functools.partial(scatter_kernel, nx),
        out_shape=jax.ShapeDtypeStruct((rows, cols), jnp.float32),
        in_specs=[pl.BlockSpec(memory_space=pltpu.VMEM)] * 2,
        out_specs=pl.BlockSpec(memory_space=pltpu.VMEM),
        scratch_shapes=[
            pltpu.VMEM((nx, rows, cols), jnp.float32),
            pltpu.VMEM((nx, rows, cols), jnp.float32),
            dma((nx,)), dma((nx,)),
        ],
        compiler_params=pltpu.CompilerParams(collective_id=1, has_side_effects=True,
                                             vmem_limit_bytes=48 * 1024 * 1024),
    )(snapshots, sketch)


def factor_kernel(b, g_ref, l_ref, w_ref):
    n = g_ref.shape[0]
    hi = lax.Precision.HIGHEST
    l_ref[...] = jnp.zeros_like(l_ref)
    w_ref[...] = jnp.zeros_like(w_ref)
    nt = (((1,), (1,)), ((), ()))
    rows = lax.broadcasted_iota(jnp.int32, (b, b), 0)
    cols = lax.broadcasted_iota(jnp.int32, (b, b), 1)

    def panel(p, carry):
        r0 = pl.multiple_of(p * b, b)
        arow = g_ref[pl.ds(r0, b), :]
        w = w_ref[...]
        x = lax.dot_general(arow, w, nt, precision=hi, preferred_element_type=jnp.float32)
        pick = (lax.broadcasted_iota(jnp.int32, (n, b), 0)
                == r0 + lax.broadcasted_iota(jnp.int32, (n, b), 1)).astype(jnp.float32)
        place = (lax.broadcasted_iota(jnp.int32, (b, n), 1)
                 == r0 + lax.broadcasted_iota(jnp.int32, (b, n), 0)).astype(jnp.float32)
        s = jnp.dot(arow, pick, precision=hi, preferred_element_type=jnp.float32)
        s = s - lax.dot_general(x, x, nt, precision=hi, preferred_element_type=jnp.float32)
        low = jnp.zeros((b, b), jnp.float32)
        inv = jnp.zeros((b, b), jnp.float32)
        rest = (rows == cols).astype(jnp.float32)
        for i in range(b):
            pivot = s[i:i + 1, i:i + 1]
            left = s[:, i:i + 1]
            s = s - left * (s[i:i + 1, :] * (1.0 / pivot))
            col = jnp.where(rows[:, i:i + 1] >= i, left / jnp.sqrt(pivot), 0.0)
            low = jnp.where(cols == i, col, low)
            irow = rest[i:i + 1, :] / col[i:i + 1, :]
            inv = jnp.where(rows == i, irow, inv)
            rest = rest - col * irow
        l_ref[pl.ds(r0, b), :] = x + jnp.dot(low, place, precision=hi,
                                             preferred_element_type=jnp.float32)
        y = jnp.dot(x, w, precision=hi, preferred_element_type=jnp.float32)
        w_ref[pl.ds(r0, b), :] = jnp.dot(inv, place - y, precision=hi,
                                         preferred_element_type=jnp.float32)
        return carry

    lax.fori_loop(0, n // b, panel, 0)


def factor(gram, b=128):
    n = gram.shape[0]
    return pl.pallas_call(
        functools.partial(factor_kernel, b),
        out_shape=(jax.ShapeDtypeStruct((n, n), jnp.float32),) * 2,
        in_specs=[pl.BlockSpec(memory_space=pltpu.VMEM)],
        out_specs=(pl.BlockSpec(memory_space=pltpu.VMEM),) * 2,
    )(gram)


def shards(sizes, snapshots, sketch, rotation):
    sketched = sketch_scatter(snapshots, sketch, sizes[3])
    gram = lax.dot_general(
        sketched,
        sketched,
        (((0,), (0,)), ((), ())),
        precision=lax.Precision.HIGHEST,
        preferred_element_type=jnp.float32,
    )
    gram = all_sum(gram, sizes)
    lower, inverse = factor(gram)
    rotated = lax.dot_general(
        inverse, rotation, (((0,), (0,)), ((), ())),
        precision=lax.Precision.HIGHEST, preferred_element_type=jnp.float32,
    )
    cell_count = sketched.shape[0] * sizes[0] * sizes[1] * sizes[2] * sizes[3]
    scale = jnp.sqrt(jnp.float32(cell_count))
    basis = scale * jnp.dot(
        sketched, rotated, precision=lax.Precision.HIGHEST, preferred_element_type=jnp.float32
    )
    triangle = lower.T / scale
    return (basis, triangle)


def physical_mesh(mesh):
    space, tm = mesh.devices.shape
    nc = 2
    ny = 4 if space % 8 == 0 else 1
    nz = space // (ny * nc)
    devs = mesh.devices.reshape(nz, ny, nc, tm)
    return Mesh(devs, AXES), (nz, ny, nc, tm)


def solution(mesh):
    m4, sizes = physical_mesh(mesh)
    in_specs = (P(SPACE, "x"), P("x", None), P())
    out_specs = (P(AXES, None), P())
    return jax.shard_map(functools.partial(shards, sizes), mesh=m4, in_specs=in_specs,
                         out_specs=out_specs, check_vma=False)
```

```python
import functools

import jax
import numpy as np
import jax.numpy as jnp
from jax import lax
from jax.experimental import pallas as pl
from jax.experimental.pallas import tpu as pltpu
from jax.sharding import Mesh, PartitionSpec as P

MESH = pl.DeviceIdType.MESH
AXES = ("z", "y", "c", "x")
SPACE = ("z", "y", "c")


def sum_kernel(sizes, a_ref, o_ref, qbuf, qsum, zbuf, full, qr, qs, zr, zs, qgr, qgs):
    nz, ny, nc, nx = sizes
    nq = nc * nx * ny
    zi, yi, ci, xi = (lax.axis_index(a) for a in AXES)
    qi = (ci * nx + xi) * ny + yi

    def peers(n, me):
        return [lax.rem(me + d, n) for d in range(1, n)]

    zdev = lambda j: (j, yi, ci, xi)
    qdev = lambda q: (zi, lax.rem(q, ny), q // (nx * ny), lax.rem(q // ny, nx))

    barrier = pltpu.get_barrier_semaphore()
    count = 0
    for n, me, make in ((nz, zi, zdev), (nq, qi, qdev)):
        for j in peers(n, me):
            pl.semaphore_signal(barrier, inc=1, device_id=make(j), device_id_type=MESH)
            count += 1
    pl.semaphore_wait(barrier, count)

    def exchange(n, me, make, src_of, dst_of, rsem, ssem):
        copies = []
        for j in peers(n, me):
            cp = pltpu.make_async_remote_copy(
                src_ref=src_of(j), dst_ref=dst_of(me), send_sem=ssem.at[j],
                recv_sem=rsem.at[me], device_id=make(j), device_id_type=MESH)
            cp.start()
            copies.append(cp)
        for j in peers(n, me):
            pltpu.make_async_remote_copy(
                src_ref=src_of(j), dst_ref=dst_of(j), send_sem=ssem.at[j],
                recv_sem=rsem.at[j], device_id=make(j), device_id_type=MESH).wait_recv()
        for cp in copies:
            cp.wait_send()

    def ordered_sum(buf, n):
        acc = buf[0]
        for j in range(1, n):
            acc = acc + buf[j]
        return acc

    c1 = a_ref.shape[0] // nq

    qbuf[qi] = a_ref[pl.ds(qi * c1, c1)]
    exchange(nq, qi, qdev, lambda j: a_ref.at[pl.ds(j * c1, c1)], lambda j: qbuf.at[j], qr, qs)
    qsum[...] = ordered_sum(qbuf, nq)

    zbuf[zi] = qsum[...]
    exchange(nz, zi, zdev, lambda j: qsum, lambda j: zbuf.at[j], zr, zs)
    own = qi * c1
    full[pl.ds(own, c1)] = ordered_sum(zbuf, nz)

    exchange(nq, qi, qdev, lambda j: full.at[pl.ds(own, c1)],
             lambda j: full.at[pl.ds(j * c1, c1)], qgr, qgs)
    o_ref[...] = full[...]


def all_sum(gram, sizes):
    nz, ny, nc, nx = sizes
    nq = nc * nx * ny
    c1 = gram.shape[0] // nq
    t = gram.shape[1:]
    dma = pltpu.SemaphoreType.DMA
    return pl.pallas_call(
        functools.partial(sum_kernel, sizes),
        out_shape=jax.ShapeDtypeStruct(gram.shape, jnp.float32),
        in_specs=[pl.BlockSpec(memory_space=pltpu.VMEM)],
        out_specs=pl.BlockSpec(memory_space=pltpu.VMEM),
        scratch_shapes=[
            pltpu.VMEM((nq, c1) + t, jnp.float32),
            pltpu.VMEM((c1,) + t, jnp.float32),
            pltpu.VMEM((nz, c1) + t, jnp.float32),
            pltpu.VMEM(gram.shape, jnp.float32),
            dma((nq,)), dma((nq,)), dma((nz,)), dma((nz,)), dma((nq,)), dma((nq,)),
        ],
        compiler_params=pltpu.CompilerParams(collective_id=0, has_side_effects=True),
    )(gram)


def scatter_kernel(nx, s_ref, k_ref, o_ref, part, rbuf, rs, ss):
    xi = lax.axis_index("x")
    rows = o_ref.shape[0]

    barrier = pltpu.get_barrier_semaphore()
    for d in range(1, nx):
        pl.semaphore_signal(barrier, inc=1, device_id={"x": lax.rem(xi + d, nx)},
                            device_id_type=MESH)
    pl.semaphore_wait(barrier, nx - 1)

    copies = []
    for d in range(1, nx):
        j = lax.rem(xi + d, nx)
        block = s_ref[pl.ds(pl.multiple_of(j * rows, rows), rows), :]
        part[j] = jnp.dot(block, k_ref[...], preferred_element_type=jnp.float32)
        cp = pltpu.make_async_remote_copy(
            src_ref=part.at[j], dst_ref=rbuf.at[xi], send_sem=ss.at[j],
            recv_sem=rs.at[xi], device_id={"x": j}, device_id_type=MESH)
        cp.start()
        copies.append(cp)
    block = s_ref[pl.ds(pl.multiple_of(xi * rows, rows), rows), :]
    rbuf[xi] = jnp.dot(block, k_ref[...], preferred_element_type=jnp.float32)
    for d in range(1, nx):
        j = lax.rem(xi + d, nx)
        pltpu.make_async_remote_copy(
            src_ref=part.at[j], dst_ref=rbuf.at[j], send_sem=ss.at[j],
            recv_sem=rs.at[j], device_id={"x": j}, device_id_type=MESH).wait_recv()
    acc = rbuf[0]
    for j in range(1, nx):
        acc = acc + rbuf[j]
    o_ref[...] = acc
    for cp in copies:
        cp.wait_send()


def sketch_scatter(snapshots, sketch, nx):
    cells = snapshots.shape[0]
    rows = cells // nx
    cols = sketch.shape[1]
    dma = pltpu.SemaphoreType.DMA
    return pl.pallas_call(
        functools.partial(scatter_kernel, nx),
        out_shape=jax.ShapeDtypeStruct((rows, cols), jnp.float32),
        in_specs=[pl.BlockSpec(memory_space=pltpu.VMEM)] * 2,
        out_specs=pl.BlockSpec(memory_space=pltpu.VMEM),
        scratch_shapes=[
            pltpu.VMEM((nx, rows, cols), jnp.float32),
            pltpu.VMEM((nx, rows, cols), jnp.float32),
            dma((nx,)), dma((nx,)),
        ],
        compiler_params=pltpu.CompilerParams(collective_id=1, has_side_effects=True,
                                             vmem_limit_bytes=48 * 1024 * 1024),
    )(snapshots, sketch)


def factor_kernel(b, scale, g_ref, q_ref, r_ref, basis_ref, tri_ref, l_ref, w_ref):
    n = g_ref.shape[0]
    hi = lax.Precision.HIGHEST
    l_ref[...] = jnp.zeros_like(l_ref)
    w_ref[...] = jnp.zeros_like(w_ref)
    nt = (((1,), (1,)), ((), ()))
    rows = lax.broadcasted_iota(jnp.int32, (b, b), 0)
    cols = lax.broadcasted_iota(jnp.int32, (b, b), 1)

    def panel(p, carry):
        r0 = pl.multiple_of(p * b, b)
        arow = g_ref[pl.ds(r0, b), :]
        w = w_ref[...]
        x = lax.dot_general(arow, w, nt, precision=hi, preferred_element_type=jnp.float32)
        pick = (lax.broadcasted_iota(jnp.int32, (n, b), 0)
                == r0 + lax.broadcasted_iota(jnp.int32, (n, b), 1)).astype(jnp.float32)
        place = (lax.broadcasted_iota(jnp.int32, (b, n), 1)
                 == r0 + lax.broadcasted_iota(jnp.int32, (b, n), 0)).astype(jnp.float32)
        s = jnp.dot(arow, pick, precision=hi, preferred_element_type=jnp.float32)
        s = s - lax.dot_general(x, x, nt, precision=hi, preferred_element_type=jnp.float32)
        low = jnp.zeros((b, b), jnp.float32)
        inv = jnp.zeros((b, b), jnp.float32)
        rest = (rows == cols).astype(jnp.float32)
        for i in range(b):
            pivot = s[i:i + 1, i:i + 1]
            left = s[:, i:i + 1]
            s = s - left * (s[i:i + 1, :] * (1.0 / pivot))
            col = jnp.where(rows[:, i:i + 1] >= i, left / jnp.sqrt(pivot), 0.0)
            low = jnp.where(cols == i, col, low)
            irow = rest[i:i + 1, :] / col[i:i + 1, :]
            inv = jnp.where(rows == i, irow, inv)
            rest = rest - col * irow
        l_ref[pl.ds(r0, b), :] = x + jnp.dot(low, place, precision=hi,
                                             preferred_element_type=jnp.float32)
        y = jnp.dot(x, w, precision=hi, preferred_element_type=jnp.float32)
        w_ref[pl.ds(r0, b), :] = jnp.dot(inv, place - y, precision=hi,
                                         preferred_element_type=jnp.float32)
        return carry

    lax.fori_loop(0, n // b, panel, 0)
    rotated = lax.dot_general(w_ref[...], r_ref[...], (((0,), (0,)), ((), ())), precision=hi,
                              preferred_element_type=jnp.float32)
    basis_ref[...] = scale * jnp.dot(q_ref[...], rotated, precision=hi,
                                     preferred_element_type=jnp.float32)
    tri_ref[...] = l_ref[...].T / scale


def factor(gram, sketched, rotation, scale, b=128):
    n = gram.shape[0]
    return pl.pallas_call(
        functools.partial(factor_kernel, b, scale),
        out_shape=(jax.ShapeDtypeStruct(sketched.shape, jnp.float32),
                   jax.ShapeDtypeStruct((n, n), jnp.float32)),
        in_specs=[pl.BlockSpec(memory_space=pltpu.VMEM)] * 3,
        out_specs=(pl.BlockSpec(memory_space=pltpu.VMEM),) * 2,
        scratch_shapes=[pltpu.VMEM((n, n), jnp.float32)] * 2,
    )(gram, sketched, rotation)


def shards(sizes, snapshots, sketch, rotation):
    sketched = sketch_scatter(snapshots, sketch, sizes[3])
    gram = lax.dot_general(
        sketched,
        sketched,
        (((0,), (0,)), ((), ())),
        precision=lax.Precision.HIGHEST,
        preferred_element_type=jnp.float32,
    )
    gram = all_sum(gram, sizes)
    cell_count = sketched.shape[0] * sizes[0] * sizes[1] * sizes[2] * sizes[3]
    scale = float(np.sqrt(np.float32(cell_count)))
    basis, triangle = factor(gram, sketched, rotation, scale)
    return (basis, triangle)


def physical_mesh(mesh):
    space, tm = mesh.devices.shape
    nc = 2
    ny = 4 if space % 8 == 0 else 1
    nz = space // (ny * nc)
    devs = mesh.devices.reshape(nz, ny, nc, tm)
    return Mesh(devs, AXES), (nz, ny, nc, tm)


def solution(mesh):
    m4, sizes = physical_mesh(mesh)
    in_specs = (P(SPACE, "x"), P("x", None), P())
    out_specs = (P(AXES, None), P())
    return jax.shard_map(functools.partial(shards, sizes), mesh=m4, in_specs=in_specs,
                         out_specs=out_specs, check_vma=False)
```

```python
import functools

import jax
import numpy as np
import jax.numpy as jnp
from jax import lax
from jax.experimental import pallas as pl
from jax.experimental.pallas import tpu as pltpu
from jax.sharding import Mesh, PartitionSpec as P

MESH = pl.DeviceIdType.MESH
AXES = ("z", "y", "c", "x")
SPACE = ("z", "y", "c")


def sum_kernel(sizes, q_ref, o_ref, a_ref, qbuf, qsum, zbuf, full, qr, qs, zr, zs, qgr, qgs):
    nz, ny, nc, nx = sizes
    nq = nc * nx * ny
    zi, yi, ci, xi = (lax.axis_index(a) for a in AXES)
    qi = (ci * nx + xi) * ny + yi

    def peers(n, me):
        return [lax.rem(me + d, n) for d in range(1, n)]

    zdev = lambda j: (j, yi, ci, xi)
    qdev = lambda q: (zi, lax.rem(q, ny), q // (nx * ny), lax.rem(q // ny, nx))

    a_ref[...] = lax.dot_general(q_ref[...], q_ref[...], (((0,), (0,)), ((), ())),
                                 precision=lax.Precision.HIGHEST,
                                 preferred_element_type=jnp.float32)

    barrier = pltpu.get_barrier_semaphore()
    count = 0
    for n, me, make in ((nz, zi, zdev), (nq, qi, qdev)):
        for j in peers(n, me):
            pl.semaphore_signal(barrier, inc=1, device_id=make(j), device_id_type=MESH)
            count += 1
    pl.semaphore_wait(barrier, count)

    def exchange(n, me, make, src_of, dst_of, rsem, ssem):
        copies = []
        for j in peers(n, me):
            cp = pltpu.make_async_remote_copy(
                src_ref=src_of(j), dst_ref=dst_of(me), send_sem=ssem.at[j],
                recv_sem=rsem.at[me], device_id=make(j), device_id_type=MESH)
            cp.start()
            copies.append(cp)
        for j in peers(n, me):
            pltpu.make_async_remote_copy(
                src_ref=src_of(j), dst_ref=dst_of(j), send_sem=ssem.at[j],
                recv_sem=rsem.at[j], device_id=make(j), device_id_type=MESH).wait_recv()
        for cp in copies:
            cp.wait_send()

    def ordered_sum(buf, n):
        acc = buf[0]
        for j in range(1, n):
            acc = acc + buf[j]
        return acc

    c1 = a_ref.shape[0] // nq

    qbuf[qi] = a_ref[pl.ds(qi * c1, c1)]
    exchange(nq, qi, qdev, lambda j: a_ref.at[pl.ds(j * c1, c1)], lambda j: qbuf.at[j], qr, qs)
    qsum[...] = ordered_sum(qbuf, nq)

    zbuf[zi] = qsum[...]
    exchange(nz, zi, zdev, lambda j: qsum, lambda j: zbuf.at[j], zr, zs)
    own = qi * c1
    full[pl.ds(own, c1)] = ordered_sum(zbuf, nz)

    exchange(nq, qi, qdev, lambda j: full.at[pl.ds(own, c1)],
             lambda j: full.at[pl.ds(j * c1, c1)], qgr, qgs)
    o_ref[...] = full[...]


def all_sum(sketched, sizes):
    nz, ny, nc, nx = sizes
    nq = nc * nx * ny
    k = sketched.shape[1]
    gram = jax.ShapeDtypeStruct((k, k), jnp.float32)
    c1 = k // nq
    t = (k,)
    dma = pltpu.SemaphoreType.DMA
    return pl.pallas_call(
        functools.partial(sum_kernel, sizes),
        out_shape=jax.ShapeDtypeStruct(gram.shape, jnp.float32),
        in_specs=[pl.BlockSpec(memory_space=pltpu.VMEM)],
        out_specs=pl.BlockSpec(memory_space=pltpu.VMEM),
        scratch_shapes=[
            pltpu.VMEM(gram.shape, jnp.float32),
            pltpu.VMEM((nq, c1) + t, jnp.float32),
            pltpu.VMEM((c1,) + t, jnp.float32),
            pltpu.VMEM((nz, c1) + t, jnp.float32),
            pltpu.VMEM(gram.shape, jnp.float32),
            dma((nq,)), dma((nq,)), dma((nz,)), dma((nz,)), dma((nq,)), dma((nq,)),
        ],
        compiler_params=pltpu.CompilerParams(collective_id=0, has_side_effects=True),
    )(sketched)


def scatter_kernel(nx, s_hbm, k_hbm, o_ref, s_ref, k_ref, part, rbuf, rs, ss, ls):
    xi = lax.axis_index("x")
    rows = o_ref.shape[0]
    fetch = [pltpu.make_async_copy(k_hbm, k_ref, ls.at[nx])]
    for j in range(nx):
        fetch.append(pltpu.make_async_copy(s_hbm.at[pl.ds(j * rows, rows)],
                                           s_ref.at[pl.ds(j * rows, rows)], ls.at[j]))
    for cp in fetch:
        cp.start()
    fetch[0].wait()

    def fetched(j):
        pltpu.make_async_copy(s_hbm.at[pl.ds(j * rows, rows)],
                              s_ref.at[pl.ds(j * rows, rows)], ls.at[j]).wait()

    barrier = pltpu.get_barrier_semaphore()
    for d in range(1, nx):
        pl.semaphore_signal(barrier, inc=1, device_id={"x": lax.rem(xi + d, nx)},
                            device_id_type=MESH)
    pl.semaphore_wait(barrier, nx - 1)

    copies = []
    for d in range(1, nx):
        j = lax.rem(xi + d, nx)
        fetched(j)
        block = s_ref[pl.ds(pl.multiple_of(j * rows, rows), rows), :]
        part[j] = jnp.dot(block, k_ref[...], preferred_element_type=jnp.float32)
        cp = pltpu.make_async_remote_copy(
            src_ref=part.at[j], dst_ref=rbuf.at[xi], send_sem=ss.at[j],
            recv_sem=rs.at[xi], device_id={"x": j}, device_id_type=MESH)
        cp.start()
        copies.append(cp)
    fetched(xi)
    block = s_ref[pl.ds(pl.multiple_of(xi * rows, rows), rows), :]
    rbuf[xi] = jnp.dot(block, k_ref[...], preferred_element_type=jnp.float32)
    for d in range(1, nx):
        j = lax.rem(xi + d, nx)
        pltpu.make_async_remote_copy(
            src_ref=part.at[j], dst_ref=rbuf.at[j], send_sem=ss.at[j],
            recv_sem=rs.at[j], device_id={"x": j}, device_id_type=MESH).wait_recv()
    acc = rbuf[0]
    for j in range(1, nx):
        acc = acc + rbuf[j]
    o_ref[...] = acc
    for cp in copies:
        cp.wait_send()


def sketch_scatter(snapshots, sketch, nx):
    cells = snapshots.shape[0]
    rows = cells // nx
    cols = sketch.shape[1]
    dma = pltpu.SemaphoreType.DMA
    return pl.pallas_call(
        functools.partial(scatter_kernel, nx),
        out_shape=jax.ShapeDtypeStruct((rows, cols), jnp.float32),
        in_specs=[pl.BlockSpec(memory_space=pl.ANY)] * 2,
        out_specs=pl.BlockSpec(memory_space=pltpu.VMEM),
        scratch_shapes=[
            pltpu.VMEM(snapshots.shape, snapshots.dtype),
            pltpu.VMEM(sketch.shape, sketch.dtype),
            pltpu.VMEM((nx, rows, cols), jnp.float32),
            pltpu.VMEM((nx, rows, cols), jnp.float32),
            dma((nx,)), dma((nx,)), dma((nx + 1,)),
        ],
        compiler_params=pltpu.CompilerParams(collective_id=1, has_side_effects=True),
    )(snapshots, sketch)


def factor_kernel(b, scale, g_ref, q_ref, r_ref, basis_ref, tri_ref, l_ref, w_ref):
    n = g_ref.shape[0]
    hi = lax.Precision.HIGHEST
    l_ref[...] = jnp.zeros_like(l_ref)
    w_ref[...] = jnp.zeros_like(w_ref)
    nt = (((1,), (1,)), ((), ()))
    rows = lax.broadcasted_iota(jnp.int32, (b, b), 0)
    cols = lax.broadcasted_iota(jnp.int32, (b, b), 1)

    def panel(p, carry):
        r0 = pl.multiple_of(p * b, b)
        arow = g_ref[pl.ds(r0, b), :]
        w = w_ref[...]
        x = lax.dot_general(arow, w, nt, precision=hi, preferred_element_type=jnp.float32)
        pick = (lax.broadcasted_iota(jnp.int32, (n, b), 0)
                == r0 + lax.broadcasted_iota(jnp.int32, (n, b), 1)).astype(jnp.float32)
        place = (lax.broadcasted_iota(jnp.int32, (b, n), 1)
                 == r0 + lax.broadcasted_iota(jnp.int32, (b, n), 0)).astype(jnp.float32)
        s = jnp.dot(arow, pick, precision=hi, preferred_element_type=jnp.float32)
        s = s - lax.dot_general(x, x, nt, precision=hi, preferred_element_type=jnp.float32)
        low = jnp.zeros((b, b), jnp.float32)
        inv = jnp.zeros((b, b), jnp.float32)
        rest = (rows == cols).astype(jnp.float32)
        for i in range(b):
            pivot = s[i:i + 1, i:i + 1]
            left = s[:, i:i + 1]
            s = s - left * (s[i:i + 1, :] * (1.0 / pivot))
            col = jnp.where(rows[:, i:i + 1] >= i, left / jnp.sqrt(pivot), 0.0)
            low = jnp.where(cols == i, col, low)
            irow = rest[i:i + 1, :] / col[i:i + 1, :]
            inv = jnp.where(rows == i, irow, inv)
            rest = rest - col * irow
        l_ref[pl.ds(r0, b), :] = x + jnp.dot(low, place, precision=hi,
                                             preferred_element_type=jnp.float32)
        y = jnp.dot(x, w, precision=hi, preferred_element_type=jnp.float32)
        w_ref[pl.ds(r0, b), :] = jnp.dot(inv, place - y, precision=hi,
                                         preferred_element_type=jnp.float32)
        return carry

    lax.fori_loop(0, n // b, panel, 0)
    rotated = lax.dot_general(w_ref[...], r_ref[...], (((0,), (0,)), ((), ())), precision=hi,
                              preferred_element_type=jnp.float32)
    basis_ref[...] = scale * jnp.dot(q_ref[...], rotated, precision=hi,
                                     preferred_element_type=jnp.float32)
    tri_ref[...] = l_ref[...].T / scale


def factor(gram, sketched, rotation, scale, b=128):
    n = gram.shape[0]
    return pl.pallas_call(
        functools.partial(factor_kernel, b, scale),
        out_shape=(jax.ShapeDtypeStruct(sketched.shape, jnp.float32),
                   jax.ShapeDtypeStruct((n, n), jnp.float32)),
        in_specs=[pl.BlockSpec(memory_space=pltpu.VMEM)] * 3,
        out_specs=(pl.BlockSpec(memory_space=pltpu.VMEM),) * 2,
        scratch_shapes=[pltpu.VMEM((n, n), jnp.float32)] * 2,
    )(gram, sketched, rotation)


def shards(sizes, snapshots, sketch, rotation):
    sketched = sketch_scatter(snapshots, sketch, sizes[3])
    gram = all_sum(sketched, sizes)
    cell_count = sketched.shape[0] * sizes[0] * sizes[1] * sizes[2] * sizes[3]
    scale = float(np.sqrt(np.float32(cell_count)))
    basis, triangle = factor(gram, sketched, rotation, scale)
    return (basis, triangle)


def physical_mesh(mesh):
    space, tm = mesh.devices.shape
    nc = 2
    ny = 4 if space % 8 == 0 else 1
    nz = space // (ny * nc)
    devs = mesh.devices.reshape(nz, ny, nc, tm)
    return Mesh(devs, AXES), (nz, ny, nc, tm)


def solution(mesh):
    m4, sizes = physical_mesh(mesh)
    in_specs = (P(SPACE, "x"), P("x", None), P())
    out_specs = (P(AXES, None), P())
    return jax.shard_map(functools.partial(shards, sizes), mesh=m4, in_specs=in_specs,
                         out_specs=out_specs, check_vma=False)
```

```python
import functools

import jax
import numpy as np
import jax.numpy as jnp
from jax import lax
from jax.experimental import pallas as pl
from jax.experimental.pallas import tpu as pltpu
from jax.sharding import Mesh, PartitionSpec as P

MESH = pl.DeviceIdType.MESH
AXES = ("z", "y", "c", "x")
SPACE = ("z", "y", "c")


def sum_kernel(sizes, q_ref, o_ref, a_ref, qbuf, qsum, zbuf, full, qr, qs, zr, zs, qgr, qgs):
    nz, ny, nc, nx = sizes
    nq = nc * nx * ny
    zi, yi, ci, xi = (lax.axis_index(a) for a in AXES)
    qi = (ci * nx + xi) * ny + yi

    def peers(n, me):
        return [lax.rem(me + d, n) for d in range(1, n)]

    zdev = lambda j: (j, yi, ci, xi)
    qdev = lambda q: (zi, lax.rem(q, ny), q // (nx * ny), lax.rem(q // ny, nx))

    a_ref[...] = lax.dot_general(q_ref[...], q_ref[...], (((0,), (0,)), ((), ())),
                                 precision=lax.Precision.HIGHEST,
                                 preferred_element_type=jnp.float32)

    barrier = pltpu.get_barrier_semaphore()
    count = 0
    for n, me, make in ((nz, zi, zdev), (nq, qi, qdev)):
        for j in peers(n, me):
            pl.semaphore_signal(barrier, inc=1, device_id=make(j), device_id_type=MESH)
            count += 1
    pl.semaphore_wait(barrier, count)

    def exchange(n, me, make, src_of, dst_of, rsem, ssem):
        copies = []
        for j in peers(n, me):
            cp = pltpu.make_async_remote_copy(
                src_ref=src_of(j), dst_ref=dst_of(me), send_sem=ssem.at[j],
                recv_sem=rsem.at[me], device_id=make(j), device_id_type=MESH)
            cp.start()
            copies.append(cp)
        for j in peers(n, me):
            pltpu.make_async_remote_copy(
                src_ref=src_of(j), dst_ref=dst_of(j), send_sem=ssem.at[j],
                recv_sem=rsem.at[j], device_id=make(j), device_id_type=MESH).wait_recv()
        for cp in copies:
            cp.wait_send()

    def ordered_sum(buf, n):
        acc = buf[0]
        for j in range(1, n):
            acc = acc + buf[j]
        return acc

    c1 = a_ref.shape[0] // nq

    qbuf[qi] = a_ref[pl.ds(qi * c1, c1)]
    exchange(nq, qi, qdev, lambda j: a_ref.at[pl.ds(j * c1, c1)], lambda j: qbuf.at[j], qr, qs)
    qsum[...] = ordered_sum(qbuf, nq)

    zbuf[zi] = qsum[...]
    exchange(nz, zi, zdev, lambda j: qsum, lambda j: zbuf.at[j], zr, zs)
    own = qi * c1
    full[pl.ds(own, c1)] = ordered_sum(zbuf, nz)

    exchange(nq, qi, qdev, lambda j: full.at[pl.ds(own, c1)],
             lambda j: full.at[pl.ds(j * c1, c1)], qgr, qgs)
    o_ref[...] = full[...]


def all_sum(sketched, sizes):
    nz, ny, nc, nx = sizes
    nq = nc * nx * ny
    k = sketched.shape[1]
    gram = jax.ShapeDtypeStruct((k, k), jnp.float32)
    c1 = k // nq
    t = (k,)
    dma = pltpu.SemaphoreType.DMA
    return pl.pallas_call(
        functools.partial(sum_kernel, sizes),
        out_shape=jax.ShapeDtypeStruct(gram.shape, jnp.float32),
        in_specs=[pl.BlockSpec(memory_space=pltpu.VMEM)],
        out_specs=pl.BlockSpec(memory_space=pltpu.VMEM),
        scratch_shapes=[
            pltpu.VMEM(gram.shape, jnp.float32),
            pltpu.VMEM((nq, c1) + t, jnp.float32),
            pltpu.VMEM((c1,) + t, jnp.float32),
            pltpu.VMEM((nz, c1) + t, jnp.float32),
            pltpu.VMEM(gram.shape, jnp.float32),
            dma((nq,)), dma((nq,)), dma((nz,)), dma((nz,)), dma((nq,)), dma((nq,)),
        ],
        compiler_params=pltpu.CompilerParams(collective_id=0, has_side_effects=True),
    )(sketched)


def scatter_kernel(nx, s_hbm, k_hbm, o_ref, s_ref, k_ref, part, rbuf, relay, rs, rh, rl, ss, ls):
    xi = lax.axis_index("x")
    rows = o_ref.shape[0]
    half = rows // 2
    right, left, opp = lax.rem(xi + 1, nx), lax.rem(xi + nx - 1, nx), lax.rem(xi + 2, nx)
    fetch = [pltpu.make_async_copy(k_hbm, k_ref, ls.at[nx])]
    for j in range(nx):
        fetch.append(pltpu.make_async_copy(s_hbm.at[pl.ds(j * rows, rows)],
                                           s_ref.at[pl.ds(j * rows, rows)], ls.at[j]))
    for cp in fetch:
        cp.start()
    fetch[0].wait()

    def compute(j):
        pltpu.make_async_copy(s_hbm.at[pl.ds(j * rows, rows)],
                              s_ref.at[pl.ds(j * rows, rows)], ls.at[j]).wait()
        block = s_ref[pl.ds(pl.multiple_of(j * rows, rows), rows), :]
        return jnp.dot(block, k_ref[...], preferred_element_type=jnp.float32)

    def send(src, dst, sem_send, sem_recv, dev):
        return pltpu.make_async_remote_copy(
            src_ref=src, dst_ref=dst, send_sem=sem_send, recv_sem=sem_recv,
            device_id={"x": dev}, device_id_type=MESH)

    barrier = pltpu.get_barrier_semaphore()
    for dev in (left, right):
        pl.semaphore_signal(barrier, inc=1, device_id={"x": dev}, device_id_type=MESH)
    pl.semaphore_wait(barrier, 2)

    part[0] = compute(opp)
    lo, hi = pl.ds(0, half), pl.ds(half, half)
    out = [send(part.at[0, lo], relay.at[0], ss.at[0], rl.at[0], right),
           send(part.at[0, hi], relay.at[1], ss.at[1], rl.at[1], left)]
    part[1] = compute(right)
    out.append(send(part.at[1], rbuf.at[xi], ss.at[2], rs.at[0], right))
    part[2] = compute(left)
    out.append(send(part.at[2], rbuf.at[xi], ss.at[3], rs.at[1], left))
    for cp in out[:2]:
        cp.start()
    for cp in out[2:]:
        cp.start()
    send(part.at[0, lo], relay.at[0], ss.at[0], rl.at[0], left).wait_recv()
    fwd = [send(relay.at[0], rbuf.at[left, lo], ss.at[4], rh.at[0], right)]
    fwd[0].start()
    send(part.at[0, hi], relay.at[1], ss.at[1], rl.at[1], right).wait_recv()
    fwd.append(send(relay.at[1], rbuf.at[right, hi], ss.at[5], rh.at[1], left))
    fwd[1].start()
    rbuf[xi] = compute(xi)
    send(part.at[1], rbuf.at[left], ss.at[2], rs.at[0], left).wait_recv()
    send(part.at[2], rbuf.at[right], ss.at[3], rs.at[1], right).wait_recv()
    send(relay.at[0], rbuf.at[opp, lo], ss.at[4], rh.at[0], left).wait_recv()
    send(relay.at[1], rbuf.at[opp, hi], ss.at[5], rh.at[1], right).wait_recv()
    acc = rbuf[0]
    for j in range(1, nx):
        acc = acc + rbuf[j]
    o_ref[...] = acc
    for cp in out + fwd:
        cp.wait_send()


def sketch_scatter(snapshots, sketch, nx):
    cells = snapshots.shape[0]
    rows = cells // nx
    cols = sketch.shape[1]
    dma = pltpu.SemaphoreType.DMA
    return pl.pallas_call(
        functools.partial(scatter_kernel, nx),
        out_shape=jax.ShapeDtypeStruct((rows, cols), jnp.float32),
        in_specs=[pl.BlockSpec(memory_space=pl.ANY)] * 2,
        out_specs=pl.BlockSpec(memory_space=pltpu.VMEM),
        scratch_shapes=[
            pltpu.VMEM(snapshots.shape, snapshots.dtype),
            pltpu.VMEM(sketch.shape, sketch.dtype),
            pltpu.VMEM((3, rows, cols), jnp.float32),
            pltpu.VMEM((nx, rows, cols), jnp.float32),
            pltpu.VMEM((2, rows // 2, cols), jnp.float32),
            dma((2,)), dma((2,)), dma((2,)), dma((6,)), dma((nx + 1,)),
        ],
        compiler_params=pltpu.CompilerParams(collective_id=1, has_side_effects=True),
    )(snapshots, sketch)


def factor_kernel(b, scale, g_ref, q_ref, r_ref, basis_ref, tri_ref, l_ref, w_ref):
    n = g_ref.shape[0]
    hi = lax.Precision.HIGHEST
    l_ref[...] = jnp.zeros_like(l_ref)
    w_ref[...] = jnp.zeros_like(w_ref)
    nt = (((1,), (1,)), ((), ()))
    rows = lax.broadcasted_iota(jnp.int32, (b, b), 0)
    cols = lax.broadcasted_iota(jnp.int32, (b, b), 1)

    def panel(p, carry):
        r0 = pl.multiple_of(p * b, b)
        arow = g_ref[pl.ds(r0, b), :]
        w = w_ref[...]
        x = lax.dot_general(arow, w, nt, precision=hi, preferred_element_type=jnp.float32)
        pick = (lax.broadcasted_iota(jnp.int32, (n, b), 0)
                == r0 + lax.broadcasted_iota(jnp.int32, (n, b), 1)).astype(jnp.float32)
        place = (lax.broadcasted_iota(jnp.int32, (b, n), 1)
                 == r0 + lax.broadcasted_iota(jnp.int32, (b, n), 0)).astype(jnp.float32)
        s = jnp.dot(arow, pick, precision=hi, preferred_element_type=jnp.float32)
        s = s - lax.dot_general(x, x, nt, precision=hi, preferred_element_type=jnp.float32)
        low = jnp.zeros((b, b), jnp.float32)
        inv = jnp.zeros((b, b), jnp.float32)
        rest = (rows == cols).astype(jnp.float32)
        for i in range(b):
            pivot = s[i:i + 1, i:i + 1]
            left = s[:, i:i + 1]
            s = s - left * (s[i:i + 1, :] * (1.0 / pivot))
            col = jnp.where(rows[:, i:i + 1] >= i, left / jnp.sqrt(pivot), 0.0)
            low = jnp.where(cols == i, col, low)
            irow = rest[i:i + 1, :] / col[i:i + 1, :]
            inv = jnp.where(rows == i, irow, inv)
            rest = rest - col * irow
        l_ref[pl.ds(r0, b), :] = x + jnp.dot(low, place, precision=hi,
                                             preferred_element_type=jnp.float32)
        y = jnp.dot(x, w, precision=hi, preferred_element_type=jnp.float32)
        w_ref[pl.ds(r0, b), :] = jnp.dot(inv, place - y, precision=hi,
                                         preferred_element_type=jnp.float32)
        return carry

    lax.fori_loop(0, n // b, panel, 0)
    rotated = lax.dot_general(w_ref[...], r_ref[...], (((0,), (0,)), ((), ())), precision=hi,
                              preferred_element_type=jnp.float32)
    basis_ref[...] = scale * jnp.dot(q_ref[...], rotated, precision=hi,
                                     preferred_element_type=jnp.float32)
    tri_ref[...] = l_ref[...].T / scale


def factor(gram, sketched, rotation, scale, b=128):
    n = gram.shape[0]
    return pl.pallas_call(
        functools.partial(factor_kernel, b, scale),
        out_shape=(jax.ShapeDtypeStruct(sketched.shape, jnp.float32),
                   jax.ShapeDtypeStruct((n, n), jnp.float32)),
        in_specs=[pl.BlockSpec(memory_space=pltpu.VMEM)] * 3,
        out_specs=(pl.BlockSpec(memory_space=pltpu.VMEM),) * 2,
        scratch_shapes=[pltpu.VMEM((n, n), jnp.float32)] * 2,
    )(gram, sketched, rotation)


def shards(sizes, snapshots, sketch, rotation):
    sketched = sketch_scatter(snapshots, sketch, sizes[3])
    gram = all_sum(sketched, sizes)
    cell_count = sketched.shape[0] * sizes[0] * sizes[1] * sizes[2] * sizes[3]
    scale = float(np.sqrt(np.float32(cell_count)))
    basis, triangle = factor(gram, sketched, rotation, scale)
    return (basis, triangle)


def physical_mesh(mesh):
    space, tm = mesh.devices.shape
    nc = 2
    ny = 4 if space % 8 == 0 else 1
    nz = space // (ny * nc)
    devs = mesh.devices.reshape(nz, ny, nc, tm)
    return Mesh(devs, AXES), (nz, ny, nc, tm)


def solution(mesh):
    m4, sizes = physical_mesh(mesh)
    in_specs = (P(SPACE, "x"), P("x", None), P())
    out_specs = (P(AXES, None), P())
    return jax.shard_map(functools.partial(shards, sizes), mesh=m4, in_specs=in_specs,
                         out_specs=out_specs, check_vma=False)
```

```python
import functools

import jax
import numpy as np
import jax.numpy as jnp
from jax import lax
from jax.experimental import pallas as pl
from jax.experimental.pallas import tpu as pltpu
from jax.sharding import Mesh, PartitionSpec as P

MESH = pl.DeviceIdType.MESH
AXES = ("z", "y", "c", "x")
SPACE = ("z", "y", "c")


def fused_kernel(sizes, s_hbm, k_hbm, q_out, g_out, s_ref, k_ref, part, rbuf, a_ref, qbuf,
                 qsum, zbuf, full, rs, ss, ls, qr, qs, zr, zs, qgr, qgs):
    nz, ny, nc, nx = sizes
    nq = nc * nx * ny
    zi, yi, ci, xi = (lax.axis_index(a) for a in AXES)
    qi = (ci * nx + xi) * ny + yi
    rows = q_out.shape[0]

    def peers(n, me):
        return [lax.rem(me + d, n) for d in range(1, n)]

    zdev = lambda j: (j, yi, ci, xi)
    xdev = lambda j: (zi, yi, ci, j)
    qdev = lambda q: (zi, lax.rem(q, ny), q // (nx * ny), lax.rem(q // ny, nx))

    fetch = [pltpu.make_async_copy(k_hbm, k_ref, ls.at[nx])]
    for j in range(nx):
        fetch.append(pltpu.make_async_copy(s_hbm.at[pl.ds(j * rows, rows)],
                                           s_ref.at[pl.ds(j * rows, rows)], ls.at[j]))
    for cp in fetch:
        cp.start()

    barrier = pltpu.get_barrier_semaphore()
    count = 0
    for n, me, make in ((nz, zi, zdev), (nq, qi, qdev)):
        for j in peers(n, me):
            pl.semaphore_signal(barrier, inc=1, device_id=make(j), device_id_type=MESH)
            count += 1
    fetch[0].wait()

    def fetched(j):
        pltpu.make_async_copy(s_hbm.at[pl.ds(j * rows, rows)],
                              s_ref.at[pl.ds(j * rows, rows)], ls.at[j]).wait()

    pl.semaphore_wait(barrier, count)

    copies = []
    for d in range(1, nx):
        j = lax.rem(xi + d, nx)
        fetched(j)
        block = s_ref[pl.ds(pl.multiple_of(j * rows, rows), rows), :]
        part[j] = jnp.dot(block, k_ref[...], preferred_element_type=jnp.float32)
        cp = pltpu.make_async_remote_copy(
            src_ref=part.at[j], dst_ref=rbuf.at[xi], send_sem=ss.at[j],
            recv_sem=rs.at[xi], device_id=xdev(j), device_id_type=MESH)
        cp.start()
        copies.append(cp)
    fetched(xi)
    block = s_ref[pl.ds(pl.multiple_of(xi * rows, rows), rows), :]
    rbuf[xi] = jnp.dot(block, k_ref[...], preferred_element_type=jnp.float32)
    for d in range(1, nx):
        j = lax.rem(xi + d, nx)
        pltpu.make_async_remote_copy(
            src_ref=part.at[j], dst_ref=rbuf.at[j], send_sem=ss.at[j],
            recv_sem=rs.at[j], device_id=xdev(j), device_id_type=MESH).wait_recv()
    acc = rbuf[0]
    for j in range(1, nx):
        acc = acc + rbuf[j]
    q_out[...] = acc
    for cp in copies:
        cp.wait_send()

    a_ref[...] = lax.dot_general(acc, acc, (((0,), (0,)), ((), ())),
                                 precision=lax.Precision.HIGHEST,
                                 preferred_element_type=jnp.float32)

    def exchange(n, me, make, src_of, dst_of, rsem, ssem):
        sent = []
        for j in peers(n, me):
            cp = pltpu.make_async_remote_copy(
                src_ref=src_of(j), dst_ref=dst_of(me), send_sem=ssem.at[j],
                recv_sem=rsem.at[me], device_id=make(j), device_id_type=MESH)
            cp.start()
            sent.append(cp)
        for j in peers(n, me):
            pltpu.make_async_remote_copy(
                src_ref=src_of(j), dst_ref=dst_of(j), send_sem=ssem.at[j],
                recv_sem=rsem.at[j], device_id=make(j), device_id_type=MESH).wait_recv()
        for cp in sent:
            cp.wait_send()

    def ordered_sum(buf, n):
        total = buf[0]
        for j in range(1, n):
            total = total + buf[j]
        return total

    c1 = a_ref.shape[0] // nq

    qbuf[qi] = a_ref[pl.ds(qi * c1, c1)]
    exchange(nq, qi, qdev, lambda j: a_ref.at[pl.ds(j * c1, c1)], lambda j: qbuf.at[j], qr, qs)
    qsum[...] = ordered_sum(qbuf, nq)

    zbuf[zi] = qsum[...]
    exchange(nz, zi, zdev, lambda j: qsum, lambda j: zbuf.at[j], zr, zs)
    own = qi * c1
    full[pl.ds(own, c1)] = ordered_sum(zbuf, nz)

    exchange(nq, qi, qdev, lambda j: full.at[pl.ds(own, c1)],
             lambda j: full.at[pl.ds(j * c1, c1)], qgr, qgs)
    g_out[...] = full[...]


def sketch_and_gram(snapshots, sketch, sizes):
    nz, ny, nc, nx = sizes
    nq = nc * nx * ny
    rows = snapshots.shape[0] // nx
    k = sketch.shape[1]
    c1 = k // nq
    dma = pltpu.SemaphoreType.DMA
    return pl.pallas_call(
        functools.partial(fused_kernel, sizes),
        out_shape=(jax.ShapeDtypeStruct((rows, k), jnp.float32),
                   jax.ShapeDtypeStruct((k, k), jnp.float32)),
        in_specs=[pl.BlockSpec(memory_space=pl.ANY)] * 2,
        out_specs=(pl.BlockSpec(memory_space=pltpu.VMEM),) * 2,
        scratch_shapes=[
            pltpu.VMEM(snapshots.shape, snapshots.dtype),
            pltpu.VMEM(sketch.shape, sketch.dtype),
            pltpu.VMEM((nx, rows, k), jnp.float32),
            pltpu.VMEM((nx, rows, k), jnp.float32),
            pltpu.VMEM((k, k), jnp.float32),
            pltpu.VMEM((nq, c1, k), jnp.float32),
            pltpu.VMEM((c1, k), jnp.float32),
            pltpu.VMEM((nz, c1, k), jnp.float32),
            pltpu.VMEM((k, k), jnp.float32),
            dma((nx,)), dma((nx,)), dma((nx + 1,)),
            dma((nq,)), dma((nq,)), dma((nz,)), dma((nz,)), dma((nq,)), dma((nq,)),
        ],
        compiler_params=pltpu.CompilerParams(collective_id=0, has_side_effects=True),
    )(snapshots, sketch)


def factor_kernel(b, scale, g_ref, q_ref, r_ref, basis_ref, tri_ref, l_ref, w_ref):
    n = g_ref.shape[0]
    hi = lax.Precision.HIGHEST
    l_ref[...] = jnp.zeros_like(l_ref)
    w_ref[...] = jnp.zeros_like(w_ref)
    nt = (((1,), (1,)), ((), ()))
    rows = lax.broadcasted_iota(jnp.int32, (b, b), 0)
    cols = lax.broadcasted_iota(jnp.int32, (b, b), 1)

    def panel(p, carry):
        r0 = pl.multiple_of(p * b, b)
        arow = g_ref[pl.ds(r0, b), :]
        w = w_ref[...]
        x = lax.dot_general(arow, w, nt, precision=hi, preferred_element_type=jnp.float32)
        pick = (lax.broadcasted_iota(jnp.int32, (n, b), 0)
                == r0 + lax.broadcasted_iota(jnp.int32, (n, b), 1)).astype(jnp.float32)
        place = (lax.broadcasted_iota(jnp.int32, (b, n), 1)
                 == r0 + lax.broadcasted_iota(jnp.int32, (b, n), 0)).astype(jnp.float32)
        s = jnp.dot(arow, pick, precision=hi, preferred_element_type=jnp.float32)
        s = s - lax.dot_general(x, x, nt, precision=hi, preferred_element_type=jnp.float32)
        low = jnp.zeros((b, b), jnp.float32)
        inv = jnp.zeros((b, b), jnp.float32)
        rest = (rows == cols).astype(jnp.float32)
        for i in range(b):
            pivot = s[i:i + 1, i:i + 1]
            left = s[:, i:i + 1]
            s = s - left * (s[i:i + 1, :] * (1.0 / pivot))
            col = jnp.where(rows[:, i:i + 1] >= i, left / jnp.sqrt(pivot), 0.0)
            low = jnp.where(cols == i, col, low)
            irow = rest[i:i + 1, :] / col[i:i + 1, :]
            inv = jnp.where(rows == i, irow, inv)
            rest = rest - col * irow
        l_ref[pl.ds(r0, b), :] = x + jnp.dot(low, place, precision=hi,
                                             preferred_element_type=jnp.float32)
        y = jnp.dot(x, w, precision=hi, preferred_element_type=jnp.float32)
        w_ref[pl.ds(r0, b), :] = jnp.dot(inv, place - y, precision=hi,
                                         preferred_element_type=jnp.float32)
        return carry

    lax.fori_loop(0, n // b, panel, 0)
    rotated = lax.dot_general(w_ref[...], r_ref[...], (((0,), (0,)), ((), ())), precision=hi,
                              preferred_element_type=jnp.float32)
    basis_ref[...] = scale * jnp.dot(q_ref[...], rotated, precision=hi,
                                     preferred_element_type=jnp.float32)
    tri_ref[...] = l_ref[...].T / scale


def factor(gram, sketched, rotation, scale, b=128):
    n = gram.shape[0]
    return pl.pallas_call(
        functools.partial(factor_kernel, b, scale),
        out_shape=(jax.ShapeDtypeStruct(sketched.shape, jnp.float32),
                   jax.ShapeDtypeStruct((n, n), jnp.float32)),
        in_specs=[pl.BlockSpec(memory_space=pltpu.VMEM)] * 3,
        out_specs=(pl.BlockSpec(memory_space=pltpu.VMEM),) * 2,
        scratch_shapes=[pltpu.VMEM((n, n), jnp.float32)] * 2,
    )(gram, sketched, rotation)


def shards(sizes, snapshots, sketch, rotation):
    sketched, gram = sketch_and_gram(snapshots, sketch, sizes)
    cell_count = sketched.shape[0] * sizes[0] * sizes[1] * sizes[2] * sizes[3]
    scale = float(np.sqrt(np.float32(cell_count)))
    basis, triangle = factor(gram, sketched, rotation, scale)
    return (basis, triangle)


def physical_mesh(mesh):
    space, tm = mesh.devices.shape
    nc = 2
    ny = 4 if space % 8 == 0 else 1
    nz = space // (ny * nc)
    devs = mesh.devices.reshape(nz, ny, nc, tm)
    return Mesh(devs, AXES), (nz, ny, nc, tm)


def solution(mesh):
    m4, sizes = physical_mesh(mesh)
    in_specs = (P(SPACE, "x"), P("x", None), P())
    out_specs = (P(AXES, None), P())
    return jax.shard_map(functools.partial(shards, sizes), mesh=m4, in_specs=in_specs,
                         out_specs=out_specs, check_vma=False)
```

```python
import functools

import jax
import numpy as np
import jax.numpy as jnp
from jax import lax
from jax.experimental import pallas as pl
from jax.experimental.pallas import tpu as pltpu
from jax.sharding import Mesh, PartitionSpec as P

MESH = pl.DeviceIdType.MESH
AXES = ("z", "y", "c", "x")
SPACE = ("z", "y", "c")


def fused_kernel(sizes, s_hbm, k_hbm, q_out, g_out, s_ref, k_ref, part, rbuf, a_ref, qbuf,
                 qsum, zbuf, full, rs, ss, ls, qr, qs, zr, zs, qgr, qgs):
    nz, ny, nc, nx = sizes
    nq = nc * nx * ny
    zi, yi, ci, xi = (lax.axis_index(a) for a in AXES)
    qi = (ci * nx + xi) * ny + yi
    rows = q_out.shape[0]

    def peers(n, me):
        return [lax.rem(me + d, n) for d in range(1, n)]

    zdev = lambda j: (j, yi, ci, xi)
    xdev = lambda j: (zi, yi, ci, j)
    qdev = lambda q: (zi, lax.rem(q, ny), q // (nx * ny), lax.rem(q // ny, nx))

    fetch = [pltpu.make_async_copy(k_hbm, k_ref, ls.at[nx])]
    for j in range(nx):
        fetch.append(pltpu.make_async_copy(s_hbm.at[pl.ds(j * rows, rows)],
                                           s_ref.at[pl.ds(j * rows, rows)], ls.at[j]))
    for cp in fetch:
        cp.start()

    barrier = pltpu.get_barrier_semaphore()
    count = 0
    for n, me, make in ((nz, zi, zdev), (nq, qi, qdev)):
        for j in peers(n, me):
            pl.semaphore_signal(barrier, inc=1, device_id=make(j), device_id_type=MESH)
            count += 1
    fetch[0].wait()

    def fetched(j):
        pltpu.make_async_copy(s_hbm.at[pl.ds(j * rows, rows)],
                              s_ref.at[pl.ds(j * rows, rows)], ls.at[j]).wait()

    pl.semaphore_wait(barrier, count)

    copies = []
    for d in range(1, nx):
        j = lax.rem(xi + d, nx)
        fetched(j)
        block = s_ref[pl.ds(pl.multiple_of(j * rows, rows), rows), :]
        part[j] = jnp.dot(block, k_ref[...], preferred_element_type=jnp.float32)
        cp = pltpu.make_async_remote_copy(
            src_ref=part.at[j], dst_ref=rbuf.at[xi], send_sem=ss.at[j],
            recv_sem=rs.at[xi], device_id=xdev(j), device_id_type=MESH)
        cp.start()
        copies.append(cp)
    fetched(xi)
    block = s_ref[pl.ds(pl.multiple_of(xi * rows, rows), rows), :]
    rbuf[xi] = jnp.dot(block, k_ref[...], preferred_element_type=jnp.float32)
    for d in range(1, nx):
        j = lax.rem(xi + d, nx)
        pltpu.make_async_remote_copy(
            src_ref=part.at[j], dst_ref=rbuf.at[j], send_sem=ss.at[j],
            recv_sem=rs.at[j], device_id=xdev(j), device_id_type=MESH).wait_recv()
    acc = rbuf[0]
    for j in range(1, nx):
        acc = acc + rbuf[j]
    q_out[...] = acc
    for cp in copies:
        cp.wait_send()

    a_ref[...] = lax.dot_general(acc, acc, (((0,), (0,)), ((), ())),
                                 precision=lax.Precision.HIGHEST,
                                 preferred_element_type=jnp.float32)

    def exchange(n, me, make, src_of, dst_of, rsem, ssem):
        sent = []
        for j in peers(n, me):
            cp = pltpu.make_async_remote_copy(
                src_ref=src_of(j), dst_ref=dst_of(me), send_sem=ssem.at[j],
                recv_sem=rsem.at[me], device_id=make(j), device_id_type=MESH)
            cp.start()
            sent.append(cp)
        for j in peers(n, me):
            pltpu.make_async_remote_copy(
                src_ref=src_of(j), dst_ref=dst_of(j), send_sem=ssem.at[j],
                recv_sem=rsem.at[j], device_id=make(j), device_id_type=MESH).wait_recv()
        for cp in sent:
            cp.wait_send()

    def ordered_sum(buf, n):
        total = buf[0]
        for j in range(1, n):
            total = total + buf[j]
        return total

    c1 = a_ref.shape[0] // nq

    qbuf[qi] = a_ref[pl.ds(qi * c1, c1)]
    exchange(nq, qi, qdev, lambda j: a_ref.at[pl.ds(j * c1, c1)], lambda j: qbuf.at[j], qr, qs)
    qsum[...] = ordered_sum(qbuf, nq)

    h = a_ref.shape[1] // 2
    width = ((0, 2 * h), (h, h))
    zbuf[zi] = qsum[...]
    for c, (lo, n) in enumerate(width):
        pl.when(ci == c)(lambda lo=lo, n=n: exchange(
            nz, zi, zdev, lambda j: qsum.at[:, pl.ds(lo, n)],
            lambda j: zbuf.at[j, :, pl.ds(lo, n)], zr, zs))
    own = qi * c1
    full[pl.ds(own, c1)] = ordered_sum(zbuf, nz)

    per = nq // nc

    def gather_copy(j, lo, n):
        return pltpu.make_async_remote_copy(
            src_ref=full.at[pl.ds(own, c1), pl.ds(lo, n)],
            dst_ref=full.at[pl.ds(own, c1), pl.ds(lo, n)], send_sem=qgs.at[j],
            recv_sem=qgr.at[qi], device_id=qdev(j), device_id_type=MESH)

    for c, (lo, n) in enumerate(width):
        def start(lo=lo, n=n):
            for j in peers(nq, qi):
                gather_copy(j, lo, n).start()
        pl.when(ci == c)(start)
    for c, (lo, n) in enumerate(width):
        for r in range(per):
            j = c * per + r
            def arrived(j=j, lo=lo, n=n):
                pltpu.make_async_remote_copy(
                    src_ref=full.at[pl.ds(j * c1, c1), pl.ds(lo, n)],
                    dst_ref=full.at[pl.ds(j * c1, c1), pl.ds(lo, n)], send_sem=qgs.at[j],
                    recv_sem=qgr.at[j], device_id=qdev(j), device_id_type=MESH).wait_recv()
            pl.when(qi != j)(arrived)
    for c, (lo, n) in enumerate(width):
        def sent(lo=lo, n=n):
            for j in peers(nq, qi):
                gather_copy(j, lo, n).wait_send()
        pl.when(ci == c)(sent)
    g_out[...] = full[...]
    g_out[h:, 0:h] = full[0:h, h:].T


def sketch_and_gram(snapshots, sketch, sizes):
    nz, ny, nc, nx = sizes
    nq = nc * nx * ny
    rows = snapshots.shape[0] // nx
    k = sketch.shape[1]
    c1 = k // nq
    dma = pltpu.SemaphoreType.DMA
    return pl.pallas_call(
        functools.partial(fused_kernel, sizes),
        out_shape=(jax.ShapeDtypeStruct((rows, k), jnp.float32),
                   jax.ShapeDtypeStruct((k, k), jnp.float32)),
        in_specs=[pl.BlockSpec(memory_space=pl.ANY)] * 2,
        out_specs=(pl.BlockSpec(memory_space=pltpu.VMEM),) * 2,
        scratch_shapes=[
            pltpu.VMEM(snapshots.shape, snapshots.dtype),
            pltpu.VMEM(sketch.shape, sketch.dtype),
            pltpu.VMEM((nx, rows, k), jnp.float32),
            pltpu.VMEM((nx, rows, k), jnp.float32),
            pltpu.VMEM((k, k), jnp.float32),
            pltpu.VMEM((nq, c1, k), jnp.float32),
            pltpu.VMEM((c1, k), jnp.float32),
            pltpu.VMEM((nz, c1, k), jnp.float32),
            pltpu.VMEM((k, k), jnp.float32),
            dma((nx,)), dma((nx,)), dma((nx + 1,)),
            dma((nq,)), dma((nq,)), dma((nz,)), dma((nz,)), dma((nq,)), dma((nq,)),
        ],
        compiler_params=pltpu.CompilerParams(collective_id=0, has_side_effects=True),
    )(snapshots, sketch)


def factor_kernel(b, scale, g_ref, q_ref, r_ref, basis_ref, tri_ref, l_ref, w_ref):
    n = g_ref.shape[0]
    hi = lax.Precision.HIGHEST
    l_ref[...] = jnp.zeros_like(l_ref)
    w_ref[...] = jnp.zeros_like(w_ref)
    nt = (((1,), (1,)), ((), ()))
    rows = lax.broadcasted_iota(jnp.int32, (b, b), 0)
    cols = lax.broadcasted_iota(jnp.int32, (b, b), 1)

    def panel(p, carry):
        r0 = pl.multiple_of(p * b, b)
        arow = g_ref[pl.ds(r0, b), :]
        w = w_ref[...]
        x = lax.dot_general(arow, w, nt, precision=hi, preferred_element_type=jnp.float32)
        pick = (lax.broadcasted_iota(jnp.int32, (n, b), 0)
                == r0 + lax.broadcasted_iota(jnp.int32, (n, b), 1)).astype(jnp.float32)
        place = (lax.broadcasted_iota(jnp.int32, (b, n), 1)
                 == r0 + lax.broadcasted_iota(jnp.int32, (b, n), 0)).astype(jnp.float32)
        s = jnp.dot(arow, pick, precision=hi, preferred_element_type=jnp.float32)
        s = s - lax.dot_general(x, x, nt, precision=hi, preferred_element_type=jnp.float32)
        low = jnp.zeros((b, b), jnp.float32)
        inv = jnp.zeros((b, b), jnp.float32)
        rest = (rows == cols).astype(jnp.float32)
        for i in range(b):
            pivot = s[i:i + 1, i:i + 1]
            left = s[:, i:i + 1]
            s = s - left * (s[i:i + 1, :] * (1.0 / pivot))
            col = jnp.where(rows[:, i:i + 1] >= i, left / jnp.sqrt(pivot), 0.0)
            low = jnp.where(cols == i, col, low)
            irow = rest[i:i + 1, :] / col[i:i + 1, :]
            inv = jnp.where(rows == i, irow, inv)
            rest = rest - col * irow
        l_ref[pl.ds(r0, b), :] = x + jnp.dot(low, place, precision=hi,
                                             preferred_element_type=jnp.float32)
        y = jnp.dot(x, w, precision=hi, preferred_element_type=jnp.float32)
        w_ref[pl.ds(r0, b), :] = jnp.dot(inv, place - y, precision=hi,
                                         preferred_element_type=jnp.float32)
        return carry

    lax.fori_loop(0, n // b, panel, 0)
    rotated = lax.dot_general(w_ref[...], r_ref[...], (((0,), (0,)), ((), ())), precision=hi,
                              preferred_element_type=jnp.float32)
    basis_ref[...] = scale * jnp.dot(q_ref[...], rotated, precision=hi,
                                     preferred_element_type=jnp.float32)
    tri_ref[...] = l_ref[...].T / scale


def factor(gram, sketched, rotation, scale, b=128):
    n = gram.shape[0]
    return pl.pallas_call(
        functools.partial(factor_kernel, b, scale),
        out_shape=(jax.ShapeDtypeStruct(sketched.shape, jnp.float32),
                   jax.ShapeDtypeStruct((n, n), jnp.float32)),
        in_specs=[pl.BlockSpec(memory_space=pltpu.VMEM)] * 3,
        out_specs=(pl.BlockSpec(memory_space=pltpu.VMEM),) * 2,
        scratch_shapes=[pltpu.VMEM((n, n), jnp.float32)] * 2,
    )(gram, sketched, rotation)


def shards(sizes, snapshots, sketch, rotation):
    sketched, gram = sketch_and_gram(snapshots, sketch, sizes)
    cell_count = sketched.shape[0] * sizes[0] * sizes[1] * sizes[2] * sizes[3]
    scale = float(np.sqrt(np.float32(cell_count)))
    basis, triangle = factor(gram, sketched, rotation, scale)
    return (basis, triangle)


def physical_mesh(mesh):
    space, tm = mesh.devices.shape
    nc = 2
    ny = 4 if space % 8 == 0 else 1
    nz = space // (ny * nc)
    devs = mesh.devices.reshape(nz, ny, nc, tm)
    return Mesh(devs, AXES), (nz, ny, nc, tm)


def solution(mesh):
    m4, sizes = physical_mesh(mesh)
    in_specs = (P(SPACE, "x"), P("x", None), P())
    out_specs = (P(AXES, None), P())
    return jax.shard_map(functools.partial(shards, sizes), mesh=m4, in_specs=in_specs,
                         out_specs=out_specs, check_vma=False)
```

```python
import functools

import jax
import numpy as np
import jax.numpy as jnp
from jax import lax
from jax.experimental import pallas as pl
from jax.experimental.pallas import tpu as pltpu
from jax.sharding import Mesh, PartitionSpec as P

MESH = pl.DeviceIdType.MESH
AXES = ("z", "y", "c", "x")
SPACE = ("z", "y", "c")


def fused_kernel(sizes, s_hbm, k_hbm, q_out, g_out, s_ref, k_ref, part, rbuf, a_ref, qbuf,
                 qsum, zbuf, full, rs, ss, ls, qr, qs, zr, zs, qgr, qgs):
    nz, ny, nc, nx = sizes
    nq = nc * nx * ny
    zi, yi, ci, xi = (lax.axis_index(a) for a in AXES)
    qi = (ci * nx + xi) * ny + yi
    rows = q_out.shape[0]

    def peers(n, me):
        return [lax.rem(me + d, n) for d in range(1, n)]

    zdev = lambda j: (j, yi, ci, xi)
    xdev = lambda j: (zi, yi, ci, j)
    qdev = lambda q: (zi, lax.rem(q, ny), q // (nx * ny), lax.rem(q // ny, nx))

    fetch = [pltpu.make_async_copy(k_hbm, k_ref, ls.at[nx])]
    for j in range(nx):
        fetch.append(pltpu.make_async_copy(s_hbm.at[pl.ds(j * rows, rows)],
                                           s_ref.at[pl.ds(j * rows, rows)], ls.at[j]))
    for cp in fetch:
        cp.start()

    barrier = pltpu.get_barrier_semaphore()
    count = 0
    for n, me, make in ((nz, zi, zdev), (nq, qi, qdev)):
        for j in peers(n, me):
            pl.semaphore_signal(barrier, inc=1, device_id=make(j), device_id_type=MESH)
            count += 1
    fetch[0].wait()

    def fetched(j):
        pltpu.make_async_copy(s_hbm.at[pl.ds(j * rows, rows)],
                              s_ref.at[pl.ds(j * rows, rows)], ls.at[j]).wait()

    for d in range(1, nx):
        j = lax.rem(xi + d, nx)
        fetched(j)
        block = s_ref[pl.ds(pl.multiple_of(j * rows, rows), rows), :]
        part[j] = jnp.dot(block, k_ref[...], preferred_element_type=jnp.float32)
    fetched(xi)
    block = s_ref[pl.ds(pl.multiple_of(xi * rows, rows), rows), :]
    rbuf[xi] = jnp.dot(block, k_ref[...], preferred_element_type=jnp.float32)

    pl.semaphore_wait(barrier, count)

    copies = []
    for d in range(1, nx):
        j = lax.rem(xi + d, nx)
        cp = pltpu.make_async_remote_copy(
            src_ref=part.at[j], dst_ref=rbuf.at[xi], send_sem=ss.at[j],
            recv_sem=rs.at[xi], device_id=xdev(j), device_id_type=MESH)
        cp.start()
        copies.append(cp)
    for d in range(1, nx):
        j = lax.rem(xi + d, nx)
        pltpu.make_async_remote_copy(
            src_ref=part.at[j], dst_ref=rbuf.at[j], send_sem=ss.at[j],
            recv_sem=rs.at[j], device_id=xdev(j), device_id_type=MESH).wait_recv()
    acc = rbuf[0]
    for j in range(1, nx):
        acc = acc + rbuf[j]
    q_out[...] = acc
    for cp in copies:
        cp.wait_send()

    a_ref[...] = lax.dot_general(acc, acc, (((0,), (0,)), ((), ())),
                                 precision=lax.Precision.HIGHEST,
                                 preferred_element_type=jnp.float32)

    def exchange(n, me, make, src_of, dst_of, rsem, ssem):
        sent = []
        for j in peers(n, me):
            cp = pltpu.make_async_remote_copy(
                src_ref=src_of(j), dst_ref=dst_of(me), send_sem=ssem.at[j],
                recv_sem=rsem.at[me], device_id=make(j), device_id_type=MESH)
            cp.start()
            sent.append(cp)
        for j in peers(n, me):
            pltpu.make_async_remote_copy(
                src_ref=src_of(j), dst_ref=dst_of(j), send_sem=ssem.at[j],
                recv_sem=rsem.at[j], device_id=make(j), device_id_type=MESH).wait_recv()
        for cp in sent:
            cp.wait_send()

    def ordered_sum(buf, n):
        total = buf[0]
        for j in range(1, n):
            total = total + buf[j]
        return total

    c1 = a_ref.shape[0] // nq

    qbuf[qi] = a_ref[pl.ds(qi * c1, c1)]
    exchange(nq, qi, qdev, lambda j: a_ref.at[pl.ds(j * c1, c1)], lambda j: qbuf.at[j], qr, qs)
    qsum[...] = ordered_sum(qbuf, nq)

    zbuf[zi] = qsum[...]
    exchange(nz, zi, zdev, lambda j: qsum, lambda j: zbuf.at[j], zr, zs)
    own = qi * c1
    full[pl.ds(own, c1)] = ordered_sum(zbuf, nz)

    exchange(nq, qi, qdev, lambda j: full.at[pl.ds(own, c1)],
             lambda j: full.at[pl.ds(j * c1, c1)], qgr, qgs)
    g_out[...] = full[...]


def sketch_and_gram(snapshots, sketch, sizes):
    nz, ny, nc, nx = sizes
    nq = nc * nx * ny
    rows = snapshots.shape[0] // nx
    k = sketch.shape[1]
    c1 = k // nq
    dma = pltpu.SemaphoreType.DMA
    return pl.pallas_call(
        functools.partial(fused_kernel, sizes),
        out_shape=(jax.ShapeDtypeStruct((rows, k), jnp.float32),
                   jax.ShapeDtypeStruct((k, k), jnp.float32)),
        in_specs=[pl.BlockSpec(memory_space=pl.ANY)] * 2,
        out_specs=(pl.BlockSpec(memory_space=pltpu.VMEM),) * 2,
        scratch_shapes=[
            pltpu.VMEM(snapshots.shape, snapshots.dtype),
            pltpu.VMEM(sketch.shape, sketch.dtype),
            pltpu.VMEM((nx, rows, k), jnp.float32),
            pltpu.VMEM((nx, rows, k), jnp.float32),
            pltpu.VMEM((k, k), jnp.float32),
            pltpu.VMEM((nq, c1, k), jnp.float32),
            pltpu.VMEM((c1, k), jnp.float32),
            pltpu.VMEM((nz, c1, k), jnp.float32),
            pltpu.VMEM((k, k), jnp.float32),
            dma((nx,)), dma((nx,)), dma((nx + 1,)),
            dma((nq,)), dma((nq,)), dma((nz,)), dma((nz,)), dma((nq,)), dma((nq,)),
        ],
        compiler_params=pltpu.CompilerParams(collective_id=0, has_side_effects=True),
    )(snapshots, sketch)


def factor_kernel(b, scale, g_ref, q_ref, r_ref, basis_ref, tri_ref, l_ref, w_ref):
    n = g_ref.shape[0]
    hi = lax.Precision.HIGHEST
    l_ref[...] = jnp.zeros_like(l_ref)
    w_ref[...] = jnp.zeros_like(w_ref)
    nt = (((1,), (1,)), ((), ()))
    rows = lax.broadcasted_iota(jnp.int32, (b, b), 0)
    cols = lax.broadcasted_iota(jnp.int32, (b, b), 1)

    def panel(p, carry):
        r0 = pl.multiple_of(p * b, b)
        arow = g_ref[pl.ds(r0, b), :]
        w = w_ref[...]
        x = lax.dot_general(arow, w, nt, precision=hi, preferred_element_type=jnp.float32)
        pick = (lax.broadcasted_iota(jnp.int32, (n, b), 0)
                == r0 + lax.broadcasted_iota(jnp.int32, (n, b), 1)).astype(jnp.float32)
        place = (lax.broadcasted_iota(jnp.int32, (b, n), 1)
                 == r0 + lax.broadcasted_iota(jnp.int32, (b, n), 0)).astype(jnp.float32)
        s = jnp.dot(arow, pick, precision=hi, preferred_element_type=jnp.float32)
        s = s - lax.dot_general(x, x, nt, precision=hi, preferred_element_type=jnp.float32)
        low = jnp.zeros((b, b), jnp.float32)
        inv = jnp.zeros((b, b), jnp.float32)
        rest = (rows == cols).astype(jnp.float32)
        for i in range(b):
            pivot = s[i:i + 1, i:i + 1]
            left = s[:, i:i + 1]
            s = s - left * (s[i:i + 1, :] * (1.0 / pivot))
            col = jnp.where(rows[:, i:i + 1] >= i, left / jnp.sqrt(pivot), 0.0)
            low = jnp.where(cols == i, col, low)
            irow = rest[i:i + 1, :] / col[i:i + 1, :]
            inv = jnp.where(rows == i, irow, inv)
            rest = rest - col * irow
        l_ref[pl.ds(r0, b), :] = x + jnp.dot(low, place, precision=hi,
                                             preferred_element_type=jnp.float32)
        y = jnp.dot(x, w, precision=hi, preferred_element_type=jnp.float32)
        w_ref[pl.ds(r0, b), :] = jnp.dot(inv, place - y, precision=hi,
                                         preferred_element_type=jnp.float32)
        return carry

    lax.fori_loop(0, n // b, panel, 0)
    rotated = lax.dot_general(w_ref[...], r_ref[...], (((0,), (0,)), ((), ())), precision=hi,
                              preferred_element_type=jnp.float32)
    basis_ref[...] = scale * jnp.dot(q_ref[...], rotated, precision=hi,
                                     preferred_element_type=jnp.float32)
    tri_ref[...] = l_ref[...].T / scale


def factor(gram, sketched, rotation, scale, b=128):
    n = gram.shape[0]
    return pl.pallas_call(
        functools.partial(factor_kernel, b, scale),
        out_shape=(jax.ShapeDtypeStruct(sketched.shape, jnp.float32),
                   jax.ShapeDtypeStruct((n, n), jnp.float32)),
        in_specs=[pl.BlockSpec(memory_space=pltpu.VMEM)] * 3,
        out_specs=(pl.BlockSpec(memory_space=pltpu.VMEM),) * 2,
        scratch_shapes=[pltpu.VMEM((n, n), jnp.float32)] * 2,
    )(gram, sketched, rotation)


def shards(sizes, snapshots, sketch, rotation):
    sketched, gram = sketch_and_gram(snapshots, sketch, sizes)
    cell_count = sketched.shape[0] * sizes[0] * sizes[1] * sizes[2] * sizes[3]
    scale = float(np.sqrt(np.float32(cell_count)))
    basis, triangle = factor(gram, sketched, rotation, scale)
    return (basis, triangle)


def physical_mesh(mesh):
    space, tm = mesh.devices.shape
    nc = 2
    ny = 4 if space % 8 == 0 else 1
    nz = space // (ny * nc)
    devs = mesh.devices.reshape(nz, ny, nc, tm)
    return Mesh(devs, AXES), (nz, ny, nc, tm)


def solution(mesh):
    m4, sizes = physical_mesh(mesh)
    in_specs = (P(SPACE, "x"), P("x", None), P())
    out_specs = (P(AXES, None), P())
    return jax.shard_map(functools.partial(shards, sizes), mesh=m4, in_specs=in_specs,
                         out_specs=out_specs, check_vma=False)
```

```python
import functools

import jax
import numpy as np
import jax.numpy as jnp
from jax import lax
from jax.experimental import pallas as pl
from jax.experimental.pallas import tpu as pltpu
from jax.sharding import Mesh, PartitionSpec as P

MESH = pl.DeviceIdType.MESH
AXES = ("z", "y", "c", "x")
SPACE = ("z", "y", "c")


def fused_kernel(sizes, s_hbm, k_hbm, q_out, g_out, s_ref, k_ref, part, rbuf, a_ref, qbuf,
                 qsum, zbuf, full, rs, ss, ls, qr, qs, zr, zs, qgr, qgs):
    nz, ny, nc, nx = sizes
    nq = nc * nx * ny
    zi, yi, ci, xi = (lax.axis_index(a) for a in AXES)
    qi = (ci * nx + xi) * ny + yi
    rows = q_out.shape[0]

    def peers(n, me):
        return [lax.rem(me + d, n) for d in range(1, n)]

    zdev = lambda j: (j, yi, ci, xi)
    xdev = lambda j: (zi, yi, ci, j)
    qdev = lambda q: (zi, lax.rem(q, ny), q // (nx * ny), lax.rem(q // ny, nx))

    fetch = [pltpu.make_async_copy(k_hbm, k_ref, ls.at[nx])]
    for j in range(nx):
        fetch.append(pltpu.make_async_copy(s_hbm.at[pl.ds(j * rows, rows)],
                                           s_ref.at[pl.ds(j * rows, rows)], ls.at[j]))
    for cp in fetch:
        cp.start()

    barrier = pltpu.get_barrier_semaphore()
    count = 0
    for n, me, make in ((nz, zi, zdev), (nq, qi, qdev)):
        for j in peers(n, me):
            pl.semaphore_signal(barrier, inc=1, device_id=make(j), device_id_type=MESH)
            count += 1
    fetch[0].wait()

    def fetched(j):
        pltpu.make_async_copy(s_hbm.at[pl.ds(j * rows, rows)],
                              s_ref.at[pl.ds(j * rows, rows)], ls.at[j]).wait()

    pl.semaphore_wait(barrier, count)

    copies = []
    for d in range(1, nx):
        j = lax.rem(xi + d, nx)
        fetched(j)
        block = s_ref[pl.ds(pl.multiple_of(j * rows, rows), rows), :]
        part[j] = jnp.dot(block, k_ref[...], preferred_element_type=jnp.float32)
        cp = pltpu.make_async_remote_copy(
            src_ref=part.at[j], dst_ref=rbuf.at[xi], send_sem=ss.at[j],
            recv_sem=rs.at[xi], device_id=xdev(j), device_id_type=MESH)
        cp.start()
        copies.append(cp)
    fetched(xi)
    block = s_ref[pl.ds(pl.multiple_of(xi * rows, rows), rows), :]
    rbuf[xi] = jnp.dot(block, k_ref[...], preferred_element_type=jnp.float32)
    for d in range(1, nx):
        j = lax.rem(xi + d, nx)
        pltpu.make_async_remote_copy(
            src_ref=part.at[j], dst_ref=rbuf.at[j], send_sem=ss.at[j],
            recv_sem=rs.at[j], device_id=xdev(j), device_id_type=MESH).wait_recv()
    acc = rbuf[0]
    for j in range(1, nx):
        acc = acc + rbuf[j]
    q_out[...] = acc
    for cp in copies:
        cp.wait_send()

    a_ref[...] = lax.dot_general(acc, acc, (((0,), (0,)), ((), ())),
                                 precision=lax.Precision.HIGHEST,
                                 preferred_element_type=jnp.float32)

    def exchange(n, me, make, src_of, dst_of, rsem, ssem):
        sent = []
        for j in peers(n, me):
            cp = pltpu.make_async_remote_copy(
                src_ref=src_of(j), dst_ref=dst_of(me), send_sem=ssem.at[j],
                recv_sem=rsem.at[me], device_id=make(j), device_id_type=MESH)
            cp.start()
            sent.append(cp)
        for j in peers(n, me):
            pltpu.make_async_remote_copy(
                src_ref=src_of(j), dst_ref=dst_of(j), send_sem=ssem.at[j],
                recv_sem=rsem.at[j], device_id=make(j), device_id_type=MESH).wait_recv()
        for cp in sent:
            cp.wait_send()

    def ordered_sum(buf, n):
        total = buf[0]
        for j in range(1, n):
            total = total + buf[j]
        return total

    c1 = a_ref.shape[0] // nq

    qbuf[qi] = a_ref[pl.ds(qi * c1, c1)]
    exchange(nq, qi, qdev, lambda j: a_ref.at[pl.ds(j * c1, c1)], lambda j: qbuf.at[j], qr, qs)
    qsum[...] = ordered_sum(qbuf, nq)

    zbuf[zi] = qsum[...]
    exchange(nz, zi, zdev, lambda j: qsum, lambda j: zbuf.at[j], zr, zs)
    own = qi * c1
    full[pl.ds(own, c1)] = ordered_sum(zbuf, nz)

    exchange(nq, qi, qdev, lambda j: full.at[pl.ds(own, c1)],
             lambda j: full.at[pl.ds(j * c1, c1)], qgr, qgs)
    g_out[...] = full[...]


def sketch_and_gram(snapshots, sketch, sizes):
    nz, ny, nc, nx = sizes
    nq = nc * nx * ny
    rows = snapshots.shape[0] // nx
    k = sketch.shape[1]
    c1 = k // nq
    dma = pltpu.SemaphoreType.DMA
    return pl.pallas_call(
        functools.partial(fused_kernel, sizes),
        out_shape=(jax.ShapeDtypeStruct((rows, k), jnp.float32),
                   jax.ShapeDtypeStruct((k, k), jnp.float32)),
        in_specs=[pl.BlockSpec(memory_space=pl.ANY)] * 2,
        out_specs=(pl.BlockSpec(memory_space=pltpu.VMEM),) * 2,
        scratch_shapes=[
            pltpu.VMEM(snapshots.shape, snapshots.dtype),
            pltpu.VMEM(sketch.shape, sketch.dtype),
            pltpu.VMEM((nx, rows, k), jnp.float32),
            pltpu.VMEM((nx, rows, k), jnp.float32),
            pltpu.VMEM((k, k), jnp.float32),
            pltpu.VMEM((nq, c1, k), jnp.float32),
            pltpu.VMEM((c1, k), jnp.float32),
            pltpu.VMEM((nz, c1, k), jnp.float32),
            pltpu.VMEM((k, k), jnp.float32),
            dma((nx,)), dma((nx,)), dma((nx + 1,)),
            dma((nq,)), dma((nq,)), dma((nz,)), dma((nz,)), dma((nq,)), dma((nq,)),
        ],
        compiler_params=pltpu.CompilerParams(collective_id=0, has_side_effects=True),
    )(snapshots, sketch)


def factor_kernel(b, scale, g_ref, q_ref, r_ref, basis_ref, tri_ref, l_ref, w_ref):
    n = g_ref.shape[0]
    hi = lax.Precision.HIGHEST
    l_ref[...] = jnp.zeros_like(l_ref)
    w_ref[...] = jnp.zeros_like(w_ref)
    nt = (((1,), (1,)), ((), ()))
    rows = lax.broadcasted_iota(jnp.int32, (b, b), 0)
    cols = lax.broadcasted_iota(jnp.int32, (b, b), 1)

    def panel(p, carry):
        r0 = pl.multiple_of(p * b, b)
        arow = g_ref[pl.ds(r0, b), :]
        w = w_ref[...]
        x = lax.dot_general(arow, w, nt, precision=hi, preferred_element_type=jnp.float32)
        s = g_ref[pl.ds(r0, b), pl.ds(r0, b)]
        s = s - lax.dot_general(x, x, nt, precision=hi, preferred_element_type=jnp.float32)
        low = jnp.zeros((b, b), jnp.float32)
        inv = jnp.zeros((b, b), jnp.float32)
        rest = (rows == cols).astype(jnp.float32)
        for i in range(b):
            pivot = s[i:i + 1, i:i + 1]
            left = s[:, i:i + 1]
            s = s - left * (s[i:i + 1, :] * (1.0 / pivot))
            col = jnp.where(rows[:, i:i + 1] >= i, left / jnp.sqrt(pivot), 0.0)
            low = jnp.where(cols == i, col, low)
            irow = rest[i:i + 1, :] / col[i:i + 1, :]
            inv = jnp.where(rows == i, irow, inv)
            rest = rest - col * irow
        l_ref[pl.ds(r0, b), :] = x
        l_ref[pl.ds(r0, b), pl.ds(r0, b)] = low
        y = jnp.dot(x, w, precision=hi, preferred_element_type=jnp.float32)
        w_ref[pl.ds(r0, b), :] = -jnp.dot(inv, y, precision=hi, preferred_element_type=jnp.float32)
        w_ref[pl.ds(r0, b), pl.ds(r0, b)] = inv
        return carry

    lax.fori_loop(0, n // b, panel, 0)
    rotated = lax.dot_general(w_ref[...], r_ref[...], (((0,), (0,)), ((), ())), precision=hi,
                              preferred_element_type=jnp.float32)
    basis_ref[...] = scale * jnp.dot(q_ref[...], rotated, precision=hi,
                                     preferred_element_type=jnp.float32)
    tri_ref[...] = l_ref[...].T / scale


def factor(gram, sketched, rotation, scale, b=128):
    n = gram.shape[0]
    return pl.pallas_call(
        functools.partial(factor_kernel, b, scale),
        out_shape=(jax.ShapeDtypeStruct(sketched.shape, jnp.float32),
                   jax.ShapeDtypeStruct((n, n), jnp.float32)),
        in_specs=[pl.BlockSpec(memory_space=pltpu.VMEM)] * 3,
        out_specs=(pl.BlockSpec(memory_space=pltpu.VMEM),) * 2,
        scratch_shapes=[pltpu.VMEM((n, n), jnp.float32)] * 2,
    )(gram, sketched, rotation)


def shards(sizes, snapshots, sketch, rotation):
    sketched, gram = sketch_and_gram(snapshots, sketch, sizes)
    cell_count = sketched.shape[0] * sizes[0] * sizes[1] * sizes[2] * sizes[3]
    scale = float(np.sqrt(np.float32(cell_count)))
    basis, triangle = factor(gram, sketched, rotation, scale)
    return (basis, triangle)


def physical_mesh(mesh):
    space, tm = mesh.devices.shape
    nc = 2
    ny = 4 if space % 8 == 0 else 1
    nz = space // (ny * nc)
    devs = mesh.devices.reshape(nz, ny, nc, tm)
    return Mesh(devs, AXES), (nz, ny, nc, tm)


def solution(mesh):
    m4, sizes = physical_mesh(mesh)
    in_specs = (P(SPACE, "x"), P("x", None), P())
    out_specs = (P(AXES, None), P())
    return jax.shard_map(functools.partial(shards, sizes), mesh=m4, in_specs=in_specs,
                         out_specs=out_specs, check_vma=False)
```

```python
import functools

import jax
import numpy as np
import jax.numpy as jnp
from jax import lax
from jax.experimental import pallas as pl
from jax.experimental.pallas import tpu as pltpu
from jax.sharding import Mesh, PartitionSpec as P

MESH = pl.DeviceIdType.MESH
AXES = ("z", "y", "c", "x")
SPACE = ("z", "y", "c")


def fused_kernel(sizes, s_hbm, k_hbm, q_out, g_out, s_ref, k_ref, part, rbuf, a_ref, qbuf,
                 qsum, zbuf, full, rs, ss, ls, qr, qs, zr, zs, qgr, qgs):
    nz, ny, nc, nx = sizes
    nq = nc * nx * ny
    zi, yi, ci, xi = (lax.axis_index(a) for a in AXES)
    qi = (ci * nx + xi) * ny + yi
    rows = q_out.shape[0]

    def peers(n, me):
        return [lax.rem(me + d, n) for d in range(1, n)]

    zdev = lambda j: (j, yi, ci, xi)
    xdev = lambda j: (zi, yi, ci, j)
    qdev = lambda q: (zi, lax.rem(q, ny), q // (nx * ny), lax.rem(q // ny, nx))

    fetch = [pltpu.make_async_copy(k_hbm, k_ref, ls.at[nx])]
    for j in range(nx):
        fetch.append(pltpu.make_async_copy(s_hbm.at[pl.ds(j * rows, rows)],
                                           s_ref.at[pl.ds(j * rows, rows)], ls.at[j]))
    for cp in fetch:
        cp.start()

    barrier = pltpu.get_barrier_semaphore()
    count = 0
    for n, me, make in ((nz, zi, zdev), (nq, qi, qdev)):
        for j in peers(n, me):
            pl.semaphore_signal(barrier, inc=1, device_id=make(j), device_id_type=MESH)
            count += 1
    fetch[0].wait()

    def fetched(j):
        pltpu.make_async_copy(s_hbm.at[pl.ds(j * rows, rows)],
                              s_ref.at[pl.ds(j * rows, rows)], ls.at[j]).wait()

    pl.semaphore_wait(barrier, count)

    copies = []
    for d in range(1, nx):
        j = lax.rem(xi + d, nx)
        fetched(j)
        block = s_ref[pl.ds(pl.multiple_of(j * rows, rows), rows), :]
        part[j] = jnp.dot(block, k_ref[...], preferred_element_type=jnp.float32)
        cp = pltpu.make_async_remote_copy(
            src_ref=part.at[j], dst_ref=rbuf.at[xi], send_sem=ss.at[j],
            recv_sem=rs.at[xi], device_id=xdev(j), device_id_type=MESH)
        cp.start()
        copies.append(cp)
    fetched(xi)
    block = s_ref[pl.ds(pl.multiple_of(xi * rows, rows), rows), :]
    rbuf[xi] = jnp.dot(block, k_ref[...], preferred_element_type=jnp.float32)
    for d in range(1, nx):
        j = lax.rem(xi + d, nx)
        pltpu.make_async_remote_copy(
            src_ref=part.at[j], dst_ref=rbuf.at[j], send_sem=ss.at[j],
            recv_sem=rs.at[j], device_id=xdev(j), device_id_type=MESH).wait_recv()
    acc = rbuf[0]
    for j in range(1, nx):
        acc = acc + rbuf[j]
    q_out[...] = acc
    for cp in copies:
        cp.wait_send()

    a_ref[...] = lax.dot_general(acc, acc, (((0,), (0,)), ((), ())),
                                 precision=lax.Precision.HIGHEST,
                                 preferred_element_type=jnp.float32)

    def exchange(n, me, make, src_of, dst_of, rsem, ssem):
        sent = []
        for j in peers(n, me):
            cp = pltpu.make_async_remote_copy(
                src_ref=src_of(j), dst_ref=dst_of(me), send_sem=ssem.at[j],
                recv_sem=rsem.at[me], device_id=make(j), device_id_type=MESH)
            cp.start()
            sent.append(cp)
        for j in peers(n, me):
            pltpu.make_async_remote_copy(
                src_ref=src_of(j), dst_ref=dst_of(j), send_sem=ssem.at[j],
                recv_sem=rsem.at[j], device_id=make(j), device_id_type=MESH).wait_recv()
        for cp in sent:
            cp.wait_send()

    def ordered_sum(buf, n):
        total = buf[0]
        for j in range(1, n):
            total = total + buf[j]
        return total

    c1 = a_ref.shape[0] // nq

    qbuf[qi] = a_ref[pl.ds(qi * c1, c1)]
    exchange(nq, qi, qdev, lambda j: a_ref.at[pl.ds(j * c1, c1)], lambda j: qbuf.at[j], qr, qs)
    qsum[...] = ordered_sum(qbuf, nq)

    zbuf[zi] = qsum[...]
    exchange(nz, zi, zdev, lambda j: qsum, lambda j: zbuf.at[j], zr, zs)
    own = qi * c1
    full[pl.ds(own, c1)] = ordered_sum(zbuf, nz)

    exchange(nq, qi, qdev, lambda j: full.at[pl.ds(own, c1)],
             lambda j: full.at[pl.ds(j * c1, c1)], qgr, qgs)
    g_out[...] = full[...]


def sketch_and_gram(snapshots, sketch, sizes):
    nz, ny, nc, nx = sizes
    nq = nc * nx * ny
    rows = snapshots.shape[0] // nx
    k = sketch.shape[1]
    c1 = k // nq
    dma = pltpu.SemaphoreType.DMA
    return pl.pallas_call(
        functools.partial(fused_kernel, sizes),
        out_shape=(jax.ShapeDtypeStruct((rows, k), jnp.float32),
                   jax.ShapeDtypeStruct((k, k), jnp.float32)),
        in_specs=[pl.BlockSpec(memory_space=pl.ANY)] * 2,
        out_specs=(pl.BlockSpec(memory_space=pltpu.VMEM),) * 2,
        scratch_shapes=[
            pltpu.VMEM(snapshots.shape, snapshots.dtype),
            pltpu.VMEM(sketch.shape, sketch.dtype),
            pltpu.VMEM((nx, rows, k), jnp.float32),
            pltpu.VMEM((nx, rows, k), jnp.float32),
            pltpu.VMEM((k, k), jnp.float32),
            pltpu.VMEM((nq, c1, k), jnp.float32),
            pltpu.VMEM((c1, k), jnp.float32),
            pltpu.VMEM((nz, c1, k), jnp.float32),
            pltpu.VMEM((k, k), jnp.float32),
            dma((nx,)), dma((nx,)), dma((nx + 1,)),
            dma((nq,)), dma((nq,)), dma((nz,)), dma((nz,)), dma((nq,)), dma((nq,)),
        ],
        compiler_params=pltpu.CompilerParams(collective_id=0, has_side_effects=True),
    )(snapshots, sketch)


def factor_kernel(b, scale, g_ref, q_ref, r_ref, basis_ref, tri_ref, l_ref, w_ref, s_ref):
    n = g_ref.shape[0]
    hi = lax.Precision.HIGHEST
    l_ref[...] = jnp.zeros_like(l_ref)
    w_ref[...] = jnp.zeros_like(w_ref)
    nt = (((1,), (1,)), ((), ()))
    rows = lax.broadcasted_iota(jnp.int32, (b, b), 0)
    cols = lax.broadcasted_iota(jnp.int32, (b, b), 1)

    def panel(p, carry):
        r0 = pl.multiple_of(p * b, b)
        s_ref[...] = g_ref[pl.ds(r0, b), pl.ds(r0, b)]

        @pl.when(p > 0)
        def _():
            x = lax.dot_general(g_ref[pl.ds(r0, b), :], w_ref[...], nt, precision=hi,
                                preferred_element_type=jnp.float32)
            l_ref[pl.ds(r0, b), :] = x
            s_ref[...] -= lax.dot_general(x, x, nt, precision=hi,
                                          preferred_element_type=jnp.float32)

        s = s_ref[...]
        low = jnp.zeros((b, b), jnp.float32)
        inv = jnp.zeros((b, b), jnp.float32)
        rest = (rows == cols).astype(jnp.float32)
        for i in range(b):
            pivot = s[i:i + 1, i:i + 1]
            left = s[:, i:i + 1]
            s = s - left * (s[i:i + 1, :] * (1.0 / pivot))
            col = jnp.where(rows[:, i:i + 1] >= i, left / jnp.sqrt(pivot), 0.0)
            low = jnp.where(cols == i, col, low)
            irow = rest[i:i + 1, :] / col[i:i + 1, :]
            inv = jnp.where(rows == i, irow, inv)
            rest = rest - col * irow

        @pl.when(p > 0)
        def _():
            y = jnp.dot(l_ref[pl.ds(r0, b), :], w_ref[...], precision=hi,
                        preferred_element_type=jnp.float32)
            w_ref[pl.ds(r0, b), :] = -jnp.dot(inv, y, precision=hi,
                                              preferred_element_type=jnp.float32)

        l_ref[pl.ds(r0, b), pl.ds(r0, b)] = low
        w_ref[pl.ds(r0, b), pl.ds(r0, b)] = inv
        return carry

    lax.fori_loop(0, n // b, panel, 0)
    rotated = lax.dot_general(w_ref[...], r_ref[...], (((0,), (0,)), ((), ())), precision=hi,
                              preferred_element_type=jnp.float32)
    basis_ref[...] = scale * jnp.dot(q_ref[...], rotated, precision=hi,
                                     preferred_element_type=jnp.float32)
    tri_ref[...] = l_ref[...].T / scale


def factor(gram, sketched, rotation, scale, b=128):
    n = gram.shape[0]
    return pl.pallas_call(
        functools.partial(factor_kernel, b, scale),
        out_shape=(jax.ShapeDtypeStruct(sketched.shape, jnp.float32),
                   jax.ShapeDtypeStruct((n, n), jnp.float32)),
        in_specs=[pl.BlockSpec(memory_space=pltpu.VMEM)] * 3,
        out_specs=(pl.BlockSpec(memory_space=pltpu.VMEM),) * 2,
        scratch_shapes=[pltpu.VMEM((n, n), jnp.float32)] * 2 + [pltpu.VMEM((b, b), jnp.float32)],
    )(gram, sketched, rotation)


def shards(sizes, snapshots, sketch, rotation):
    sketched, gram = sketch_and_gram(snapshots, sketch, sizes)
    cell_count = sketched.shape[0] * sizes[0] * sizes[1] * sizes[2] * sizes[3]
    scale = float(np.sqrt(np.float32(cell_count)))
    basis, triangle = factor(gram, sketched, rotation, scale)
    return (basis, triangle)


def physical_mesh(mesh):
    space, tm = mesh.devices.shape
    nc = 2
    ny = 4 if space % 8 == 0 else 1
    nz = space // (ny * nc)
    devs = mesh.devices.reshape(nz, ny, nc, tm)
    return Mesh(devs, AXES), (nz, ny, nc, tm)


def solution(mesh):
    m4, sizes = physical_mesh(mesh)
    in_specs = (P(SPACE, "x"), P("x", None), P())
    out_specs = (P(AXES, None), P())
    return jax.shard_map(functools.partial(shards, sizes), mesh=m4, in_specs=in_specs,
                         out_specs=out_specs, check_vma=False)
```

```python
import functools

import jax
import numpy as np
import jax.numpy as jnp
from jax import lax
from jax.experimental import pallas as pl
from jax.experimental.pallas import tpu as pltpu
from jax.sharding import Mesh, PartitionSpec as P

MESH = pl.DeviceIdType.MESH
AXES = ("z", "y", "c", "x")
SPACE = ("z", "y", "c")


def fused_kernel(sizes, s_hbm, k_hbm, q_out, g_out, s_ref, k_ref, part, rbuf, a_ref, qbuf,
                 qsum, zbuf, full, rs, ss, ls, qr, qs, zr, zs, qgr, qgs):
    nz, ny, nc, nx = sizes
    nq = nc * nx * ny
    zi, yi, ci, xi = (lax.axis_index(a) for a in AXES)
    qi = (ci * nx + xi) * ny + yi
    rows = q_out.shape[0]

    def peers(n, me):
        return [lax.rem(me + d, n) for d in range(1, n)]

    zdev = lambda j: (j, yi, ci, xi)
    xdev = lambda j: (zi, yi, ci, j)
    qdev = lambda q: (zi, lax.rem(q, ny), q // (nx * ny), lax.rem(q // ny, nx))

    fetch = [pltpu.make_async_copy(k_hbm, k_ref, ls.at[nx])]
    for j in range(nx):
        fetch.append(pltpu.make_async_copy(s_hbm.at[pl.ds(j * rows, rows)],
                                           s_ref.at[pl.ds(j * rows, rows)], ls.at[j]))
    for cp in fetch:
        cp.start()

    barrier = pltpu.get_barrier_semaphore()
    count = 0
    for n, me, make in ((nz, zi, zdev), (nq, qi, qdev)):
        for j in peers(n, me):
            pl.semaphore_signal(barrier, inc=1, device_id=make(j), device_id_type=MESH)
            count += 1
    fetch[0].wait()

    def fetched(j):
        pltpu.make_async_copy(s_hbm.at[pl.ds(j * rows, rows)],
                              s_ref.at[pl.ds(j * rows, rows)], ls.at[j]).wait()

    pl.semaphore_wait(barrier, count)

    copies = []
    for d in range(1, nx):
        j = lax.rem(xi + d, nx)
        fetched(j)
        block = s_ref[pl.ds(pl.multiple_of(j * rows, rows), rows), :]
        part[j] = jnp.dot(block, k_ref[...], preferred_element_type=jnp.float32)
        cp = pltpu.make_async_remote_copy(
            src_ref=part.at[j], dst_ref=rbuf.at[xi], send_sem=ss.at[j],
            recv_sem=rs.at[xi], device_id=xdev(j), device_id_type=MESH)
        cp.start()
        copies.append(cp)
    fetched(xi)
    block = s_ref[pl.ds(pl.multiple_of(xi * rows, rows), rows), :]
    rbuf[xi] = jnp.dot(block, k_ref[...], preferred_element_type=jnp.float32)
    for d in range(1, nx):
        j = lax.rem(xi + d, nx)
        pltpu.make_async_remote_copy(
            src_ref=part.at[j], dst_ref=rbuf.at[j], send_sem=ss.at[j],
            recv_sem=rs.at[j], device_id=xdev(j), device_id_type=MESH).wait_recv()
    acc = rbuf[0]
    for j in range(1, nx):
        acc = acc + rbuf[j]
    q_out[...] = acc
    for cp in copies:
        cp.wait_send()

    a_ref[...] = lax.dot_general(acc, acc, (((0,), (0,)), ((), ())),
                                 precision=lax.Precision.HIGHEST,
                                 preferred_element_type=jnp.float32)

    def exchange(n, me, make, src_of, dst_of, rsem, ssem):
        sent = []
        for j in peers(n, me):
            cp = pltpu.make_async_remote_copy(
                src_ref=src_of(j), dst_ref=dst_of(me), send_sem=ssem.at[j],
                recv_sem=rsem.at[me], device_id=make(j), device_id_type=MESH)
            cp.start()
            sent.append(cp)
        for j in peers(n, me):
            pltpu.make_async_remote_copy(
                src_ref=src_of(j), dst_ref=dst_of(j), send_sem=ssem.at[j],
                recv_sem=rsem.at[j], device_id=make(j), device_id_type=MESH).wait_recv()
        for cp in sent:
            cp.wait_send()

    def ordered_sum(buf, n):
        total = buf[0]
        for j in range(1, n):
            total = total + buf[j]
        return total

    c1 = a_ref.shape[0] // nq

    qbuf[qi] = a_ref[pl.ds(qi * c1, c1)]
    exchange(nq, qi, qdev, lambda j: a_ref.at[pl.ds(j * c1, c1)], lambda j: qbuf.at[j], qr, qs)
    qsum[...] = ordered_sum(qbuf, nq)

    zbuf[zi] = qsum[...]
    exchange(nz, zi, zdev, lambda j: qsum, lambda j: zbuf.at[j], zr, zs)
    own = qi * c1
    full[pl.ds(own, c1)] = ordered_sum(zbuf, nz)

    exchange(nq, qi, qdev, lambda j: full.at[pl.ds(own, c1)],
             lambda j: full.at[pl.ds(j * c1, c1)], qgr, qgs)
    g_out[...] = full[...]


def sketch_and_gram(snapshots, sketch, sizes):
    nz, ny, nc, nx = sizes
    nq = nc * nx * ny
    rows = snapshots.shape[0] // nx
    k = sketch.shape[1]
    c1 = k // nq
    dma = pltpu.SemaphoreType.DMA
    return pl.pallas_call(
        functools.partial(fused_kernel, sizes),
        out_shape=(jax.ShapeDtypeStruct((rows, k), jnp.float32),
                   jax.ShapeDtypeStruct((k, k), jnp.float32)),
        in_specs=[pl.BlockSpec(memory_space=pl.ANY)] * 2,
        out_specs=(pl.BlockSpec(memory_space=pltpu.VMEM),) * 2,
        scratch_shapes=[
            pltpu.VMEM(snapshots.shape, snapshots.dtype),
            pltpu.VMEM(sketch.shape, sketch.dtype),
            pltpu.VMEM((nx, rows, k), jnp.float32),
            pltpu.VMEM((nx, rows, k), jnp.float32),
            pltpu.VMEM((k, k), jnp.float32),
            pltpu.VMEM((nq, c1, k), jnp.float32),
            pltpu.VMEM((c1, k), jnp.float32),
            pltpu.VMEM((nz, c1, k), jnp.float32),
            pltpu.VMEM((k, k), jnp.float32),
            dma((nx,)), dma((nx,)), dma((nx + 1,)),
            dma((nq,)), dma((nq,)), dma((nz,)), dma((nz,)), dma((nq,)), dma((nq,)),
        ],
        compiler_params=pltpu.CompilerParams(collective_id=0, has_side_effects=True),
    )(snapshots, sketch)


def factor_kernel(b, scale, g_ref, q_ref, r_ref, basis_ref, tri_ref, l_ref, w_ref, s_ref):
    n = g_ref.shape[0]
    hi = lax.Precision.HIGHEST
    l_ref[...] = jnp.zeros_like(l_ref)
    w_ref[...] = jnp.zeros_like(w_ref)
    nt = (((1,), (1,)), ((), ()))
    rows = lax.broadcasted_iota(jnp.int32, (b, b), 0)
    cols = lax.broadcasted_iota(jnp.int32, (b, b), 1)

    def panel(p, carry):
        r0 = pl.multiple_of(p * b, b)
        s_ref[...] = g_ref[pl.ds(r0, b), pl.ds(r0, b)]

        @pl.when(p > 0)
        def _():
            x = lax.dot_general(g_ref[pl.ds(r0, b), :], w_ref[...], nt, precision=hi,
                                preferred_element_type=jnp.float32)
            l_ref[pl.ds(r0, b), :] = x
            s_ref[...] -= lax.dot_general(x, x, nt, precision=hi,
                                          preferred_element_type=jnp.float32)

        s = s_ref[...]
        low = jnp.zeros((b, b), jnp.float32)
        inv = jnp.zeros((b, b), jnp.float32)
        rest = (rows == cols).astype(jnp.float32)
        for i in range(b):
            pivot = s[i:i + 1, i:i + 1]
            left = s[:, i:i + 1]
            s = s - left * (s[i:i + 1, :] * (1.0 / pivot))
            col = jnp.where(rows[:, i:i + 1] >= i, left / jnp.sqrt(pivot), 0.0)
            low = jnp.where(cols == i, col, low)
            irow = rest[i:i + 1, :] / col[i:i + 1, :]
            inv = jnp.where(rows == i, irow, inv)
            rest = rest - col * irow

        @pl.when(p > 0)
        def _():
            y = jnp.dot(l_ref[pl.ds(r0, b), :], w_ref[...], precision=hi,
                        preferred_element_type=jnp.float32)
            w_ref[pl.ds(r0, b), :] = -jnp.dot(inv, y, precision=hi,
                                              preferred_element_type=jnp.float32)

        l_ref[pl.ds(r0, b), pl.ds(r0, b)] = low
        w_ref[pl.ds(r0, b), pl.ds(r0, b)] = inv
        return carry

    lax.fori_loop(0, n // b, panel, 0)
    orthonormal = lax.dot_general(q_ref[...], w_ref[...], nt, precision=hi,
                                  preferred_element_type=jnp.float32)
    basis_ref[...] = scale * jnp.dot(orthonormal, r_ref[...], precision=hi,
                                     preferred_element_type=jnp.float32)
    tri_ref[...] = l_ref[...].T / scale


def factor(gram, sketched, rotation, scale, b=128):
    n = gram.shape[0]
    return pl.pallas_call(
        functools.partial(factor_kernel, b, scale),
        out_shape=(jax.ShapeDtypeStruct(sketched.shape, jnp.float32),
                   jax.ShapeDtypeStruct((n, n), jnp.float32)),
        in_specs=[pl.BlockSpec(memory_space=pltpu.VMEM)] * 3,
        out_specs=(pl.BlockSpec(memory_space=pltpu.VMEM),) * 2,
        scratch_shapes=[pltpu.VMEM((n, n), jnp.float32)] * 2 + [pltpu.VMEM((b, b), jnp.float32)],
    )(gram, sketched, rotation)


def shards(sizes, snapshots, sketch, rotation):
    sketched, gram = sketch_and_gram(snapshots, sketch, sizes)
    cell_count = sketched.shape[0] * sizes[0] * sizes[1] * sizes[2] * sizes[3]
    scale = float(np.sqrt(np.float32(cell_count)))
    basis, triangle = factor(gram, sketched, rotation, scale)
    return (basis, triangle)


def physical_mesh(mesh):
    space, tm = mesh.devices.shape
    nc = 2
    ny = 4 if space % 8 == 0 else 1
    nz = space // (ny * nc)
    devs = mesh.devices.reshape(nz, ny, nc, tm)
    return Mesh(devs, AXES), (nz, ny, nc, tm)


def solution(mesh):
    m4, sizes = physical_mesh(mesh)
    in_specs = (P(SPACE, "x"), P("x", None), P())
    out_specs = (P(AXES, None), P())
    return jax.shard_map(functools.partial(shards, sizes), mesh=m4, in_specs=in_specs,
                         out_specs=out_specs, check_vma=False)
```
